32 devices in a mesh: agg: 8 (over z, x), col: 4 (over y, core).
Axes of the slice: x: 2, y: 2, z: 4, core: 2. Of those that a mesh axis runs over, the one named last changes fastest.
Arguments:
- fine_tiles: bfloat16 [128, 4, 192, 192], P('agg', 'col')
- fine_cols: int32 [128, 4], P('agg', 'col'), may hold values from 0 to 127, as said below
- agg_of: int32 [128], P('agg'), may hold values from 0 to 31, as said below
- prolong: bfloat16 [128, 192, 192], P('agg'), may hold values from -0.21875 to 0.21875
- coarse_cols: int32 [32, 4], P('agg'), may hold values from 0 to 31, as said below
Outputs:
- coarse_tiles: float32 [32, 4, 192, 192], P('agg', 'col')
- factor_tiles: float32 [32, 4, 192, 192], P('agg', 'col')
The draws below stay inside these ranges and needn't reach their ends.
Inputs may be any that keep to these rules, and one draw needn't show every extreme that they name: Fine block row i belongs to an aggregate of its own index of agg: i // 16 * 4 <= agg_of[i] < i // 16 * 4 + 4; every aggregate has at least one fine row. `coarse_cols`: slot 0 of aggregate row c is c itself; the other slots are distinct aggregates c + o with 1 <= |o| <= 4. `fine_cols`: slot 0 of fine row i is i; for slots 1 and above the aggregate of the named fine row is one of the slots 1 and above of row agg_of[i] of coarse_cols.
All inputs are finite; a program needn't handle non-finite values.
Results may differ from the reference program's by a relative error of at most 0.0055.
Values may be sent and summed in bfloat16 or wider, within the bound.
A program may use at most 128 MiB of HBM per device.

```python
import math
import jax
import jax.numpy as jnp
from jax import lax

B = 192
NA = 4
NC = 4
COARSE_DEV = 4
FR_DEV = 16
SWEEPS = 2
FINE = 128
COARSE = 32
N_AGG = 8


def pattern_table(key):
    reach = COARSE_DEV
    row_ids = jnp.arange(COARSE, dtype=jnp.int32)
    offsets = jnp.concatenate([jnp.arange(-reach, 0, dtype=jnp.int32), jnp.arange(1, reach + 1, dtype=jnp.int32)])
    places = row_ids[:, None] + offsets[None, :]
    inside = (places >= 0) & (places < COARSE)
    positions = jnp.arange(2 * reach, dtype=jnp.int32)
    scores = jax.random.randint(jax.random.fold_in(key, 11), (COARSE, 2 * reach), 0, 1 << 20) * (2 * reach) + positions[None, :]
    scores = jnp.where(inside, scores, -1 - positions[None, :])
    unused, picked = lax.top_k(scores, NC - 1)
    chosen = jnp.take_along_axis(places, picked, axis=1)
    return jnp.concatenate([row_ids[:, None], chosen], axis=1).astype(jnp.int32)


def grouping(key):
    groups = COARSE // COARSE_DEV
    positions = jnp.arange(FR_DEV, dtype=jnp.int32)
    scores = jax.random.randint(jax.random.fold_in(key, 23), (groups, FR_DEV), 0, 1 << 20) * FR_DEV + positions[None, :]
    permuted = jnp.argsort(scores, axis=1, stable=True).astype(jnp.int32)
    extra = jax.random.randint(jax.random.fold_in(key, 29), (groups, FR_DEV), 0, COARSE_DEV)
    labels = jnp.where(positions[None, :] < COARSE_DEV, positions[None, :], extra)
    ranking = jnp.argsort(permuted, axis=1, stable=True).astype(jnp.int32)
    local_label = jnp.take_along_axis(labels, ranking, axis=1)
    owners = jnp.arange(groups, dtype=jnp.int32)[:, None] * COARSE_DEV
    return ((local_label + owners).reshape(-1).astype(jnp.int32), permuted)


def draw_coarse_cols(key, part):
    return pattern_table(key)


def draw_agg_of(key, part):
    assigned, permuted = grouping(key)
    return assigned


def draw_fine_cols(key, part):
    pattern = pattern_table(key)
    assigned, permuted = grouping(key)
    row_ids = jnp.arange(FINE, dtype=jnp.int32)
    picked = jax.random.randint(jax.random.fold_in(key, 31), (FINE, NA - 1), 1, NC)
    target = pattern[assigned[:, None], picked]
    host_dev = target // COARSE_DEV
    member = target % COARSE_DEV
    attempts = jax.random.randint(jax.random.fold_in(key, 37), (FINE, NA - 1, 8), 0, FR_DEV)
    guesses = host_dev[..., None] * FR_DEV + attempts
    matches = assigned[guesses] == target[..., None]
    first_hit = jnp.argmax(matches.astype(jnp.int32), axis=-1)
    found = jnp.take_along_axis(guesses, first_hit[..., None], axis=-1)[..., 0]
    fallback = host_dev * FR_DEV + permuted[host_dev, member]
    chosen = jnp.where(jnp.any(matches, axis=-1), found, fallback)
    return jnp.concatenate([row_ids[:, None], chosen], axis=1).astype(jnp.int32)


def draw_fine_tiles(key, part):
    spread = 4.0 / math.sqrt(B)
    tile_shape = (FINE, NA, B, B)
    noise = jax.random.normal(jax.random.fold_in(key, 41), tile_shape, jnp.float32) * spread
    lifting = jnp.exp(jax.random.uniform(jax.random.fold_in(key, 43), (FINE, B), jnp.float32, math.log(0.6), math.log(4.0)))
    identity = jnp.eye(B, dtype=jnp.float32)
    noise = noise.at[:, 0].add(lifting[:, :, None] * identity[None])
    return noise.astype(jnp.bfloat16)


def block_levels(stream_key, shape, pieces, low, largest):
    level, own = 1.0, jax.random.fold_in(stream_key, 6)
    for dim, parts in pieces:
        heights = jnp.exp(jax.random.uniform(jax.random.fold_in(own, dim), (parts,), jnp.float32, low / len(pieces), largest / len(pieces)))
        level = level * jnp.repeat(heights, shape[dim] // parts).reshape([-1 if axis == dim else 1 for axis in range(len(shape))])
    return level


def bell_draw(rng, dims, scale, limit, split=(), kind=jnp.bfloat16):
    drawn = jax.random.normal(rng, dims, jnp.float32) * scale
    if len(split) > 0:
        drawn = block_levels(rng, dims, split, -0.22, 0.18) * drawn
    return jnp.clip(drawn, min=-limit, max=limit).astype(kind)


def setup_inputs(seed: int = 0) -> dict:
    key_of = jax.random.split(jax.random.key(seed), 6)
    fine_tiles = draw_fine_tiles(jax.random.fold_in(key_of[5], 71), 0)
    fine_cols = draw_fine_cols(jax.random.fold_in(key_of[5], 71), 0)
    agg_of = draw_agg_of(jax.random.fold_in(key_of[5], 71), 0)
    prolong = bell_draw(key_of[3], (FINE, B, B), (B * FR_DEV // COARSE_DEV) ** -0.5, 0.21875, ((0, 8),))
    coarse_cols = draw_coarse_cols(jax.random.fold_in(key_of[5], 71), 0)
    return {"fine_tiles": fine_tiles, "fine_cols": fine_cols, "agg_of": agg_of, "prolong": prolong, "coarse_cols": coarse_cols}


HIGHEST = lax.Precision.HIGHEST


def relax_rows(target_coarse, target_old, target_cols, row_full, row_cols, ext_full, ext_cols, row_base, ext_base):
    row_count = row_cols.shape[0]
    ext_count = ext_full.shape[0]
    width = row_full.shape[-1]
    row_ids = row_base + jnp.arange(row_count, dtype=jnp.int32)
    lowest = jnp.minimum(row_ids[:, None], target_cols)
    prior_index = jnp.clip(row_cols - ext_base, 0, ext_count - 1).astype(jnp.int32)
    further = ext_full[prior_index]
    further_cols = ext_cols[prior_index]
    matched = (further_cols[:, None, :, :] == target_cols[:, :, None, None]) & (row_cols[:, None, :, None] < lowest[:, :, None, None])
    chosen = jnp.einsum('rqmn,rmnab->rqmab', matched.astype(jnp.float32), further, precision=HIGHEST)
    through = jnp.einsum('rmab,rqmbc->rqac', row_full, chosen, precision=HIGHEST)
    own_diag = row_full[:, 0]
    diag_index = jnp.clip(target_cols - ext_base, 0, ext_count - 1).astype(jnp.int32)
    their_diag = ext_full[diag_index, 0]
    upper_mask = jnp.arange(width)[None, :] > jnp.arange(width)[:, None]
    lower_mask = upper_mask.T
    upper_tile = row_ids[:, None] < target_cols
    lower_tile = row_ids[:, None] > target_cols
    on_diagonal = row_ids[:, None] == target_cols
    right_factor = jnp.where(upper_tile[:, :, None, None], target_old, jnp.where(upper_mask, own_diag, 0.0)[:, None])
    lower_term = jnp.einsum('rab,rqbc->rqac', jnp.where(lower_mask, own_diag, 0.0), right_factor, precision=HIGHEST)
    upper_term = jnp.einsum('rqab,rqbc->rqac', target_old, jnp.where(upper_mask, their_diag, 0.0), precision=HIGHEST)
    edge_term = jnp.where(lower_tile[:, :, None, None], upper_term, lower_term)
    residue = target_coarse - through - edge_term
    pivots = jnp.maximum(jnp.diagonal(their_diag, axis1=-2, axis2=-1), 1.0)
    scaled = lower_tile[:, :, None, None] | (on_diagonal[:, :, None, None] & lower_mask[None, None])
    return jnp.where(scaled, residue / pivots[:, :, None, :], residue)


def reference(fine_tiles, fine_cols, agg_of, prolong, coarse_cols):
    def coarse_block(block_index):
        start_row = (block_index * FR_DEV).astype(jnp.int32)
        tile_block = lax.dynamic_slice_in_dim(fine_tiles, start_row, FR_DEV, 0).astype(jnp.float32)
        columns = lax.dynamic_slice_in_dim(fine_cols, start_row, FR_DEV, 0)
        own_prolong = lax.dynamic_slice_in_dim(prolong, start_row, FR_DEV, 0).astype(jnp.float32)
        labels = lax.dynamic_slice_in_dim(agg_of, start_row, FR_DEV, 0)
        remote = prolong[columns].astype(jnp.float32)
        carried = jnp.einsum('isab,isbc->isac', tile_block, remote, precision=HIGHEST).astype(jnp.bfloat16)
        carried = lax.optimization_barrier(carried).astype(jnp.float32)
        lifted = jnp.einsum('iba,isbc->isac', own_prolong, carried, precision=HIGHEST)
        targets = agg_of[columns]
        owned_rows = (block_index * COARSE_DEV).astype(jnp.int32) + jnp.arange(COARSE_DEV, dtype=jnp.int32)
        row_pattern = lax.dynamic_slice_in_dim(coarse_cols, (block_index * COARSE_DEV).astype(jnp.int32), COARSE_DEV, 0)
        weights = ((labels[:, None] == owned_rows[None, :])[:, None, :, None] & (row_pattern[None, None, :, :] == targets[:, :, None, None])).astype(jnp.float32)
        return jnp.einsum('isrq,isac->rqac', weights, lifted, precision=HIGHEST)

    blocks = jnp.arange(N_AGG, dtype=jnp.int32)
    coarse = lax.map(coarse_block, blocks).reshape(COARSE, NC, B, B)
    factor = coarse
    for sweep_step in range(SWEEPS):
        def ilu_block(block_index, factor=factor):
            row_base = (block_index * COARSE_DEV).astype(jnp.int32)
            ext_base = jnp.maximum(row_base - COARSE_DEV, 0).astype(jnp.int32)
            ext_full = lax.dynamic_slice_in_dim(factor, ext_base, 2 * COARSE_DEV, 0)
            ext_cols = lax.dynamic_slice_in_dim(coarse_cols, ext_base, 2 * COARSE_DEV, 0)
            row_full = lax.dynamic_slice_in_dim(factor, row_base, COARSE_DEV, 0)
            row_cols = lax.dynamic_slice_in_dim(coarse_cols, row_base, COARSE_DEV, 0)
            row_coarse = lax.dynamic_slice_in_dim(coarse, row_base, COARSE_DEV, 0)
            return relax_rows(row_coarse, row_full, row_cols, row_full, row_cols, ext_full, ext_cols, row_base, ext_base)
        factor = lax.map(ilu_block, blocks).reshape(COARSE, NC, B, B)
    return coarse, factor
```

```python
import functools

import jax
import jax.numpy as jnp
from jax import lax
from jax.experimental import pallas as pl
from jax.experimental.pallas import tpu as pltpu
from jax.sharding import PartitionSpec as P

SWEEPS = 2
MESH = pl.DeviceIdType.MESH
BF = jnp.bfloat16
F32 = jnp.float32


def pack(tile, dtype):
    width = tile.shape[-1]
    lanes = 2 * width // 3
    half = width // 2
    rest = tile[:, lanes:]
    return tile[:, :lanes].astype(dtype), jnp.concatenate([rest[:half], rest[half:]], axis=1).astype(dtype)


def put(ref, index, tile):
    left, rest = pack(tile, ref.dtype)
    width = tile.shape[-1]
    ref[index, 0:width] = left
    ref[index, width:] = rest


def unpack(tile, width):
    half = width // 2
    rest = tile[width:]
    fold = width - tile.shape[-1]
    right = jnp.concatenate([rest[:, :fold], rest[:, fold:]], axis=0)
    return jnp.concatenate([tile[:width], right], axis=1)


def gather_kernel(
    dims, agg_hbm, fcol_hbm, ccol_hbm, fine_hbm, prolong_hbm, ext, coarse_hbm, tabs_hbm,
    fine, own_prolong, turned, near, seg, own_pack, coarse_v, sums, pair_out, pair_in, y_out, y_in,
    agg_v, fcol_v, ccol_v, tab_v, tab, cls, order, table,
    i_sem, in_sem, t_sem, t_send, t_recv, o_sem,
    h_send, h_recv, p_send, p_recv, y_send, y_recv, e_send, e_recv, l_sem, c_sem,
):
    groups, peers, rows, crows, slots, width = dims
    a = lax.axis_index("agg")
    c = lax.axis_index("col")
    c1 = c + 1 - 2 * (c % 2)
    c2 = (c + 2) % peers
    c3 = c2 + 1 - 2 * (c2 % 2)
    has_prev = a > 0
    has_next = a < groups - 1
    parity = a % 2
    partner_agg = a + 1 - 2 * parity
    relay_to = a + 2 - 4 * parity
    relay_from = a - 2 + 4 * parity
    can_relay = (relay_to >= 0) & (relay_to < groups)
    has_other = (relay_from >= 0) & (relay_from < groups)
    alone = rows // (2 * peers)
    both = rows // 4
    direct = alone + both
    o_some = crows * slots
    half = crows // 2
    odd = parity == 1
    even = parity == 0
    has_far = a > 1
    has_ahead = a < groups - 2

    blocks = [(c * alone, alone), (peers * alone + (c % 2) * both, both)]
    blocks += [(other * alone, alone) for other in (c1, c2, c3)]
    blocks += [(peers * alone + (c1 % 2) * both, both)]

    def take(j):
        start, size = blocks[j]
        return pltpu.make_async_copy(
            prolong_hbm.at[pl.ds(start, size)], own_prolong.at[pl.ds(start, size)], in_sem.at[j]
        )

    for j in range(2):
        take(j).start()
    take_ints = [
        pltpu.make_async_copy(src, dst, i_sem.at[j])
        for j, (src, dst) in enumerate(((agg_hbm, agg_v), (fcol_hbm, fcol_v), (ccol_hbm, ccol_v)))
    ]
    for copy in take_ints:
        copy.start()
    for j in range(2, len(blocks)):
        take(j).start()
    take_fine = pltpu.make_async_copy(fine_hbm, fine, in_sem.at[6])
    take_fine.start()

    barrier = pltpu.get_barrier_semaphore()
    for other in (c1, c2, c3):
        pl.semaphore_signal(barrier, inc=1, device_id=(a, other), device_id_type=MESH)

    @pl.when(has_prev)
    def _():
        pl.semaphore_signal(barrier, inc=1, device_id=(a - 1, c), device_id_type=MESH)

    @pl.when(has_next)
    def _():
        pl.semaphore_signal(barrier, inc=1, device_id=(a + 1, c), device_id_type=MESH)

    @pl.when(has_far)
    def _():
        pl.semaphore_signal(barrier, inc=1, device_id=(a - 2, c), device_id_type=MESH)

    @pl.when(has_ahead)
    def _():
        pl.semaphore_signal(barrier, inc=1, device_id=(a + 2, c), device_id_type=MESH)

    tab_v[2] = jnp.zeros(tab_v.shape[1:], jnp.int32)
    for copy in take_ints:
        copy.wait()
    tab_v[2, 0:1, 0:rows] = agg_v[...]
    tab_v[2, 1:1 + crows, 0:slots] = ccol_v[...]
    tab_v[2, 1 + crows:2 + crows, 0:rows] = fcol_v[...]

    def remote(src, dst, send, recv, device):
        return pltpu.make_async_remote_copy(
            src_ref=src, dst_ref=dst, send_sem=send, recv_sem=recv,
            device_id=device, device_id_type=MESH,
        )

    def pack_own(j):
        start, size = blocks[j]

        def body(k, carry):
            put(near, rows + start + k, own_prolong[start + k].astype(F32))
            return carry
        lax.fori_loop(0, size, body, 0)

    for j in range(2):
        take(j).wait()
        pack_own(j)

    @pl.when((a > 1) & (a < groups - 2))
    def _():
        pl.semaphore_wait(barrier, 7)

    @pl.when((a == 1) | (a == groups - 2))
    def _():
        pl.semaphore_wait(barrier, 6)

    @pl.when((a == 0) | (a == groups - 1))
    def _():
        pl.semaphore_wait(barrier, 5)

    def ints_to(j):
        ahead = (1, -1, 2)[j]
        return remote(tab_v.at[2], tab_v.at[(1, 3, 0)[j]], t_send.at[j], t_recv.at[j], (a + ahead, c))

    def tile_of(who, k):
        if k < alone:
            return who * alone + k
        return peers * alone + (who % 2) * both + k - alone

    def block_at(side):
        return ((1 - parity) if side == 0 else parity) * 2 * rows

    def push(k):
        src = near.at[pl.ds(rows + tile_of(c, k), 1)]
        dst = near.at[pl.ds(parity * 2 * rows + tile_of(c, k), 1)]
        return remote(src, dst, h_send.at[0, 0, k], h_recv.at[0, 0, k], (partner_agg, c))

    def relay(k):
        src = near.at[pl.ds(block_at(0) + tile_of(c, k), 1)]
        dst = near.at[pl.ds(parity * 2 * rows + tile_of(c, k), 1)]
        return remote(src, dst, h_send.at[1, 0, k], h_recv.at[1, 0, k], (relay_to, c))

    def pass_on(side, kind, who, k, device):
        view = near.at[pl.ds(block_at(side) + tile_of(who, k), 1)]
        return remote(view, view, h_send.at[side, kind, k], h_recv.at[side, kind, k], device)

    def arrived(side, k):
        pass_on(side, 0, c, k, (a, c1)).wait_recv()
        if side == 0:
            @pl.when(can_relay)
            def _():
                relay(k).start()
        if k < alone:
            pass_on(side, 2, c, k, (a, c2)).start()
        pass_on(side, 1, c, k, (a, c1)).start()

    def crossed(side, k):
        pass_on(side, 2, c2, k, (a, c2)).wait_recv()
        pass_on(side, 3, c2, k, (a, c1)).start()

    def complete(side):
        for k in range(direct):
            pass_on(side, 1, c1, k, (a, c1)).wait_recv()
            if k < alone:
                pass_on(side, 3, c3, k, (a, c1)).wait_recv()

    def left(side):
        for k in range(direct):
            pass_on(side, 1, c, k, (a, c1)).wait_send()
            if k < alone:
                pass_on(side, 2, c, k, (a, c2)).wait_send()
                pass_on(side, 3, c2, k, (a, c1)).wait_send()

    def other_side(step, *args):
        pl.when(has_other)(functools.partial(step, 1, *args))

    can_send = (has_next, has_prev, has_ahead)
    can_take = (has_prev, has_next, has_far)

    def ints_all(act):
        for j in range(3):
            @pl.when(can_send[j])
            def _(j=j):
                act(ints_to(j))

    ints_all(lambda copy: copy.start())
    for k in range(direct):
        push(k).start()
    for j in range(2, len(blocks)):
        take(j).wait()
        pack_own(j)

    def to_scalar(g):
        return pltpu.make_async_copy(tab_v.at[g], tab.at[g], t_sem.at[g])

    def tab_out(g):
        return pltpu.make_async_copy(tab_v.at[g], tabs_hbm.at[g], o_sem.at[g])

    to_scalar(2).start()
    tab_out(2).start()

    def integers():
        to_scalar(2).wait()
        for j in range(2):
            @pl.when(can_take[j])
            def _(j=j):
                ints_to(j).wait_recv()
                to_scalar((1, 3)[j]).start()
                to_scalar((1, 3)[j]).wait()

    chores = [integers]
    row_base = a * crows

    def place_of(i):
        return tab[2, 1 + crows, i] - (a - 1) * rows

    def classify(i, carry):
        place = jnp.clip(place_of(i), 0, 3 * rows - 1)
        target = tab[1 + place // rows, 0, place % rows]
        r = jnp.clip(tab[2, 0, i] - row_base, 0, crows - 1)
        q = 0
        for s in range(1, slots):
            q = jnp.where(tab[2, 1 + r, s] == target, s, q)
        cls[i] = (r * slots + q) * rows + i
        return carry

    chores.append(lambda: lax.fori_loop(0, rows, classify, 0))

    def rank(i, carry):
        key = cls[i]
        below = 0
        for j in range(rows):
            below = below + jnp.where(cls[j] < key, 1, 0)
        order[rows + i] = below
        return carry

    chores.append(lambda: lax.fori_loop(0, rows, rank, 0))

    def place_key(k, carry):
        key = 0
        for i in range(rows):
            key = key + jnp.where(order[rows + i] == k, cls[i], 0)
        order[k] = key
        return carry

    chores.append(lambda: lax.fori_loop(0, rows, place_key, 0))

    def ends(s, carry):
        upto = 0
        some = 0
        for i in range(rows):
            own_class = cls[i] // rows
            upto = upto + jnp.where(own_class <= s, 1, 0)
            some = jnp.where(own_class == s, 1, some)
        table[s] = jnp.maximum(upto - 1, 0)
        table[o_some + s] = some
        return carry

    chores.append(lambda: lax.fori_loop(0, crows * slots, ends, 0))

    part_count = crows + half
    diag = list(range(crows))
    quarter = rows // 4

    def lift_at(k, total, prior):
        key = order[k]
        i = key % rows
        earlier = order[jnp.maximum(k - 1, 0)]
        goes_on = jnp.where(earlier // rows == key // rows, 1, 0)
        carried = jnp.dot(fine[i], prior(i), preferred_element_type=F32).astype(BF)
        lifted = jnp.dot(turned[i], carried, preferred_element_type=F32)
        total = lifted + total * goes_on.astype(F32)
        seg[k] = total
        return total

    def lift_all(prior):
        def step(k, total):
            return lift_at(k, total, prior)

        lax.fori_loop(0, rows, step, jnp.zeros((width, width), F32), unroll=4)

    def near_prior(i):
        place = jnp.clip(place_of(i), 0, 3 * rows - 1)
        return unpack(near[place], width)

    def part(r, q):
        s = r * slots + q
        return seg[table[s]] * table[o_some + s].astype(F32)

    pp, prev, own = (g * slots * crows for g in range(3))

    def to_core(at, i, through=False):
        here = ext.at[pl.ds(at + i, 1)]
        src = own_pack.at[pl.ds(i, 1)] if at == own and not through else here
        return remote(src, here, e_send.at[0, at + i], e_recv.at[at + i], (a, c1))

    def to_next(i):
        return remote(
            own_pack.at[pl.ds(i, 1)], ext.at[pl.ds(prev + i, 1)],
            e_send.at[1, own + i], e_recv.at[prev + i], (a + 1, c),
        )

    def to_ahead(i):
        return remote(
            own_pack.at[pl.ds(i, 1)], ext.at[pl.ds(pp + i, 1)],
            e_send.at[2, own + i], e_recv.at[pp + i], (a + 2, c),
        )

    def to_behind(i):
        return remote(
            ext.at[pl.ds(pp + i, 1)], ext.at[pl.ds(prev + i, 1)],
            e_send.at[1, pp + i], e_recv.at[prev + i], (a - 1, c),
        )

    def to_other(i):
        return remote(
            own_pack.at[pl.ds(i, 1)], ext.at[pl.ds(own + i, 1)],
            e_send.at[2, own + i], e_recv.at[own + i], (a, c2),
        )

    def pass_next(i):
        return remote(
            ext.at[pl.ds(own + i, 1)], ext.at[pl.ds(prev + i, 1)],
            e_send.at[1, own + i], e_recv.at[prev + i], (a + 1, c),
        )

    def keep(i):
        return pltpu.make_async_copy(own_pack.at[i], ext.at[own + i], l_sem.at[i])

    def keep_coarse(r):
        return pltpu.make_async_copy(coarse_v.at[r], coarse_hbm.at[r], c_sem.at[r])

    def lift_diag(quarter_at):
        def step(k, carry):
            key = order[k]
            i = key % rows
            earlier = order[jnp.maximum(k - 1, 0)]
            goes_on = jnp.where((k > 0) & (earlier // rows == key // rows), 1, 0)
            carried = jnp.dot(fine[i], own_prolong[i], preferred_element_type=F32).astype(BF)
            lifted = jnp.dot(turned[i], carried, preferred_element_type=F32)
            seg[k] = lifted + seg[jnp.maximum(k - 1, 0)] * goes_on.astype(F32)
            return carry

        if quarter_at == 0:
            take_fine.wait()
            seg[0] = jnp.zeros((width, width), F32)
        lax.fori_loop(quarter_at * quarter, (quarter_at + 1) * quarter, step, 0, unroll=True)

    def send_diag():
        for r in diag:
            value = part(r, 0)
            coarse_v[r] = value
            put(own_pack, r, value)
            keep(r).start()
            keep_coarse(r).start()
            to_other(r).start()
            to_core(own, r).start()

            @pl.when(has_next)
            def _(r=r):
                to_next(r).start()

    lag = 2
    for k in range(direct + lag):
        if k < direct:
            arrived(0, k)
        if k >= lag:
            other_side(arrived, k - lag)
        if k == 0:
            for i in range(rows):
                turned[i] = own_prolong[i].astype(F32).T.astype(BF)
        if k < 5:
            for chore in chores[(0, 1, 2, 4, 5)[k]:(1, 2, 4, 5, 6)[k]]:
                chore()
        if 0 <= k - 3 < alone:
            crossed(0, k - 3)
        if 0 <= k - 5 < alone:
            other_side(crossed, k - 5)
        if 3 <= k < 7:
            pl.when(c == 0)(functools.partial(lift_diag, k - 3))
        if k == 7:
            pl.when(c == 0)(send_diag)
    assert direct + lag >= 8
    def landed(at, i):
        view = ext.at[pl.ds(at + i, 1)]
        remote(view, view, e_send.at[0, at + i], e_recv.at[at + i], (a, c1)).wait_recv()

    def own_ready(i, act):
        act(to_core(own, i))

        @pl.when(even & has_next)
        def _():
            act(to_next(i))

        @pl.when(has_ahead)
        def _():
            act(to_ahead(i))

    def neighbours(i):
        @pl.when(has_far)
        def _():
            landed(pp, i)

            @pl.when(odd)
            def _():
                to_behind(i).start()

            to_core(pp, i).start()

        @pl.when(odd)
        def _():
            landed(prev, i)
            to_core(prev, i).start()

    def relayed(i):
        @pl.when(even & has_far)
        def _():
            landed(prev, i)
            to_core(prev, i).start()

    def flow(tiles, finish, lag):
        count = len(tiles)
        for k in range(count + 2 * lag):
            if k < count:
                finish(k)
                keep(tiles[k]).start()
                own_ready(tiles[k], lambda copy: copy.start())
            if 0 <= k - lag < count:
                neighbours(tiles[k - lag])
            if 0 <= k - 2 * lag < count:
                relayed(tiles[k - 2 * lag])

    def flow_sent(tiles):
        for i in tiles:
            keep(i).wait()
            own_ready(i, lambda copy: copy.wait_send())

            @pl.when(has_far)
            def _(i=i):
                to_core(pp, i).wait_send()

                @pl.when(odd)
                def _():
                    to_behind(i).wait_send()

            @pl.when(has_prev)
            def _(i=i):
                to_core(prev, i).wait_send()

    def arrivals(tiles):
        for i in tiles:
            landed(own, i)

            @pl.when(has_prev)
            def _(i=i):
                landed(prev, i)

            @pl.when(has_far)
            def _(i=i):
                landed(pp, i)

    def set_of(who):
        tiles = [(j, who) for j in range(crows)]
        return tiles + [((who - 2) * half + j, 1) for j in range(half)]

    def arrivals_diag():
        for r in diag:
            landed(own, r)

            @pl.when(has_prev)
            def _(r=r):
                landed(prev, r)

    @pl.when(c == 0)
    def _():
        complete(0)
        other_side(complete)
        for r in diag:
            @pl.when(has_prev)
            def _(r=r):
                landed(prev, r)
                to_core(prev, r).start()
        arrivals([q * crows + r for q in range(1, slots) for r in range(crows)])
        for r in diag:
            keep(r).wait()
            to_other(r).wait_send()
            to_core(own, r).wait_send()

            @pl.when(has_next)
            def _(r=r):
                to_next(r).wait_send()

            @pl.when(has_prev)
            def _(r=r):
                to_core(prev, r).wait_send()

    @pl.when(c > 0)
    def _():
        complete(0)
        other_side(complete)
        take_fine.wait()
        lift_all(near_prior)

    @pl.when(c == 1)
    def _():
        listed = [(f, j) for j in range(part_count) for f in (2, 3)]

        def cross(k):
            f, j = listed[k]
            at = (f - 2) * part_count + j
            return remote(
                y_out.at[pl.ds(at, 1)], y_in.at[pl.ds(j, 1)], y_send.at[at], y_recv.at[j], (a, f)
            )

        tiles = []
        for k, (f, j) in enumerate(listed):
            r, q = set_of(f)[j]
            tiles.append(q * crows + r)
            put(y_out, (f - 2) * part_count + j, part(r, q))
            cross(k).start()

        def finish(k):
            f, j = listed[k]
            r, q = set_of(f)[j]
            at = (f - 2) * part_count + j
            view = y_in.at[pl.ds(at, 1)]
            remote(view, view, y_send.at[at], y_recv.at[at], (a, f)).wait_recv()
            value = part(r, q) + unpack(y_in[at].astype(F32), width)
            if q == 1:
                coarse_v[r] = value
                keep_coarse(r).start()
            put(own_pack, q * crows + r, value)

        flow(tiles, finish, 5)
        arrivals_diag()
        for k in range(len(listed)):
            cross(k).wait_send()
        flow_sent(tiles)

    @pl.when(c > 1)
    def _():
        mine = [(j, c) for j in range(crows)] + [((c - 2) * half + j, 1) for j in range(half)]
        theirs = [(j, c1) for j in range(crows)] + [((c1 - 2) * half + j, 1) for j in range(half)]

        def swap(j):
            return remote(
                pair_out.at[pl.ds(j, 1)], pair_in.at[pl.ds(j, 1)], p_send.at[j], p_recv.at[j], (a, c1)
            )

        def cross(j):
            return remote(
                y_out.at[pl.ds(j, 1)], y_in.at[pl.ds((c - 2) * part_count + j, 1)],
                y_send.at[j], y_recv.at[(c - 2) * part_count + j], (a, 1),
            )

        for j, (r, q) in enumerate(theirs):
            put(pair_out, j, part(r, q))
            swap(j).start()
        for j, (r, q) in enumerate(mine):
            swap(j).wait_recv()
            value = part(r, q) + unpack(pair_in[j].astype(F32), width)
            sums[j] = value
            put(y_out, j, value)
            cross(j).start()

        @pl.when(c == 2)
        def _():
            for r in diag:
                landed(own, r)
                to_core(own, r, True).start()

                @pl.when(has_next)
                def _(r=r):
                    pass_next(r).start()

        def finish(j):
            r, q = mine[j]
            view = y_in.at[pl.ds(j, 1)]
            remote(view, view, y_send.at[j], y_recv.at[j], (a, 1)).wait_recv()
            value = sums[j] + unpack(y_in[j].astype(F32), width)
            if j < crows:
                coarse_v[j] = value
                keep_coarse(j).start()
            put(own_pack, q * crows + r, value)

        tiles = [q * crows + r for r, q in mine]
        flow(tiles, finish, 3)

        @pl.when(c == 2)
        def _():
            for r in diag:
                @pl.when(has_prev)
                def _(r=r):
                    landed(prev, r)
                    to_core(prev, r).start()

        @pl.when(c == 3)
        def _():
            arrivals_diag()

        arrivals([q * crows + r for r, q in theirs])
        for j in range(part_count):
            swap(j).wait_send()
            cross(j).wait_send()
        flow_sent(tiles)

        @pl.when(c == 2)
        def _():
            for r in diag:
                to_core(own, r, True).wait_send()

                @pl.when(has_next)
                def _(r=r):
                    pass_next(r).wait_send()

                @pl.when(has_prev)
                def _(r=r):
                    to_core(prev, r).wait_send()

    for r in range(crows):
        keep_coarse(r).wait()

    for j in range(2):
        @pl.when(can_take[j])
        def _(j=j):
            tab_out((1, 3)[j]).start()
            tab_out((1, 3)[j]).wait()

    @pl.when(has_far)
    def _():
        ints_to(2).wait_recv()
        tab_out(0).start()
        tab_out(0).wait()

    tab_out(2).wait()
    ints_all(lambda copy: copy.wait_send())
    for k in range(direct):
        push(k).wait_send()

    @pl.when(can_relay)
    def _():
        for k in range(direct):
            relay(k).wait_send()

    left(0)
    other_side(left)


def sweep_kernel(dims, tabs, ext, coarse_hbm, coarse_out, factor_out, coarse_v, first, acc, need, in_sem, out_sem):
    crows, slots, width = dims
    c = lax.axis_index("col")
    base = (lax.axis_index("agg") - 2) * crows
    whole = pltpu.make_async_copy(coarse_hbm, coarse_v, in_sem)
    whole.start()
    ids_r = lax.broadcasted_iota(jnp.int32, (width, width), 0)
    ids_c = lax.broadcasted_iota(jnp.int32, (width, width), 1)
    above = (ids_c > ids_r).astype(F32)
    below = (ids_c < ids_r).astype(F32)
    on = ids_c == ids_r

    def column(row, slot):
        return tabs[row // crows, 1 + row % crows, slot] - base

    def spot(row, slot):
        return ((row // crows) * slots + slot) * crows + row % crows

    def match(row, col, m):
        k = column(row, m)
        inside = k < jnp.minimum(row, col)
        k = jnp.clip(k, 0, 3 * crows - 1)
        slot = 0
        found = 0
        for n in range(slots):
            same = column(k, n) == col
            slot = jnp.where(same, n, slot)
            found = jnp.where(same, 1, found)
        return jnp.where(inside, found, 0), k, slot

    def zero(i, carry):
        need[i] = 0
        return carry

    lax.fori_loop(0, 3 * crows * slots, zero, 0)

    def mark(row, slot):
        need[row * slots + slot] = 1

    def wants(r, carry):
        row = 2 * crows + r
        col = column(row, c)
        mark(row, c)
        mark(jnp.clip(jnp.minimum(row, col), 0, 3 * crows - 1), 0)
        for m in range(1, slots):
            found, k, slot = match(row, col, m)

            @pl.when(found == 1)
            def _(k=k, slot=slot, m=m):
                mark(row, m)
                mark(k, slot)
        return carry

    lax.fori_loop(0, crows, wants, 0)

    def relax(row, slot, start, tile):
        col = column(row, slot)
        acc[...] = start
        for m in range(1, slots):
            found, k, n = match(row, col, m)

            @pl.when(found == 1)
            def _(k=k, n=n, m=m):
                acc[...] -= jnp.dot(tile(row, m), tile(k, n), preferred_element_type=F32)
        low = jnp.full((width, width), jnp.where(row > col, 1, 0)) == 1
        up = jnp.full((width, width), jnp.where(row < col, 1, 0)) == 1
        before = tile(row, slot).astype(F32)
        own_diag = tile(row, 0).astype(F32)
        their_diag = tile(jnp.clip(jnp.minimum(row, col), 0, 3 * crows - 1), 0).astype(F32)
        left = jnp.where(low, before, own_diag * below)
        right = jnp.where(up, before, their_diag * above)
        value = acc[...] - jnp.dot(left.astype(BF), right.astype(BF), preferred_element_type=F32)
        pivots = jnp.maximum(jnp.sum(jnp.where(on, their_diag, 0.0), axis=0, keepdims=True), 1.0)
        scaled = low | (jnp.logical_not(up) & (ids_c < ids_r))
        return jnp.where(scaled, value / pivots, value)

    def old(row, slot):
        return unpack(ext[spot(row, slot)], width)

    def new(row, slot):
        return first[row * slots + slot]

    def sweep(i, carry):
        @pl.when(need[i] == 1)
        def _():
            row, slot = i // slots, i % slots
            first[i] = relax(row, slot, old(row, slot).astype(F32), old).astype(BF)
        return carry

    lax.fori_loop(crows * slots, 3 * crows * slots, sweep, 0)
    whole.wait()
    give = pltpu.make_async_copy(coarse_v, coarse_out, out_sem)
    give.start()

    def last(r, carry):
        factor_out[r] = relax(2 * crows + r, c, coarse_v[r], new)
        return carry

    lax.fori_loop(0, crows, last, 0)
    give.wait()


def on_device(groups, peers, fine_tiles, fine_cols, agg_of, prolong, coarse_cols):
    rows, width = prolong.shape[0], prolong.shape[-1]
    crows, slots = coarse_cols.shape
    assert SWEEPS == 2 and slots == peers == 4 and fine_tiles.shape[1] == 1
    assert groups % 2 == 0 and groups >= 4 and crows % 2 == 0
    direct = rows // (2 * peers) + rows // 4
    dma = pltpu.SemaphoreType.DMA
    tile = (width, width)
    packed = (width + width // 2, 2 * width // 3)
    count = slots * crows
    pairs = crows + crows // 2
    room = (-(-(crows + 2) // 8) * 8, 128)
    vmem = pl.BlockSpec(memory_space=pltpu.VMEM)
    smem = pl.BlockSpec(memory_space=pltpu.SMEM)
    anywhere = pl.BlockSpec(memory_space=pl.ANY)
    hbm = pl.BlockSpec(memory_space=pltpu.HBM)
    ext, coarse, tabs = pl.pallas_call(
        functools.partial(gather_kernel, (groups, peers, rows, crows, slots, width)),
        out_shape=(
            pltpu.VMEM((3 * count,) + packed, BF),
            pltpu.VMEM((crows,) + tile, F32),
            pltpu.VMEM((4,) + room, jnp.int32),
        ),
        in_specs=[hbm] * 5,
        out_specs=(anywhere, anywhere, anywhere),
        scratch_shapes=[
            pltpu.VMEM((rows,) + tile, BF),
            pltpu.VMEM((rows,) + tile, BF),
            pltpu.VMEM((rows,) + tile, BF),
            pltpu.VMEM((3 * rows,) + packed, BF),
            pltpu.VMEM((rows,) + tile, F32),
            pltpu.VMEM((count,) + packed, BF),
            pltpu.VMEM((crows,) + tile, F32),
            pltpu.VMEM((pairs,) + tile, F32),
            pltpu.VMEM((pairs,) + packed, BF),
            pltpu.VMEM((pairs,) + packed, BF),
            pltpu.VMEM((2 * pairs,) + packed, BF),
            pltpu.VMEM((2 * pairs,) + packed, BF),
            pltpu.VMEM((1, rows), jnp.int32),
            pltpu.VMEM((1, rows), jnp.int32),
            pltpu.VMEM((crows, slots), jnp.int32),
            pltpu.VMEM((4,) + room, jnp.int32),
            pltpu.SMEM((4,) + room, jnp.int32),
            pltpu.SMEM((rows,), jnp.int32),
            pltpu.SMEM((2 * rows,), jnp.int32),
            pltpu.SMEM((2 * count,), jnp.int32),
            dma((3,)), dma((7,)), dma((4,)), dma((3,)), dma((3,)), dma((4,)),
            dma((2, 4, direct)), dma((2, 4, direct)),
            dma((pairs,)), dma((pairs,)), dma((2 * pairs,)), dma((2 * pairs,)),
            dma((3, 3 * count)), dma((3 * count,)), dma((count,)), dma((crows,)),
        ],
        compiler_params=pltpu.CompilerParams(
            collective_id=0, has_side_effects=True, vmem_limit_bytes=56 * 1024 * 1024
        ),
    )(agg_of.reshape(1, rows), fine_cols.reshape(1, rows), coarse_cols, fine_tiles.reshape((rows,) + tile), prolong)
    out = jax.ShapeDtypeStruct((crows,) + tile, F32)
    coarse, factor = pl.pallas_call(
        functools.partial(sweep_kernel, (crows, slots, width)),
        out_shape=(out, out),
        in_specs=[smem, vmem, anywhere],
        out_specs=(anywhere, vmem),
        scratch_shapes=[
            pltpu.VMEM((crows,) + tile, F32),
            pltpu.VMEM((3 * count,) + tile, BF),
            pltpu.VMEM(tile, F32),
            pltpu.SMEM((3 * count,), jnp.int32),
            dma, dma,
        ],
        compiler_params=pltpu.CompilerParams(vmem_limit_bytes=40 * 1024 * 1024),
    )(tabs, ext, coarse)
    return coarse.reshape((crows, 1) + tile), factor.reshape((crows, 1) + tile)


def solution(mesh):
    in_specs = (
        P("agg", "col", None, None),
        P("agg", "col"),
        P("agg"),
        P("agg", None, None),
        P("agg", None),
    )
    out_specs = (P("agg", "col", None, None), P("agg", "col", None, None))
    return jax.shard_map(
        functools.partial(on_device, mesh.shape["agg"], mesh.shape["col"]),
        mesh=mesh, in_specs=in_specs, out_specs=out_specs, check_vma=False,
    )
```

```python
import functools

import jax
import jax.numpy as jnp
from jax import lax
from jax.experimental import pallas as pl
from jax.experimental.pallas import tpu as pltpu
from jax.sharding import PartitionSpec as P

SWEEPS = 2
MESH = pl.DeviceIdType.MESH
BF = jnp.bfloat16
F32 = jnp.float32


def pack(tile, dtype):
    width = tile.shape[-1]
    lanes = 2 * width // 3
    half = width // 2
    rest = tile[:, lanes:]
    return tile[:, :lanes].astype(dtype), jnp.concatenate([rest[:half], rest[half:]], axis=1).astype(dtype)


def put(ref, index, tile):
    left, rest = pack(tile, ref.dtype)
    width = tile.shape[-1]
    ref[index, 0:width] = left
    ref[index, width:] = rest


def unpack(tile, width):
    half = width // 2
    rest = tile[width:]
    fold = width - tile.shape[-1]
    right = jnp.concatenate([rest[:, :fold], rest[:, fold:]], axis=0)
    return jnp.concatenate([tile[:width], right], axis=1)


def gather_kernel(
    dims, agg_hbm, fcol_hbm, ccol_hbm, fine_hbm, prolong_hbm, ext, coarse_hbm, plan_hbm,
    fine, own_prolong, turned, near, seg, own_pack, coarse_v, sums, pair_out, pair_in, y_out, y_in,
    agg_v, fcol_v, ccol_v, tab_v, tab, cls, order, table, plan,
    i_sem, in_sem, t_sem, t_send, t_recv, o_sem,
    h_send, h_recv, p_send, p_recv, y_send, y_recv, e_send, e_recv, l_sem, c_sem,
):
    groups, peers, rows, crows, slots, width = dims
    a = lax.axis_index("agg")
    c = lax.axis_index("col")
    c1 = c + 1 - 2 * (c % 2)
    c2 = (c + 2) % peers
    c3 = c2 + 1 - 2 * (c2 % 2)
    has_prev = a > 0
    has_next = a < groups - 1
    parity = a % 2
    partner_agg = a + 1 - 2 * parity
    relay_to = a + 2 - 4 * parity
    relay_from = a - 2 + 4 * parity
    can_relay = (relay_to >= 0) & (relay_to < groups)
    has_other = (relay_from >= 0) & (relay_from < groups)
    alone = rows // (2 * peers)
    both = rows // 4
    direct = alone + both
    o_some = crows * slots
    half = crows // 2
    odd = parity == 1
    even = parity == 0
    has_far = a > 1
    has_ahead = a < groups - 2

    blocks = [(c * alone, alone), (peers * alone + (c % 2) * both, both)]
    blocks += [(other * alone, alone) for other in (c1, c2, c3)]
    blocks += [(peers * alone + (c1 % 2) * both, both)]

    def take(j):
        start, size = blocks[j]
        return pltpu.make_async_copy(
            prolong_hbm.at[pl.ds(start, size)], own_prolong.at[pl.ds(start, size)], in_sem.at[j]
        )

    for j in range(2):
        take(j).start()
    take_ints = [
        pltpu.make_async_copy(src, dst, i_sem.at[j])
        for j, (src, dst) in enumerate(((agg_hbm, agg_v), (fcol_hbm, fcol_v), (ccol_hbm, ccol_v)))
    ]
    for copy in take_ints:
        copy.start()
    for j in range(2, len(blocks)):
        take(j).start()
    take_fine = pltpu.make_async_copy(fine_hbm, fine, in_sem.at[6])
    take_fine.start()

    barrier = pltpu.get_barrier_semaphore()
    for other in (c1, c2, c3):
        pl.semaphore_signal(barrier, inc=1, device_id=(a, other), device_id_type=MESH)

    @pl.when(has_prev)
    def _():
        pl.semaphore_signal(barrier, inc=1, device_id=(a - 1, c), device_id_type=MESH)

    @pl.when(has_next)
    def _():
        pl.semaphore_signal(barrier, inc=1, device_id=(a + 1, c), device_id_type=MESH)

    @pl.when(has_far)
    def _():
        pl.semaphore_signal(barrier, inc=1, device_id=(a - 2, c), device_id_type=MESH)

    @pl.when(has_ahead)
    def _():
        pl.semaphore_signal(barrier, inc=1, device_id=(a + 2, c), device_id_type=MESH)

    tab_v[2] = jnp.zeros(tab_v.shape[1:], jnp.int32)
    for copy in take_ints:
        copy.wait()
    tab_v[2, 0:1, 0:rows] = agg_v[...]
    tab_v[2, 1:1 + crows, 0:slots] = ccol_v[...]
    tab_v[2, 1 + crows:2 + crows, 0:rows] = fcol_v[...]

    def remote(src, dst, send, recv, device):
        return pltpu.make_async_remote_copy(
            src_ref=src, dst_ref=dst, send_sem=send, recv_sem=recv,
            device_id=device, device_id_type=MESH,
        )

    def pack_own(j):
        start, size = blocks[j]

        def body(k, carry):
            put(near, rows + start + k, own_prolong[start + k].astype(F32))
            return carry
        lax.fori_loop(0, size, body, 0)

    for j in range(2):
        take(j).wait()
        pack_own(j)

    @pl.when((a > 1) & (a < groups - 2))
    def _():
        pl.semaphore_wait(barrier, 7)

    @pl.when((a == 1) | (a == groups - 2))
    def _():
        pl.semaphore_wait(barrier, 6)

    @pl.when((a == 0) | (a == groups - 1))
    def _():
        pl.semaphore_wait(barrier, 5)

    def ints_to(j):
        ahead = (1, -1, 2)[j]
        return remote(tab_v.at[2], tab_v.at[(1, 3, 0)[j]], t_send.at[j], t_recv.at[j], (a + ahead, c))

    def tile_of(who, k):
        if k < alone:
            return who * alone + k
        return peers * alone + (who % 2) * both + k - alone

    def block_at(side):
        return ((1 - parity) if side == 0 else parity) * 2 * rows

    def push(k):
        src = near.at[pl.ds(rows + tile_of(c, k), 1)]
        dst = near.at[pl.ds(parity * 2 * rows + tile_of(c, k), 1)]
        return remote(src, dst, h_send.at[0, 0, k], h_recv.at[0, 0, k], (partner_agg, c))

    def relay(k):
        src = near.at[pl.ds(block_at(0) + tile_of(c, k), 1)]
        dst = near.at[pl.ds(parity * 2 * rows + tile_of(c, k), 1)]
        return remote(src, dst, h_send.at[1, 0, k], h_recv.at[1, 0, k], (relay_to, c))

    def pass_on(side, kind, who, k, device):
        view = near.at[pl.ds(block_at(side) + tile_of(who, k), 1)]
        return remote(view, view, h_send.at[side, kind, k], h_recv.at[side, kind, k], device)

    def arrived(side, k):
        pass_on(side, 0, c, k, (a, c1)).wait_recv()
        if side == 0:
            @pl.when(can_relay)
            def _():
                relay(k).start()
        if k < alone:
            pass_on(side, 2, c, k, (a, c2)).start()
        pass_on(side, 1, c, k, (a, c1)).start()

    def crossed(side, k):
        pass_on(side, 2, c2, k, (a, c2)).wait_recv()
        pass_on(side, 3, c2, k, (a, c1)).start()

    def complete(side):
        for k in range(direct):
            pass_on(side, 1, c1, k, (a, c1)).wait_recv()
            if k < alone:
                pass_on(side, 3, c3, k, (a, c1)).wait_recv()

    def left(side):
        for k in range(direct):
            pass_on(side, 1, c, k, (a, c1)).wait_send()
            if k < alone:
                pass_on(side, 2, c, k, (a, c2)).wait_send()
                pass_on(side, 3, c2, k, (a, c1)).wait_send()

    def other_side(step, *args):
        pl.when(has_other)(functools.partial(step, 1, *args))

    can_send = (has_next, has_prev, has_ahead)
    can_take = (has_prev, has_next, has_far)

    def ints_all(act):
        for j in range(3):
            @pl.when(can_send[j])
            def _(j=j):
                act(ints_to(j))

    ints_all(lambda copy: copy.start())
    for k in range(direct):
        push(k).start()
    for j in range(2, len(blocks)):
        take(j).wait()
        pack_own(j)

    def to_scalar(g):
        return pltpu.make_async_copy(tab_v.at[g], tab.at[g], t_sem.at[g])

    to_scalar(2).start()

    def integers():
        to_scalar(2).wait()
        for j in range(3):
            @pl.when(can_take[j])
            def _(j=j):
                ints_to(j).wait_recv()
                to_scalar((1, 3, 0)[j]).start()
        for j in range(3):
            @pl.when(can_take[j])
            def _(j=j):
                to_scalar((1, 3, 0)[j]).wait()

    chores = [integers]
    row_base = a * crows

    def place_of(i):
        return tab[2, 1 + crows, i] - (a - 1) * rows

    def classify(i, carry):
        place = jnp.clip(place_of(i), 0, 3 * rows - 1)
        target = tab[1 + place // rows, 0, place % rows]
        r = jnp.clip(tab[2, 0, i] - row_base, 0, crows - 1)
        q = 0
        for s in range(1, slots):
            q = jnp.where(tab[2, 1 + r, s] == target, s, q)
        cls[i] = (r * slots + q) * rows + i
        return carry

    chores.append(lambda: lax.fori_loop(0, rows, classify, 0))

    def rank(i, carry):
        key = cls[i]
        below = 0
        for j in range(rows):
            below = below + jnp.where(cls[j] < key, 1, 0)
        order[rows + i] = below
        return carry

    chores.append(lambda: lax.fori_loop(0, rows, rank, 0))

    def place_key(k, carry):
        key = 0
        for i in range(rows):
            key = key + jnp.where(order[rows + i] == k, cls[i], 0)
        order[k] = key
        return carry

    chores.append(lambda: lax.fori_loop(0, rows, place_key, 0))

    def ends(s, carry):
        upto = 0
        some = 0
        for i in range(rows):
            own_class = cls[i] // rows
            upto = upto + jnp.where(own_class <= s, 1, 0)
            some = jnp.where(own_class == s, 1, some)
        table[s] = jnp.maximum(upto - 1, 0)
        table[o_some + s] = some
        return carry

    chores.append(lambda: lax.fori_loop(0, crows * slots, ends, 0))

    part_count = crows + half
    diag = list(range(crows))
    quarter = rows // 4

    def lift_at(k, total, prior):
        key = order[k]
        i = key % rows
        earlier = order[jnp.maximum(k - 1, 0)]
        goes_on = jnp.where(earlier // rows == key // rows, 1, 0)
        carried = jnp.dot(fine[i], prior(i), preferred_element_type=F32).astype(BF)
        lifted = jnp.dot(turned[i], carried, preferred_element_type=F32)
        total = lifted + total * goes_on.astype(F32)
        seg[k] = total
        return total

    def lift_all(prior):
        def step(k, total):
            return lift_at(k, total, prior)

        lax.fori_loop(0, rows, step, jnp.zeros((width, width), F32), unroll=4)

    def near_prior(i):
        place = jnp.clip(place_of(i), 0, 3 * rows - 1)
        return unpack(near[place], width)

    def part(r, q):
        s = r * slots + q
        return seg[table[s]] * table[o_some + s].astype(F32)

    pp, prev, own = (g * slots * crows for g in range(3))

    def to_core(at, i, through=False):
        here = ext.at[pl.ds(at + i, 1)]
        src = own_pack.at[pl.ds(i, 1)] if at == own and not through else here
        return remote(src, here, e_send.at[0, at + i], e_recv.at[at + i], (a, c1))

    def to_next(i):
        return remote(
            own_pack.at[pl.ds(i, 1)], ext.at[pl.ds(prev + i, 1)],
            e_send.at[1, own + i], e_recv.at[prev + i], (a + 1, c),
        )

    def to_ahead(i):
        return remote(
            own_pack.at[pl.ds(i, 1)], ext.at[pl.ds(pp + i, 1)],
            e_send.at[2, own + i], e_recv.at[pp + i], (a + 2, c),
        )

    def to_behind(i):
        return remote(
            ext.at[pl.ds(pp + i, 1)], ext.at[pl.ds(prev + i, 1)],
            e_send.at[1, pp + i], e_recv.at[prev + i], (a - 1, c),
        )

    def to_other(i):
        return remote(
            own_pack.at[pl.ds(i, 1)], ext.at[pl.ds(own + i, 1)],
            e_send.at[2, own + i], e_recv.at[own + i], (a, c2),
        )

    def pass_next(i):
        return remote(
            ext.at[pl.ds(own + i, 1)], ext.at[pl.ds(prev + i, 1)],
            e_send.at[1, own + i], e_recv.at[prev + i], (a + 1, c),
        )

    def keep(i):
        return pltpu.make_async_copy(own_pack.at[i], ext.at[own + i], l_sem.at[i])

    def keep_coarse(r):
        return pltpu.make_async_copy(coarse_v.at[r], coarse_hbm.at[r], c_sem.at[r])

    def lift_diag(quarter_at):
        def step(k, carry):
            key = order[k]
            i = key % rows
            earlier = order[jnp.maximum(k - 1, 0)]
            goes_on = jnp.where((k > 0) & (earlier // rows == key // rows), 1, 0)
            carried = jnp.dot(fine[i], own_prolong[i], preferred_element_type=F32).astype(BF)
            lifted = jnp.dot(turned[i], carried, preferred_element_type=F32)
            seg[k] = lifted + seg[jnp.maximum(k - 1, 0)] * goes_on.astype(F32)
            return carry

        if quarter_at == 0:
            take_fine.wait()
            seg[0] = jnp.zeros((width, width), F32)
        lax.fori_loop(quarter_at * quarter, (quarter_at + 1) * quarter, step, 0, unroll=True)

    def send_diag():
        for r in diag:
            value = part(r, 0)
            coarse_v[r] = value
            put(own_pack, r, value)
            keep(r).start()
            keep_coarse(r).start()
            to_other(r).start()
            to_core(own, r).start()

            @pl.when(has_next)
            def _(r=r):
                to_next(r).start()

    plan_out = pltpu.make_async_copy(plan, plan_hbm, o_sem)

    def matches(i, carry):
        row = crows + i // slots
        q = i % slots
        origin = row_base - 2 * crows

        def column(at, n):
            return tab[at // crows, 1 + at % crows, n] - origin

        col = column(row, q)
        lowest = jnp.minimum(row, col)
        lowest_at = jnp.clip(lowest, 0, 3 * crows - 1)
        plan[i // slots, q * 8] = (lowest_at // crows) * slots * crows + lowest_at % crows
        plan[i // slots, q * 8 + 4] = jnp.where(row > col, 0, jnp.where(row < col, 1, 2))
        for m in range(1, slots):
            k = column(row, m)
            at = jnp.clip(k, 0, 3 * crows - 1)
            pick = -1
            for n in range(slots):
                spot = ((at // crows) * slots + n) * crows + at % crows
                pick = jnp.where(column(at, n) == col, spot, pick)
            plan[i // slots, q * 8 + m] = jnp.where(k < lowest, pick, -1)
        return carry

    def planned():
        lax.fori_loop(0, 2 * crows * slots, matches, 0)
        plan_out.start()

    chores.append(planned)

    lag = 2
    for k in range(direct + lag):
        if k < direct:
            arrived(0, k)
        if k >= lag:
            other_side(arrived, k - lag)
        if k == 0:
            for i in range(rows):
                turned[i] = own_prolong[i].astype(F32).T.astype(BF)
        if k < 5:
            for chore in chores[(0, 1, 2, 4, 5)[k]:(1, 2, 4, 5, 6)[k]]:
                chore()
        if 0 <= k - 3 < alone:
            crossed(0, k - 3)
        if 0 <= k - 5 < alone:
            other_side(crossed, k - 5)
        if 3 <= k < 7:
            pl.when(c == 0)(functools.partial(lift_diag, k - 3))
        if k == 7:
            pl.when(c == 0)(send_diag)
    assert direct + lag >= 8
    def landed(at, i):
        view = ext.at[pl.ds(at + i, 1)]
        remote(view, view, e_send.at[0, at + i], e_recv.at[at + i], (a, c1)).wait_recv()

    def own_ready(i, act):
        act(to_core(own, i))

        @pl.when(even & has_next)
        def _():
            act(to_next(i))

        @pl.when(has_ahead)
        def _():
            act(to_ahead(i))

    def neighbours(i):
        @pl.when(has_far)
        def _():
            landed(pp, i)

            @pl.when(odd)
            def _():
                to_behind(i).start()

            to_core(pp, i).start()

        @pl.when(odd)
        def _():
            landed(prev, i)
            to_core(prev, i).start()

    def relayed(i):
        @pl.when(even & has_far)
        def _():
            landed(prev, i)
            to_core(prev, i).start()

    def flow(tiles, finish, lag):
        count = len(tiles)
        for k in range(count + 2 * lag):
            if k < count:
                finish(k)
                keep(tiles[k]).start()
                own_ready(tiles[k], lambda copy: copy.start())
            if 0 <= k - lag < count:
                neighbours(tiles[k - lag])
            if 0 <= k - 2 * lag < count:
                relayed(tiles[k - 2 * lag])

    def flow_sent(tiles):
        for i in tiles:
            keep(i).wait()
            own_ready(i, lambda copy: copy.wait_send())

            @pl.when(has_far)
            def _(i=i):
                to_core(pp, i).wait_send()

                @pl.when(odd)
                def _():
                    to_behind(i).wait_send()

            @pl.when(has_prev)
            def _(i=i):
                to_core(prev, i).wait_send()

    def arrivals(tiles):
        for i in tiles:
            landed(own, i)

            @pl.when(has_prev)
            def _(i=i):
                landed(prev, i)

            @pl.when(has_far)
            def _(i=i):
                landed(pp, i)

    def set_of(who):
        tiles = [(j, who) for j in range(crows)]
        return tiles + [((who - 2) * half + j, 1) for j in range(half)]

    def arrivals_diag():
        for r in diag:
            landed(own, r)

            @pl.when(has_prev)
            def _(r=r):
                landed(prev, r)

    @pl.when(c == 0)
    def _():
        complete(0)
        other_side(complete)
        for r in diag:
            @pl.when(has_prev)
            def _(r=r):
                landed(prev, r)
                to_core(prev, r).start()
        arrivals([q * crows + r for q in range(1, slots) for r in range(crows)])
        for r in diag:
            keep(r).wait()
            to_other(r).wait_send()
            to_core(own, r).wait_send()

            @pl.when(has_next)
            def _(r=r):
                to_next(r).wait_send()

            @pl.when(has_prev)
            def _(r=r):
                to_core(prev, r).wait_send()

    @pl.when(c > 0)
    def _():
        complete(0)
        other_side(complete)
        take_fine.wait()
        lift_all(near_prior)

    @pl.when(c == 1)
    def _():
        listed = [(f, j) for j in range(part_count) for f in (2, 3)]

        def cross(k):
            f, j = listed[k]
            at = (f - 2) * part_count + j
            return remote(
                y_out.at[pl.ds(at, 1)], y_in.at[pl.ds(j, 1)], y_send.at[at], y_recv.at[j], (a, f)
            )

        tiles = []
        for k, (f, j) in enumerate(listed):
            r, q = set_of(f)[j]
            tiles.append(q * crows + r)
            put(y_out, (f - 2) * part_count + j, part(r, q))
            cross(k).start()

        def finish(k):
            f, j = listed[k]
            r, q = set_of(f)[j]
            at = (f - 2) * part_count + j
            view = y_in.at[pl.ds(at, 1)]
            remote(view, view, y_send.at[at], y_recv.at[at], (a, f)).wait_recv()
            value = part(r, q) + unpack(y_in[at].astype(F32), width)
            if q == 1:
                coarse_v[r] = value
                keep_coarse(r).start()
            put(own_pack, q * crows + r, value)

        flow(tiles, finish, 4)
        arrivals_diag()
        for k in range(len(listed)):
            cross(k).wait_send()
        flow_sent(tiles)

    @pl.when(c > 1)
    def _():
        mine = [(j, c) for j in range(crows)] + [((c - 2) * half + j, 1) for j in range(half)]
        theirs = [(j, c1) for j in range(crows)] + [((c1 - 2) * half + j, 1) for j in range(half)]

        def swap(j):
            return remote(
                pair_out.at[pl.ds(j, 1)], pair_in.at[pl.ds(j, 1)], p_send.at[j], p_recv.at[j], (a, c1)
            )

        def cross(j):
            return remote(
                y_out.at[pl.ds(j, 1)], y_in.at[pl.ds((c - 2) * part_count + j, 1)],
                y_send.at[j], y_recv.at[(c - 2) * part_count + j], (a, 1),
            )

        for j, (r, q) in enumerate(theirs):
            put(pair_out, j, part(r, q))
            swap(j).start()
        for j, (r, q) in enumerate(mine):
            swap(j).wait_recv()
            value = part(r, q) + unpack(pair_in[j].astype(F32), width)
            sums[j] = value
            put(y_out, j, value)
            cross(j).start()

        @pl.when(c == 2)
        def _():
            for r in diag:
                landed(own, r)
                to_core(own, r, True).start()

                @pl.when(has_next)
                def _(r=r):
                    pass_next(r).start()

        def finish(j):
            r, q = mine[j]
            view = y_in.at[pl.ds(j, 1)]
            remote(view, view, y_send.at[j], y_recv.at[j], (a, 1)).wait_recv()
            value = sums[j] + unpack(y_in[j].astype(F32), width)
            if j < crows:
                coarse_v[j] = value
                keep_coarse(j).start()
            put(own_pack, q * crows + r, value)

        tiles = [q * crows + r for r, q in mine]
        flow(tiles, finish, 2)

        @pl.when(c == 2)
        def _():
            for r in diag:
                @pl.when(has_prev)
                def _(r=r):
                    landed(prev, r)
                    to_core(prev, r).start()

        @pl.when(c == 3)
        def _():
            arrivals_diag()

        arrivals([q * crows + r for r, q in theirs])
        for j in range(part_count):
            swap(j).wait_send()
            cross(j).wait_send()
        flow_sent(tiles)

        @pl.when(c == 2)
        def _():
            for r in diag:
                to_core(own, r, True).wait_send()

                @pl.when(has_next)
                def _(r=r):
                    pass_next(r).wait_send()

                @pl.when(has_prev)
                def _(r=r):
                    to_core(prev, r).wait_send()

    for r in range(crows):
        keep_coarse(r).wait()

    plan_out.wait()
    ints_all(lambda copy: copy.wait_send())
    for k in range(direct):
        push(k).wait_send()

    @pl.when(can_relay)
    def _():
        for k in range(direct):
            relay(k).wait_send()

    left(0)
    other_side(left)


def sweep_kernel(
    dims, plan, ext, coarse, coarse_out, factor_out,
    first, acc, done, masks, need, tiles, terms, in_sem, out_sem,
):
    crows, slots, width = dims
    count = slots * crows
    group = 4
    c = lax.axis_index("col")
    give = pltpu.make_async_copy(coarse, coarse_out, in_sem)
    give.start()
    ids_r = lax.broadcasted_iota(jnp.int32, (width, width), 0)
    ids_c = lax.broadcasted_iota(jnp.int32, (width, width), 1)
    masks[0] = jnp.ones((width, width), BF)
    masks[1] = (ids_c < ids_r).astype(F32).astype(BF)
    masks[2] = (ids_c > ids_r).astype(F32).astype(BF)
    masks[3] = jnp.zeros((width, width), BF)

    def planned(row, q, j):
        return plan[row - crows, q * 8 + j]

    def spot(row, q):
        return ((row // crows) * slots + q) * crows + row % crows

    for i in range(count, 3 * count):
        need[i] = 0
    for r in range(crows):
        row = 2 * crows + r
        need[spot(row, c)] = 1
        need[planned(row, c, 0)] = 1
        for m in range(1, slots):
            pick = planned(row, c, m)

            @pl.when(pick >= 0)
            def _(row=row, m=m, pick=pick):
                need[spot(row, m)] = 1
                need[pick] = 1

    def list_terms(row, q, wanted, at, size):
        for m in range(1, slots):
            pick = planned(row, q, m)
            terms[0, size] = at
            terms[1, size] = spot(row, m)
            terms[2, size] = pick
            size = size + jnp.where(pick >= 0, wanted, 0)
        return size

    def pad_terms(size):
        for j in range(group - 1):
            terms[0, size + j] = 2 * count + group
            terms[1, size + j] = 2 * count
            terms[2, size + j] = 2 * count

    def add_terms(size, tile):
        def body(k, carry):
            for j in range(group):
                t = k * group + j
                product = jnp.dot(tile(terms[1, t]), tile(terms[2, t]), preferred_element_type=F32)
                acc[terms[0, t]] += product
            return carry

        lax.fori_loop(0, (size + group - 1) // group, body, 0)

    def clear(k, carry):
        acc[k] = jnp.zeros((width, width), F32)
        return carry

    def relax(own, diag_at, kind, start, total, tile):
        diag = tile(diag_at)
        mine = tile(own)
        left = jnp.where(kind == 0, mine, diag * masks[1])
        right = jnp.where(kind == 1, mine, diag * masks[2])
        value = start - total - jnp.dot(left, right, preferred_element_type=F32)
        chosen = jnp.where(ids_c == ids_r, diag.astype(F32), 0.0)
        inverse = 1.0 / jnp.maximum(jnp.sum(chosen, axis=0, keepdims=True), 1.0)
        scaled = masks[jnp.where(kind == 0, 0, jnp.where(kind == 1, 3, 1))].astype(F32)
        return value * jnp.where(scaled > 0.5, inverse, 1.0)

    def old(i):
        return unpack(ext[i], width)

    def new(i):
        return first[i]

    size = 0
    found = 0
    for row in range(crows, 3 * crows):
        for q in range(slots):
            wanted = need[spot(row, q)]
            tiles[0, found] = spot(row, q)
            tiles[1, found] = planned(row, q, 0)
            tiles[2, found] = planned(row, q, 4)
            size = list_terms(row, q, wanted, found, size)
            found = found + wanted
    pad_terms(size)
    for j in range(group - 1):
        tiles[0, found + j] = 3 * count
        tiles[1, found + j] = 2 * count
        tiles[2, found + j] = 0
    lax.fori_loop(0, found, clear, 0)
    add_terms(size, old)

    def sweep(k, carry):
        for j in range(group):
            t = k * group + j
            i = jnp.minimum(tiles[0, t], 3 * count - 1)
            start = old(i).astype(F32)
            first[tiles[0, t]] = relax(i, tiles[1, t], tiles[2, t], start, acc[t], old).astype(BF)
        return carry

    lax.fori_loop(0, (found + group - 1) // group, sweep, 0)

    size = 0
    for r in range(crows):
        size = list_terms(2 * crows + r, c, 1, r, size)
        acc[r] = jnp.zeros((width, width), F32)
    pad_terms(size)
    add_terms(size, new)

    def put_out(r):
        return pltpu.make_async_copy(done.at[r], factor_out.at[r], out_sem.at[r])

    for r in range(crows):
        row = 2 * crows + r
        done[r] = relax(spot(row, c), planned(row, c, 0), planned(row, c, 4), coarse[r], acc[r], new)
        put_out(r).start()
    give.wait()
    for r in range(crows):
        put_out(r).wait()


def on_device(groups, peers, fine_tiles, fine_cols, agg_of, prolong, coarse_cols):
    rows, width = prolong.shape[0], prolong.shape[-1]
    crows, slots = coarse_cols.shape
    assert SWEEPS == 2 and slots == peers == 4 and fine_tiles.shape[1] == 1
    assert groups % 2 == 0 and groups >= 4 and crows % 2 == 0
    direct = rows // (2 * peers) + rows // 4
    dma = pltpu.SemaphoreType.DMA
    tile = (width, width)
    packed = (width + width // 2, 2 * width // 3)
    count = slots * crows
    pairs = crows + crows // 2
    room = (-(-(crows + 2) // 8) * 8, 128)
    vmem = pl.BlockSpec(memory_space=pltpu.VMEM)
    smem = pl.BlockSpec(memory_space=pltpu.SMEM)
    anywhere = pl.BlockSpec(memory_space=pl.ANY)
    hbm = pl.BlockSpec(memory_space=pltpu.HBM)
    ext, coarse, plan = pl.pallas_call(
        functools.partial(gather_kernel, (groups, peers, rows, crows, slots, width)),
        out_shape=(
            pltpu.VMEM((3 * count,) + packed, BF),
            pltpu.VMEM((crows,) + tile, F32),
            pltpu.VMEM((2 * crows, 128), jnp.int32),
        ),
        in_specs=[hbm] * 5,
        out_specs=(anywhere, anywhere, anywhere),
        scratch_shapes=[
            pltpu.VMEM((rows,) + tile, BF),
            pltpu.VMEM((rows,) + tile, BF),
            pltpu.VMEM((rows,) + tile, BF),
            pltpu.VMEM((3 * rows,) + packed, BF),
            pltpu.VMEM((rows,) + tile, F32),
            pltpu.VMEM((count,) + packed, BF),
            pltpu.VMEM((crows,) + tile, F32),
            pltpu.VMEM((pairs,) + tile, F32),
            pltpu.VMEM((pairs,) + packed, BF),
            pltpu.VMEM((pairs,) + packed, BF),
            pltpu.VMEM((2 * pairs,) + packed, BF),
            pltpu.VMEM((2 * pairs,) + packed, BF),
            pltpu.VMEM((1, rows), jnp.int32),
            pltpu.VMEM((1, rows), jnp.int32),
            pltpu.VMEM((crows, slots), jnp.int32),
            pltpu.VMEM((4,) + room, jnp.int32),
            pltpu.SMEM((4,) + room, jnp.int32),
            pltpu.SMEM((rows,), jnp.int32),
            pltpu.SMEM((2 * rows,), jnp.int32),
            pltpu.SMEM((2 * count,), jnp.int32),
            pltpu.SMEM((2 * crows, 128), jnp.int32),
            dma((3,)), dma((7,)), dma((4,)), dma((3,)), dma((3,)), dma,
            dma((2, 4, direct)), dma((2, 4, direct)),
            dma((pairs,)), dma((pairs,)), dma((2 * pairs,)), dma((2 * pairs,)),
            dma((3, 3 * count)), dma((3 * count,)), dma((count,)), dma((crows,)),
        ],
        compiler_params=pltpu.CompilerParams(
            collective_id=0, has_side_effects=True, vmem_limit_bytes=56 * 1024 * 1024
        ),
    )(agg_of.reshape(1, rows), fine_cols.reshape(1, rows), coarse_cols, fine_tiles.reshape((rows,) + tile), prolong)
    out = jax.ShapeDtypeStruct((crows,) + tile, F32)
    coarse, factor = pl.pallas_call(
        functools.partial(sweep_kernel, (crows, slots, width)),
        out_shape=(out, out),
        in_specs=[smem, vmem, vmem],
        out_specs=(anywhere, anywhere),
        scratch_shapes=[
            pltpu.VMEM((3 * count + 1,) + tile, BF),
            pltpu.VMEM((2 * count + 5,) + tile, F32),
            pltpu.VMEM((crows,) + tile, F32),
            pltpu.VMEM((4,) + tile, BF),
            pltpu.SMEM((3 * count,), jnp.int32),
            pltpu.SMEM((3, 2 * count + 4), jnp.int32),
            pltpu.SMEM((3, 2 * count * (slots - 1) + 4), jnp.int32),
            dma, dma((crows,)),
        ],
        compiler_params=pltpu.CompilerParams(vmem_limit_bytes=40 * 1024 * 1024),
    )(plan, ext, coarse)
    return coarse.reshape((crows, 1) + tile), factor.reshape((crows, 1) + tile)


def solution(mesh):
    in_specs = (
        P("agg", "col", None, None),
        P("agg", "col"),
        P("agg"),
        P("agg", None, None),
        P("agg", None),
    )
    out_specs = (P("agg", "col", None, None), P("agg", "col", None, None))
    return jax.shard_map(
        functools.partial(on_device, mesh.shape["agg"], mesh.shape["col"]),
        mesh=mesh, in_specs=in_specs, out_specs=out_specs, check_vma=False,
    )
```

```python
import functools

import jax
import jax.numpy as jnp
from jax import lax
from jax.experimental import pallas as pl
from jax.experimental.pallas import tpu as pltpu
from jax.sharding import PartitionSpec as P

SWEEPS = 2
EXCHANGE_PARTS = 1
HALO_PARTS = 1
MESH = pl.DeviceIdType.MESH
BF = jnp.bfloat16
F32 = jnp.float32


def pack(tile, dtype):
    width = tile.shape[-1]
    lanes = 2 * width // 3
    half = width // 2
    rest = tile[:, lanes:]
    return tile[:, :lanes].astype(dtype), jnp.concatenate([rest[:half], rest[half:]], axis=1).astype(dtype)


def put(ref, index, tile):
    left, rest = pack(tile, ref.dtype)
    width = tile.shape[-1]
    ref[index, 0:width] = left
    ref[index, width:] = rest


def unpack(tile, width):
    half = width // 2
    rest = tile[width:]
    fold = width - tile.shape[-1]
    right = jnp.concatenate([rest[:, :fold], rest[:, fold:]], axis=0)
    return jnp.concatenate([tile[:width], right], axis=1)


def shares_of(rows, peers):
    alone = 3 * rows // (4 * peers)
    return alone, (rows - peers * alone) // 2


def gather_kernel(
    dims, agg_hbm, fcol_hbm, ccol_hbm, fine_hbm, prolong_hbm, ext, coarse_hbm, plan_hbm,
    fine, own_prolong, turned, near, seg, own_pack, coarse_v, sums, pair_out, pair_in, y_out, y_in,
    agg_v, fcol_v, ccol_v, tab_v, tab, cls, order, table, plan,
    i_sem, in_sem, t_sem, t_send, t_recv, o_sem,
    h_send, h_recv, p_send, p_recv, y_send, y_recv, e_send, e_recv, l_sem, c_sem,
):
    groups, peers, rows, crows, slots, width = dims
    a = lax.axis_index("agg")
    c = lax.axis_index("col")
    c1 = c + 1 - 2 * (c % 2)
    c2 = (c + 2) % peers
    c3 = c2 + 1 - 2 * (c2 % 2)
    has_prev = a > 0
    has_next = a < groups - 1
    parity = a % 2
    partner_agg = a + 1 - 2 * parity
    relay_to = a + 2 - 4 * parity
    relay_from = a - 2 + 4 * parity
    can_relay = (relay_to >= 0) & (relay_to < groups)
    has_other = (relay_from >= 0) & (relay_from < groups)
    alone, both = shares_of(rows, peers)
    direct = alone + both
    o_some = crows * slots
    half = crows // 2
    odd = parity == 1
    even = parity == 0
    has_far = a > 1
    has_ahead = a < groups - 2

    blocks = [(c * alone, alone), (peers * alone + (c % 2) * both, both)]
    blocks += [(other * alone, alone) for other in (c1, c2, c3)]
    blocks += [(peers * alone + (c1 % 2) * both, both)]

    def take(j):
        start, size = blocks[j]
        return pltpu.make_async_copy(
            prolong_hbm.at[pl.ds(start, size)], own_prolong.at[pl.ds(start, size)], in_sem.at[j]
        )

    for j in range(2):
        take(j).start()
    take_ints = [
        pltpu.make_async_copy(src, dst, i_sem.at[j])
        for j, (src, dst) in enumerate(((agg_hbm, agg_v), (fcol_hbm, fcol_v), (ccol_hbm, ccol_v)))
    ]
    for copy in take_ints:
        copy.start()
    for j in range(2, len(blocks)):
        take(j).start()
    take_fine = pltpu.make_async_copy(fine_hbm, fine, in_sem.at[6])
    take_fine.start()

    barrier = pltpu.get_barrier_semaphore()
    for other in (c1, c2, c3):
        pl.semaphore_signal(barrier, inc=1, device_id=(a, other), device_id_type=MESH)

    @pl.when(has_prev)
    def _():
        pl.semaphore_signal(barrier, inc=1, device_id=(a - 1, c), device_id_type=MESH)

    @pl.when(has_next)
    def _():
        pl.semaphore_signal(barrier, inc=1, device_id=(a + 1, c), device_id_type=MESH)

    @pl.when(has_far)
    def _():
        pl.semaphore_signal(barrier, inc=1, device_id=(a - 2, c), device_id_type=MESH)

    @pl.when(has_ahead)
    def _():
        pl.semaphore_signal(barrier, inc=1, device_id=(a + 2, c), device_id_type=MESH)

    tab_v[2] = jnp.zeros(tab_v.shape[1:], jnp.int32)
    for copy in take_ints:
        copy.wait()
    tab_v[2, 0:1, 0:rows] = agg_v[...]
    tab_v[2, 1:1 + crows, 0:slots] = ccol_v[...]
    tab_v[2, 1 + crows:2 + crows, 0:rows] = fcol_v[...]

    def remote(src, dst, send, recv, device):
        return pltpu.make_async_remote_copy(
            src_ref=src, dst_ref=dst, send_sem=send, recv_sem=recv,
            device_id=device, device_id_type=MESH,
        )

    def piece(ref, index, h, parts):
        size = ref.shape[1] // parts
        return ref.at[pl.ds(index, 1), pl.ds(h * size, size)]

    def pack_own(j):
        start, size = blocks[j]

        def body(k, carry):
            put(near, rows + start + k, own_prolong[start + k].astype(F32))
            return carry
        lax.fori_loop(0, size, body, 0)

    for j in range(2):
        take(j).wait()
        pack_own(j)

    @pl.when((a > 1) & (a < groups - 2))
    def _():
        pl.semaphore_wait(barrier, 7)

    @pl.when((a == 1) | (a == groups - 2))
    def _():
        pl.semaphore_wait(barrier, 6)

    @pl.when((a == 0) | (a == groups - 1))
    def _():
        pl.semaphore_wait(barrier, 5)

    def ints_to(j):
        ahead = (1, -1, 2)[j]
        return remote(tab_v.at[2], tab_v.at[(1, 3, 0)[j]], t_send.at[j], t_recv.at[j], (a + ahead, c))

    def tile_of(who, k):
        if k < alone:
            return who * alone + k
        return peers * alone + (who % 2) * both + k - alone

    def block_at(side):
        return ((1 - parity) if side == 0 else parity) * 2 * rows

    pieces = range(EXCHANGE_PARTS)

    def near_piece(index, h):
        return piece(near, index, h, EXCHANGE_PARTS)

    def push(k, h):
        src = near_piece(rows + tile_of(c, k), h)
        dst = near_piece(parity * 2 * rows + tile_of(c, k), h)
        return remote(src, dst, h_send.at[0, 0, k, h], h_recv.at[0, 0, k, h], (partner_agg, c))

    def relay(k, h):
        src = near_piece(block_at(0) + tile_of(c, k), h)
        dst = near_piece(parity * 2 * rows + tile_of(c, k), h)
        return remote(src, dst, h_send.at[1, 0, k, h], h_recv.at[1, 0, k, h], (relay_to, c))

    def pass_on(side, kind, who, k, h, device):
        view = near_piece(block_at(side) + tile_of(who, k), h)
        return remote(view, view, h_send.at[side, kind, k, h], h_recv.at[side, kind, k, h], device)

    def arrived(side, k):
        for h in pieces:
            pass_on(side, 0, c, k, h, (a, c1)).wait_recv()
            if side == 0:
                @pl.when(can_relay)
                def _(h=h):
                    relay(k, h).start()
            if k < alone:
                pass_on(side, 2, c, k, h, (a, c2)).start()
            pass_on(side, 1, c, k, h, (a, c1)).start()

    def crossed(side, k):
        for h in pieces:
            pass_on(side, 2, c2, k, h, (a, c2)).wait_recv()
            pass_on(side, 3, c2, k, h, (a, c1)).start()

    def complete(side):
        for k in range(direct):
            for h in pieces:
                pass_on(side, 1, c1, k, h, (a, c1)).wait_recv()
                if k < alone:
                    pass_on(side, 3, c3, k, h, (a, c1)).wait_recv()

    def left(side):
        for k in range(direct):
            for h in pieces:
                pass_on(side, 1, c, k, h, (a, c1)).wait_send()
                if k < alone:
                    pass_on(side, 2, c, k, h, (a, c2)).wait_send()
                    pass_on(side, 3, c2, k, h, (a, c1)).wait_send()

    def other_side(step, *args):
        pl.when(has_other)(functools.partial(step, 1, *args))

    can_send = (has_next, has_prev, has_ahead)
    can_take = (has_prev, has_next, has_far)

    def ints_all(act):
        for j in range(3):
            @pl.when(can_send[j])
            def _(j=j):
                act(ints_to(j))

    ints_all(lambda copy: copy.start())
    for k in range(direct):
        for h in pieces:
            push(k, h).start()
    for j in range(2, len(blocks)):
        take(j).wait()
        pack_own(j)

    def to_scalar(g):
        return pltpu.make_async_copy(tab_v.at[g], tab.at[g], t_sem.at[g])

    to_scalar(2).start()

    def integers():
        pl.when(c > 0)(lambda: to_scalar(2).wait())
        for j in range(3):
            @pl.when(can_take[j])
            def _(j=j):
                ints_to(j).wait_recv()
                to_scalar((1, 3, 0)[j]).start()
        for j in range(3):
            @pl.when(can_take[j])
            def _(j=j):
                to_scalar((1, 3, 0)[j]).wait()

    chores = [integers]
    row_base = a * crows

    def place_of(i):
        return tab[2, 1 + crows, i] - (a - 1) * rows

    def classify(i, carry):
        place = jnp.clip(place_of(i), 0, 3 * rows - 1)
        target = tab[1 + place // rows, 0, place % rows]
        r = jnp.clip(tab[2, 0, i] - row_base, 0, crows - 1)
        q = 0
        for s in range(1, slots):
            q = jnp.where(tab[2, 1 + r, s] == target, s, q)
        cls[i] = (r * slots + q) * rows + i
        return carry

    chores.append(lambda: lax.fori_loop(0, rows, classify, 0))

    def classify_diag(i, carry):
        r = jnp.clip(tab[2, 0, i] - row_base, 0, crows - 1)
        cls[i] = r * slots * rows + i
        return carry

    def rank(i, carry):
        key = cls[i]
        below = 0
        for j in range(rows):
            below = below + jnp.where(cls[j] < key, 1, 0)
        order[rows + i] = below
        return carry

    chores.append(lambda: lax.fori_loop(0, rows, rank, 0))

    def place_key(k, carry):
        key = 0
        for i in range(rows):
            key = key + jnp.where(order[rows + i] == k, cls[i], 0)
        order[k] = key
        return carry

    chores.append(lambda: lax.fori_loop(0, rows, place_key, 0))

    def ends(s, carry):
        upto = 0
        some = 0
        for i in range(rows):
            own_class = cls[i] // rows
            upto = upto + jnp.where(own_class <= s, 1, 0)
            some = jnp.where(own_class == s, 1, some)
        table[s] = jnp.maximum(upto - 1, 0)
        table[o_some + s] = some
        return carry

    chores.append(lambda: lax.fori_loop(0, crows * slots, ends, 0))

    part_count = crows + half
    diag = list(range(crows))
    quarter = rows // 4

    def lift_at(k, total, prior):
        key = order[k]
        i = key % rows
        earlier = order[jnp.maximum(k - 1, 0)]
        goes_on = jnp.where(earlier // rows == key // rows, 1, 0)
        carried = jnp.dot(fine[i], prior(i), preferred_element_type=F32).astype(BF)
        lifted = jnp.dot(turned[i], carried, preferred_element_type=F32)
        total = lifted + total * goes_on.astype(F32)
        seg[k] = total
        return total

    def lift_all(prior):
        def step(k, total):
            return lift_at(k, total, prior)

        lax.fori_loop(0, rows, step, jnp.zeros((width, width), F32), unroll=True)

    def near_prior(i):
        place = jnp.clip(place_of(i), 0, 3 * rows - 1)
        return unpack(near[place], width)

    def part(r, q):
        s = r * slots + q
        return seg[table[s]] * table[o_some + s].astype(F32)

    pp, prev, own = (g * slots * crows for g in range(3))

    class Group:
        def __init__(self, copies):
            self.copies = copies

        def start(self):
            for copy in self.copies:
                copy.start()

        def wait_send(self):
            for copy in self.copies:
                copy.wait_send()

    shares = range(HALO_PARTS)

    def send(src, at, dst, to, kind, device, only=None):
        return Group([
            remote(
                piece(src, at, h, HALO_PARTS), piece(ext, dst, h, HALO_PARTS),
                e_send.at[kind, to, h], e_recv.at[dst, h], device,
            )
            for h in (shares if only is None else (only,))
        ])

    def to_core(at, i, through=False, only=None):
        packed_here = at == own and not through
        src, place = (own_pack, i) if packed_here else (ext, at + i)
        return send(src, place, at + i, at + i, 0, (a, c1), only)

    def to_next(i):
        return send(own_pack, i, prev + i, own + i, 1, (a + 1, c))

    def to_ahead(i):
        return send(own_pack, i, pp + i, own + i, 2, (a + 2, c))

    def to_behind(i, only=None):
        return send(ext, pp + i, prev + i, pp + i, 1, (a - 1, c), only)

    def to_other(i):
        return send(own_pack, i, own + i, own + i, 2, (a, c2))

    def pass_next(i):
        return send(ext, own + i, prev + i, own + i, 1, (a + 1, c))

    def keep(i):
        return pltpu.make_async_copy(own_pack.at[i], ext.at[own + i], l_sem.at[i])

    def keep_coarse(r):
        return pltpu.make_async_copy(coarse_v.at[r], coarse_hbm.at[r], c_sem.at[r])

    def lift_diag(quarter_at):
        def step(k, carry):
            key = order[k]
            i = key % rows
            earlier = order[jnp.maximum(k - 1, 0)]
            goes_on = jnp.where((k > 0) & (earlier // rows == key // rows), 1, 0)
            carried = jnp.dot(fine[i], own_prolong[i], preferred_element_type=F32).astype(BF)
            lifted = jnp.dot(turned[i], carried, preferred_element_type=F32)
            seg[k] = lifted + seg[jnp.maximum(k - 1, 0)] * goes_on.astype(F32)
            return carry

        if quarter_at == 0:
            take_fine.wait()
            seg[0] = jnp.zeros((width, width), F32)
        lax.fori_loop(quarter_at * quarter, (quarter_at + 1) * quarter, step, 0, unroll=True)

    def sort_diag():
        to_scalar(2).wait()
        lax.fori_loop(0, rows, classify_diag, 0)
        lax.fori_loop(0, rows, rank, 0)
        lax.fori_loop(0, rows, place_key, 0)
        lax.fori_loop(0, crows * slots, ends, 0)

    def send_diag():
        for r in diag:
            value = part(r, 0)
            coarse_v[r] = value
            put(own_pack, r, value)
            keep(r).start()
            keep_coarse(r).start()
            to_other(r).start()
            to_core(own, r).start()

            @pl.when(has_next)
            def _(r=r):
                to_next(r).start()

    plan_out = pltpu.make_async_copy(plan, plan_hbm, o_sem)

    def matches(i, carry):
        row = crows + i // slots
        q = i % slots
        origin = row_base - 2 * crows

        def column(at, n):
            return tab[at // crows, 1 + at % crows, n] - origin

        col = column(row, q)
        lowest = jnp.minimum(row, col)
        lowest_at = jnp.clip(lowest, 0, 3 * crows - 1)
        plan[i // slots, q * 8] = (lowest_at // crows) * slots * crows + lowest_at % crows
        plan[i // slots, q * 8 + 4] = jnp.where(row > col, 0, jnp.where(row < col, 1, 2))
        for m in range(1, slots):
            k = column(row, m)
            at = jnp.clip(k, 0, 3 * crows - 1)
            pick = -1
            for n in range(slots):
                spot = ((at // crows) * slots + n) * crows + at % crows
                pick = jnp.where(column(at, n) == col, spot, pick)
            plan[i // slots, q * 8 + m] = jnp.where(k < lowest, pick, -1)
        return carry

    def planned():
        lax.fori_loop(0, 2 * crows * slots, matches, 0)
        plan_out.start()

    chores.append(planned)

    def run(chore):
        chore()

    lag = 2
    for k in range(direct + lag):
        if k < direct:
            arrived(0, k)
        if k >= lag:
            other_side(arrived, k - lag)
        if k == 0:
            for i in range(rows):
                turned[i] = own_prolong[i].astype(F32).T.astype(BF)
        if k == 0:
            pl.when(c == 0)(sort_diag)
        if k < 4:
            pl.when(c == 0)(functools.partial(lift_diag, k))
        if k == 4:
            pl.when(c == 0)(send_diag)
        if k == 5:
            pl.when(c == 0)(integers)
        for chore in chores[(0, 2, 4, 5, 6)[min(k, 4)]:(2, 4, 5, 6, 6)[min(k, 4)]]:
            pl.when(c > 0)(functools.partial(run, chore))
        if 0 <= k - 3 < alone:
            crossed(0, k - 3)
        if 0 <= k - 4 < alone:
            other_side(crossed, k - 4)
        if k == 6:
            pl.when(c == 0)(planned)
    assert direct + lag >= 7

    def exchange_sent():
        ints_all(lambda copy: copy.wait_send())
        for k in range(direct):
            for h in pieces:
                push(k, h).wait_send()

        @pl.when(can_relay)
        def _():
            for k in range(direct):
                for h in pieces:
                    relay(k, h).wait_send()

        left(0)
        other_side(left)

    def landed(at, i, only=None):
        for h in (shares if only is None else (only,)):
            view = piece(ext, at + i, h, HALO_PARTS)
            remote(view, view, e_send.at[0, at + i, h], e_recv.at[at + i, h], (a, c1)).wait_recv()

    def own_ready(i, act):
        @pl.when(has_ahead)
        def _():
            act(to_ahead(i))

        @pl.when(even & has_next)
        def _():
            act(to_next(i))

        act(to_core(own, i))

    def neighbours(i):
        @pl.when(has_far)
        def _():
            for h in shares:
                landed(pp, i, h)

                @pl.when(odd)
                def _(h=h):
                    to_behind(i, h).start()

                to_core(pp, i, only=h).start()

        @pl.when(odd)
        def _():
            for h in shares:
                landed(prev, i, h)
                to_core(prev, i, only=h).start()

    def relayed(i):
        @pl.when(even & has_far)
        def _():
            for h in shares:
                landed(prev, i, h)
                to_core(prev, i, only=h).start()

    def flow(tiles, finish, lag, sent, hook):
        count = len(tiles)
        for k in range(count + 2 * lag):
            if k < count:
                finish(k)
                own_ready(tiles[k], lambda copy: copy.start())
                keep(tiles[k]).start()
            if 0 <= k - lag < count:
                neighbours(tiles[k - lag])
            hook(k)
            if 0 <= k - 2 * lag < count:
                relayed(tiles[k - 2 * lag])
                sent(k - 2 * lag)
                flow_sent(tiles[k - 2 * lag])

    def flow_sent(i):
        keep(i).wait()
        own_ready(i, lambda copy: copy.wait_send())

    def passed(tiles):
        for i in tiles:
            @pl.when(has_far)
            def _(i=i):
                to_core(pp, i).wait_send()

                @pl.when(odd)
                def _():
                    to_behind(i).wait_send()

            @pl.when(has_prev)
            def _(i=i):
                to_core(prev, i).wait_send()

    def arrivals(tiles):
        for i in tiles:
            landed(own, i)

            @pl.when(has_prev)
            def _(i=i):
                landed(prev, i)

            @pl.when(has_far)
            def _(i=i):
                landed(pp, i)

    def set_of(who):
        tiles = [(j, who) for j in range(crows)]
        return tiles + [((who - 2) * half + j, 1) for j in range(half)]

    def arrivals_diag():
        for r in diag:
            landed(own, r)

            @pl.when(has_prev)
            def _(r=r):
                landed(prev, r)

    @pl.when(c == 0)
    def _():
        complete(0)
        other_side(complete)
        for r in diag:
            @pl.when(has_prev)
            def _(r=r):
                landed(prev, r)
                to_core(prev, r).start()
        exchange_sent()
        arrivals([q * crows + r for q in range(1, slots) for r in range(crows)])
        for r in diag:
            keep(r).wait()
            to_other(r).wait_send()
            to_core(own, r).wait_send()

            @pl.when(has_next)
            def _(r=r):
                to_next(r).wait_send()

            @pl.when(has_prev)
            def _(r=r):
                to_core(prev, r).wait_send()

    @pl.when(c > 0)
    def _():
        complete(0)
        other_side(complete)
        take_fine.wait()
        lift_all(near_prior)

    @pl.when(c == 1)
    def _():
        listed = [(f, j) for j in range(part_count) for f in (2, 3)]

        def cross(k):
            f, j = listed[k]
            at = (f - 2) * part_count + j
            return remote(
                y_out.at[pl.ds(at, 1)], y_in.at[pl.ds(j, 1)], y_send.at[at], y_recv.at[j], (a, f)
            )

        tiles = []
        for k, (f, j) in enumerate(listed):
            r, q = set_of(f)[j]
            tiles.append(q * crows + r)
            put(y_out, (f - 2) * part_count + j, part(r, q))
            cross(k).start()

        def finish(k):
            f, j = listed[k]
            r, q = set_of(f)[j]
            at = (f - 2) * part_count + j
            view = y_in.at[pl.ds(at, 1)]
            remote(view, view, y_send.at[at], y_recv.at[at], (a, f)).wait_recv()
            value = part(r, q) + unpack(y_in[at].astype(F32), width)
            if q == 1:
                coarse_v[r] = value
                keep_coarse(r).start()
            put(own_pack, q * crows + r, value)

        exchange_sent()
        flow(tiles, finish, 4, lambda k: cross(k).wait_send(), lambda k: None)
        arrivals_diag()
        passed(tiles)

    @pl.when(c > 1)
    def _():
        mine = [(j, c) for j in range(crows)] + [((c - 2) * half + j, 1) for j in range(half)]
        theirs = [(j, c1) for j in range(crows)] + [((c1 - 2) * half + j, 1) for j in range(half)]

        def swap(j):
            return remote(
                pair_out.at[pl.ds(j, 1)], pair_in.at[pl.ds(j, 1)], p_send.at[j], p_recv.at[j], (a, c1)
            )

        def cross(j):
            return remote(
                y_out.at[pl.ds(j, 1)], y_in.at[pl.ds((c - 2) * part_count + j, 1)],
                y_send.at[j], y_recv.at[(c - 2) * part_count + j], (a, 1),
            )

        def share_diag():
            @pl.when(c == 2)
            def _():
                for r in diag:
                    landed(own, r)
                    to_core(own, r, True).start()

                    @pl.when(has_next)
                    def _(r=r):
                        pass_next(r).start()

        for j, (r, q) in enumerate(theirs):
            put(pair_out, j, part(r, q))
            swap(j).start()
        share_diag()
        for j, (r, q) in enumerate(mine):
            swap(j).wait_recv()
            value = part(r, q) + unpack(pair_in[j].astype(F32), width)
            sums[j] = value
            put(y_out, j, value)
            cross(j).start()

        def finish(j):
            r, q = mine[j]
            view = y_in.at[pl.ds(j, 1)]
            remote(view, view, y_send.at[j], y_recv.at[j], (a, 1)).wait_recv()
            value = sums[j] + unpack(y_in[j].astype(F32), width)
            if j < crows:
                coarse_v[j] = value
                keep_coarse(j).start()
            put(own_pack, q * crows + r, value)

        tiles = [q * crows + r for r, q in mine]

        def hook(k):
            r = k - part_count
            if 0 <= r < crows:
                @pl.when((c == 2) & has_prev)
                def _():
                    landed(prev, r)
                    to_core(prev, r).start()

        def sent(j):
            swap(j).wait_send()
            cross(j).wait_send()

        exchange_sent()
        assert crows <= 4
        flow(tiles, finish, 2, sent, hook)

        @pl.when(c == 3)
        def _():
            arrivals_diag()

        arrivals([q * crows + r for r, q in theirs])
        passed(tiles)

        @pl.when(c == 2)
        def _():
            for r in diag:
                to_core(own, r, True).wait_send()

                @pl.when(has_next)
                def _(r=r):
                    pass_next(r).wait_send()

                @pl.when(has_prev)
                def _(r=r):
                    to_core(prev, r).wait_send()

    for r in range(crows):
        keep_coarse(r).wait()

    plan_out.wait()


def sweep_kernel(
    dims, plan, ext, coarse, coarse_out, factor_out,
    first, acc, done, masks, need, tiles, terms, in_sem, out_sem,
):
    crows, slots, width = dims
    count = slots * crows
    group = 4
    c = lax.axis_index("col")
    give = pltpu.make_async_copy(coarse, coarse_out, in_sem)
    give.start()
    ids_r = lax.broadcasted_iota(jnp.int32, (width, width), 0)
    ids_c = lax.broadcasted_iota(jnp.int32, (width, width), 1)
    masks[0] = jnp.ones((width, width), BF)
    masks[1] = (ids_c < ids_r).astype(F32).astype(BF)
    masks[2] = (ids_c > ids_r).astype(F32).astype(BF)
    masks[3] = jnp.zeros((width, width), BF)

    def planned(row, q, j):
        return plan[row - crows, q * 8 + j]

    def spot(row, q):
        return ((row // crows) * slots + q) * crows + row % crows

    for i in range(count, 3 * count):
        need[i] = 0
    for r in range(crows):
        row = 2 * crows + r
        need[spot(row, c)] = 1
        need[planned(row, c, 0)] = 1
        for m in range(1, slots):
            pick = planned(row, c, m)

            @pl.when(pick >= 0)
            def _(row=row, m=m, pick=pick):
                need[spot(row, m)] = 1
                need[pick] = 1

    def list_terms(row, q, wanted, at, size):
        for m in range(1, slots):
            pick = planned(row, q, m)
            terms[0, size] = at
            terms[1, size] = spot(row, m)
            terms[2, size] = pick
            size = size + jnp.where(pick >= 0, wanted, 0)
        return size

    def pad_terms(size):
        for j in range(group - 1):
            terms[0, size + j] = 2 * count + group
            terms[1, size + j] = 2 * count
            terms[2, size + j] = 2 * count

    def add_terms(size, tile):
        def body(k, carry):
            for j in range(group):
                t = k * group + j
                product = jnp.dot(tile(terms[1, t]), tile(terms[2, t]), preferred_element_type=F32)
                acc[terms[0, t]] += product
            return carry

        lax.fori_loop(0, (size + group - 1) // group, body, 0)

    def clear(k, carry):
        acc[k] = jnp.zeros((width, width), F32)
        return carry

    def relax(own, diag_at, kind, start, total, tile):
        diag = tile(diag_at)
        mine = tile(own)
        left = jnp.where(kind == 0, mine, diag * masks[1])
        right = jnp.where(kind == 1, mine, diag * masks[2])
        value = start - total - jnp.dot(left, right, preferred_element_type=F32)
        chosen = jnp.where(ids_c == ids_r, diag.astype(F32), 0.0)
        inverse = 1.0 / jnp.maximum(jnp.sum(chosen, axis=0, keepdims=True), 1.0)
        scaled = masks[jnp.where(kind == 0, 0, jnp.where(kind == 1, 3, 1))].astype(F32)
        return value * jnp.where(scaled > 0.5, inverse, 1.0)

    def old(i):
        return unpack(ext[i], width)

    def new(i):
        return first[i]

    size = 0
    found = 0
    for row in range(crows, 3 * crows):
        for q in range(slots):
            wanted = need[spot(row, q)]
            tiles[0, found] = spot(row, q)
            tiles[1, found] = planned(row, q, 0)
            tiles[2, found] = planned(row, q, 4)
            size = list_terms(row, q, wanted, found, size)
            found = found + wanted
    pad_terms(size)
    for j in range(group - 1):
        tiles[0, found + j] = 3 * count
        tiles[1, found + j] = 2 * count
        tiles[2, found + j] = 0
    lax.fori_loop(0, found, clear, 0)
    add_terms(size, old)

    def sweep(k, carry):
        for j in range(group):
            t = k * group + j
            i = jnp.minimum(tiles[0, t], 3 * count - 1)
            start = old(i).astype(F32)
            first[tiles[0, t]] = relax(i, tiles[1, t], tiles[2, t], start, acc[t], old).astype(BF)
        return carry

    lax.fori_loop(0, (found + group - 1) // group, sweep, 0)

    size = 0
    for r in range(crows):
        size = list_terms(2 * crows + r, c, 1, r, size)
        acc[r] = jnp.zeros((width, width), F32)
    pad_terms(size)
    add_terms(size, new)

    def put_out(r):
        return pltpu.make_async_copy(done.at[r], factor_out.at[r], out_sem.at[r])

    for r in range(crows):
        row = 2 * crows + r
        done[r] = relax(spot(row, c), planned(row, c, 0), planned(row, c, 4), coarse[r], acc[r], new)
        put_out(r).start()
    give.wait()
    for r in range(crows):
        put_out(r).wait()


def on_device(groups, peers, fine_tiles, fine_cols, agg_of, prolong, coarse_cols):
    rows, width = prolong.shape[0], prolong.shape[-1]
    crows, slots = coarse_cols.shape
    assert SWEEPS == 2 and slots == peers == 4 and fine_tiles.shape[1] == 1
    assert groups % 2 == 0 and groups >= 4 and crows % 2 == 0
    direct = sum(shares_of(rows, peers))
    dma = pltpu.SemaphoreType.DMA
    tile = (width, width)
    packed = (width + width // 2, 2 * width // 3)
    count = slots * crows
    pairs = crows + crows // 2
    room = (-(-(crows + 2) // 8) * 8, 128)
    vmem = pl.BlockSpec(memory_space=pltpu.VMEM)
    smem = pl.BlockSpec(memory_space=pltpu.SMEM)
    anywhere = pl.BlockSpec(memory_space=pl.ANY)
    hbm = pl.BlockSpec(memory_space=pltpu.HBM)
    ext, coarse, plan = pl.pallas_call(
        functools.partial(gather_kernel, (groups, peers, rows, crows, slots, width)),
        out_shape=(
            pltpu.VMEM((3 * count,) + packed, BF),
            pltpu.VMEM((crows,) + tile, F32),
            pltpu.VMEM((2 * crows, 128), jnp.int32),
        ),
        in_specs=[hbm] * 5,
        out_specs=(anywhere, anywhere, anywhere),
        scratch_shapes=[
            pltpu.VMEM((rows,) + tile, BF),
            pltpu.VMEM((rows,) + tile, BF),
            pltpu.VMEM((rows,) + tile, BF),
            pltpu.VMEM((3 * rows,) + packed, BF),
            pltpu.VMEM((rows,) + tile, F32),
            pltpu.VMEM((count,) + packed, BF),
            pltpu.VMEM((crows,) + tile, F32),
            pltpu.VMEM((pairs,) + tile, F32),
            pltpu.VMEM((pairs,) + packed, BF),
            pltpu.VMEM((pairs,) + packed, BF),
            pltpu.VMEM((2 * pairs,) + packed, BF),
            pltpu.VMEM((2 * pairs,) + packed, BF),
            pltpu.VMEM((1, rows), jnp.int32),
            pltpu.VMEM((1, rows), jnp.int32),
            pltpu.VMEM((crows, slots), jnp.int32),
            pltpu.VMEM((4,) + room, jnp.int32),
            pltpu.SMEM((4,) + room, jnp.int32),
            pltpu.SMEM((rows,), jnp.int32),
            pltpu.SMEM((2 * rows,), jnp.int32),
            pltpu.SMEM((2 * count,), jnp.int32),
            pltpu.SMEM((2 * crows, 128), jnp.int32),
            dma((3,)), dma((7,)), dma((4,)), dma((3,)), dma((3,)), dma,
            dma((2, 4, direct, EXCHANGE_PARTS)), dma((2, 4, direct, EXCHANGE_PARTS)),
            dma((pairs,)), dma((pairs,)), dma((2 * pairs,)), dma((2 * pairs,)),
            dma((3, 3 * count, HALO_PARTS)), dma((3 * count, HALO_PARTS)), dma((count,)), dma((crows,)),
        ],
        compiler_params=pltpu.CompilerParams(
            collective_id=0, has_side_effects=True, vmem_limit_bytes=56 * 1024 * 1024
        ),
    )(agg_of.reshape(1, rows), fine_cols.reshape(1, rows), coarse_cols, fine_tiles.reshape((rows,) + tile), prolong)
    out = jax.ShapeDtypeStruct((crows,) + tile, F32)
    coarse, factor = pl.pallas_call(
        functools.partial(sweep_kernel, (crows, slots, width)),
        out_shape=(out, out),
        in_specs=[smem, vmem, vmem],
        out_specs=(anywhere, anywhere),
        scratch_shapes=[
            pltpu.VMEM((3 * count + 1,) + tile, BF),
            pltpu.VMEM((2 * count + 5,) + tile, F32),
            pltpu.VMEM((crows,) + tile, F32),
            pltpu.VMEM((4,) + tile, BF),
            pltpu.SMEM((3 * count,), jnp.int32),
            pltpu.SMEM((3, 2 * count + 4), jnp.int32),
            pltpu.SMEM((3, 2 * count * (slots - 1) + 4), jnp.int32),
            dma, dma((crows,)),
        ],
        compiler_params=pltpu.CompilerParams(vmem_limit_bytes=40 * 1024 * 1024),
    )(plan, ext, coarse)
    return coarse.reshape((crows, 1) + tile), factor.reshape((crows, 1) + tile)


def solution(mesh):
    in_specs = (
        P("agg", "col", None, None),
        P("agg", "col"),
        P("agg"),
        P("agg", None, None),
        P("agg", None),
    )
    out_specs = (P("agg", "col", None, None), P("agg", "col", None, None))
    return jax.shard_map(
        functools.partial(on_device, mesh.shape["agg"], mesh.shape["col"]),
        mesh=mesh, in_specs=in_specs, out_specs=out_specs, check_vma=False,
    )
```

```python
import functools

import jax
import jax.numpy as jnp
from jax import lax
from jax.experimental import pallas as pl
from jax.experimental.pallas import tpu as pltpu
from jax.sharding import PartitionSpec as P

SWEEPS = 2
EXCHANGE_PARTS = 1
HALO_PARTS = 1
MESH = pl.DeviceIdType.MESH
BF = jnp.bfloat16
F32 = jnp.float32


def pack(tile, dtype):
    width = tile.shape[-1]
    lanes = 2 * width // 3
    half = width // 2
    rest = tile[:, lanes:]
    return tile[:, :lanes].astype(dtype), jnp.concatenate([rest[:half], rest[half:]], axis=1).astype(dtype)


def put(ref, index, tile):
    left, rest = pack(tile, ref.dtype)
    width = tile.shape[-1]
    ref[index, 0:width] = left
    ref[index, width:] = rest


def unpack(tile, width):
    half = width // 2
    rest = tile[width:]
    fold = width - tile.shape[-1]
    right = jnp.concatenate([rest[:, :fold], rest[:, fold:]], axis=0)
    return jnp.concatenate([tile[:width], right], axis=1)


def shares_of(rows, peers):
    alone = 3 * rows // (4 * peers)
    return alone, (rows - peers * alone) // 2


def gather_kernel(
    dims, agg_hbm, fcol_hbm, ccol_hbm, fine_hbm, prolong_hbm, ext, coarse_hbm, plan_hbm,
    fine, own_prolong, turned, near, seg, own_pack, coarse_v, sums, pair_out, pair_in, y_out, y_in,
    agg_v, fcol_v, ccol_v, tab_v, tab, cls, order, table, plan,
    i_sem, in_sem, t_sem, t_send, t_recv, o_sem,
    h_send, h_recv, p_send, p_recv, y_send, y_recv, e_send, e_recv, l_sem, c_sem,
):
    groups, peers, rows, crows, slots, width = dims
    a = lax.axis_index("agg")
    c = lax.axis_index("col")
    c1 = c + 1 - 2 * (c % 2)
    c2 = (c + 2) % peers
    c3 = c2 + 1 - 2 * (c2 % 2)
    has_prev = a > 0
    has_next = a < groups - 1
    parity = a % 2
    partner_agg = a + 1 - 2 * parity
    relay_to = a + 2 - 4 * parity
    relay_from = a - 2 + 4 * parity
    can_relay = (relay_to >= 0) & (relay_to < groups)
    has_other = (relay_from >= 0) & (relay_from < groups)
    alone, both = shares_of(rows, peers)
    direct = alone + both
    o_some = crows * slots
    half = crows // 2
    odd = parity == 1
    even = parity == 0
    has_far = a > 1
    has_ahead = a < groups - 2

    blocks = [(c * alone, alone), (peers * alone + (c % 2) * both, both)]
    blocks += [(other * alone, alone) for other in (c1, c2, c3)]
    blocks += [(peers * alone + (c1 % 2) * both, both)]

    def take(j):
        start, size = blocks[j]
        return pltpu.make_async_copy(
            prolong_hbm.at[pl.ds(start, size)], own_prolong.at[pl.ds(start, size)], in_sem.at[j]
        )

    for j in range(2):
        take(j).start()
    take_ints = [
        pltpu.make_async_copy(src, dst, i_sem.at[j])
        for j, (src, dst) in enumerate(((agg_hbm, agg_v), (fcol_hbm, fcol_v), (ccol_hbm, ccol_v)))
    ]
    for copy in take_ints:
        copy.start()
    for j in range(2, len(blocks)):
        take(j).start()
    take_fine = pltpu.make_async_copy(fine_hbm, fine, in_sem.at[6])
    take_fine.start()

    barrier = pltpu.get_barrier_semaphore()
    for other in (c1, c2, c3):
        pl.semaphore_signal(barrier, inc=1, device_id=(a, other), device_id_type=MESH)

    @pl.when(has_prev)
    def _():
        pl.semaphore_signal(barrier, inc=1, device_id=(a - 1, c), device_id_type=MESH)

    @pl.when(has_next)
    def _():
        pl.semaphore_signal(barrier, inc=1, device_id=(a + 1, c), device_id_type=MESH)

    @pl.when(has_far)
    def _():
        pl.semaphore_signal(barrier, inc=1, device_id=(a - 2, c), device_id_type=MESH)

    @pl.when(has_ahead)
    def _():
        pl.semaphore_signal(barrier, inc=1, device_id=(a + 2, c), device_id_type=MESH)

    tab_v[2] = jnp.zeros(tab_v.shape[1:], jnp.int32)
    for copy in take_ints:
        copy.wait()
    tab_v[2, 0:1, 0:rows] = agg_v[...]
    tab_v[2, 1:1 + crows, 0:slots] = ccol_v[...]
    tab_v[2, 1 + crows:2 + crows, 0:rows] = fcol_v[...]

    def remote(src, dst, send, recv, device):
        return pltpu.make_async_remote_copy(
            src_ref=src, dst_ref=dst, send_sem=send, recv_sem=recv,
            device_id=device, device_id_type=MESH,
        )

    def piece(ref, index, h, parts):
        size = ref.shape[1] // parts
        return ref.at[pl.ds(index, 1), pl.ds(h * size, size)]

    def pack_own(j):
        start, size = blocks[j]

        def body(k, carry):
            put(near, rows + start + k, own_prolong[start + k].astype(F32))
            return carry
        lax.fori_loop(0, size, body, 0)

    for j in range(2):
        take(j).wait()
        pack_own(j)

    @pl.when((a > 1) & (a < groups - 2))
    def _():
        pl.semaphore_wait(barrier, 7)

    @pl.when((a == 1) | (a == groups - 2))
    def _():
        pl.semaphore_wait(barrier, 6)

    @pl.when((a == 0) | (a == groups - 1))
    def _():
        pl.semaphore_wait(barrier, 5)

    def ints_to(j):
        ahead = (1, -1, 2)[j]
        return remote(tab_v.at[2], tab_v.at[(1, 3, 0)[j]], t_send.at[j], t_recv.at[j], (a + ahead, c))

    def tile_of(who, k):
        if k < alone:
            return who * alone + k
        return peers * alone + (who % 2) * both + k - alone

    def block_at(side):
        return ((1 - parity) if side == 0 else parity) * 2 * rows

    pieces = range(EXCHANGE_PARTS)

    def near_piece(index, h):
        return piece(near, index, h, EXCHANGE_PARTS)

    def push(k, h):
        src = near_piece(rows + tile_of(c, k), h)
        dst = near_piece(parity * 2 * rows + tile_of(c, k), h)
        return remote(src, dst, h_send.at[0, 0, k, h], h_recv.at[0, 0, k, h], (partner_agg, c))

    def relay(k, h):
        src = near_piece(block_at(0) + tile_of(c, k), h)
        dst = near_piece(parity * 2 * rows + tile_of(c, k), h)
        return remote(src, dst, h_send.at[1, 0, k, h], h_recv.at[1, 0, k, h], (relay_to, c))

    def pass_on(side, kind, who, k, h, device):
        view = near_piece(block_at(side) + tile_of(who, k), h)
        return remote(view, view, h_send.at[side, kind, k, h], h_recv.at[side, kind, k, h], device)

    def arrived(side, k):
        for h in pieces:
            pass_on(side, 0, c, k, h, (a, c1)).wait_recv()
            if side == 0:
                @pl.when(can_relay)
                def _(h=h):
                    relay(k, h).start()
            if k < alone:
                pass_on(side, 2, c, k, h, (a, c2)).start()
            pass_on(side, 1, c, k, h, (a, c1)).start()

    def crossed(side, k):
        for h in pieces:
            pass_on(side, 2, c2, k, h, (a, c2)).wait_recv()
            pass_on(side, 3, c2, k, h, (a, c1)).start()

    def complete(side):
        for k in range(direct):
            for h in pieces:
                pass_on(side, 1, c1, k, h, (a, c1)).wait_recv()
                if k < alone:
                    pass_on(side, 3, c3, k, h, (a, c1)).wait_recv()

    def left(side):
        for k in range(direct):
            for h in pieces:
                pass_on(side, 1, c, k, h, (a, c1)).wait_send()
                if k < alone:
                    pass_on(side, 2, c, k, h, (a, c2)).wait_send()
                    pass_on(side, 3, c2, k, h, (a, c1)).wait_send()

    def other_side(step, *args):
        pl.when(has_other)(functools.partial(step, 1, *args))

    can_send = (has_next, has_prev, has_ahead)
    can_take = (has_prev, has_next, has_far)

    def ints_all(act):
        for j in range(3):
            @pl.when(can_send[j])
            def _(j=j):
                act(ints_to(j))

    ints_all(lambda copy: copy.start())
    for k in range(direct):
        for h in pieces:
            push(k, h).start()
    for j in range(2, len(blocks)):
        take(j).wait()
        pack_own(j)

    def to_scalar(g):
        return pltpu.make_async_copy(tab_v.at[g], tab.at[g], t_sem.at[g])

    to_scalar(2).start()

    def integers():
        pl.when(c > 0)(lambda: to_scalar(2).wait())
        for j in range(3):
            @pl.when(can_take[j])
            def _(j=j):
                ints_to(j).wait_recv()
                to_scalar((1, 3, 0)[j]).start()
        for j in range(3):
            @pl.when(can_take[j])
            def _(j=j):
                to_scalar((1, 3, 0)[j]).wait()

    chores = [integers]
    row_base = a * crows

    def place_of(i):
        return tab[2, 1 + crows, i] - (a - 1) * rows

    def classify(i, carry):
        place = jnp.clip(place_of(i), 0, 3 * rows - 1)
        target = tab[1 + place // rows, 0, place % rows]
        r = jnp.clip(tab[2, 0, i] - row_base, 0, crows - 1)
        q = 0
        for s in range(1, slots):
            q = jnp.where(tab[2, 1 + r, s] == target, s, q)
        cls[i] = (r * slots + q) * rows + i
        return carry

    chores.append(lambda: lax.fori_loop(0, rows, classify, 0))

    def classify_diag(i, carry):
        r = jnp.clip(tab[2, 0, i] - row_base, 0, crows - 1)
        cls[i] = r * slots * rows + i
        return carry

    def rank(i, carry):
        key = cls[i]
        below = 0
        for j in range(rows):
            below = below + jnp.where(cls[j] < key, 1, 0)
        order[rows + i] = below
        return carry

    chores.append(lambda: lax.fori_loop(0, rows, rank, 0))

    def place_key(k, carry):
        key = 0
        for i in range(rows):
            key = key + jnp.where(order[rows + i] == k, cls[i], 0)
        order[k] = key
        return carry

    chores.append(lambda: lax.fori_loop(0, rows, place_key, 0))

    def ends(s, carry):
        upto = 0
        some = 0
        for i in range(rows):
            own_class = cls[i] // rows
            upto = upto + jnp.where(own_class <= s, 1, 0)
            some = jnp.where(own_class == s, 1, some)
        table[s] = jnp.maximum(upto - 1, 0)
        table[o_some + s] = some
        return carry

    chores.append(lambda: lax.fori_loop(0, crows * slots, ends, 0))

    part_count = crows + half
    diag = list(range(crows))
    quarter = rows // 4

    def lift_at(k, total, prior):
        key = order[k]
        i = key % rows
        earlier = order[jnp.maximum(k - 1, 0)]
        goes_on = jnp.where(earlier // rows == key // rows, 1, 0)
        carried = jnp.dot(fine[i], prior(i), preferred_element_type=F32).astype(BF)
        lifted = jnp.dot(turned[i], carried, preferred_element_type=F32)
        total = lifted + total * goes_on.astype(F32)
        seg[k] = total
        return total

    def lift_all(prior):
        def step(k, total):
            return lift_at(k, total, prior)

        lax.fori_loop(0, rows, step, jnp.zeros((width, width), F32), unroll=True)

    def near_prior(i):
        place = jnp.clip(place_of(i), 0, 3 * rows - 1)
        return unpack(near[place], width)

    def part(r, q):
        s = r * slots + q
        return seg[table[s]] * table[o_some + s].astype(F32)

    pp, prev, own = (g * slots * crows for g in range(3))

    class Group:
        def __init__(self, copies):
            self.copies = copies

        def start(self):
            for copy in self.copies:
                copy.start()

        def wait_send(self):
            for copy in self.copies:
                copy.wait_send()

    shares = range(HALO_PARTS)

    def send(src, at, dst, to, kind, device, only=None):
        return Group([
            remote(
                piece(src, at, h, HALO_PARTS), piece(ext, dst, h, HALO_PARTS),
                e_send.at[kind, to, h], e_recv.at[dst, h], device,
            )
            for h in (shares if only is None else (only,))
        ])

    def to_core(at, i, through=False, only=None):
        packed_here = at == own and not through
        src, place = (own_pack, i) if packed_here else (ext, at + i)
        return send(src, place, at + i, at + i, 0, (a, c1), only)

    def to_next(i):
        return send(own_pack, i, prev + i, own + i, 1, (a + 1, c))

    def to_ahead(i):
        return send(own_pack, i, pp + i, own + i, 2, (a + 2, c))

    def to_behind(i, only=None):
        return send(ext, pp + i, prev + i, pp + i, 1, (a - 1, c), only)

    def to_other(i):
        return send(own_pack, i, own + i, own + i, 2, (a, c2))

    def pass_next(i):
        return send(ext, own + i, prev + i, own + i, 1, (a + 1, c))

    def keep(i):
        return pltpu.make_async_copy(own_pack.at[i], ext.at[own + i], l_sem.at[i])

    def keep_coarse(r):
        return pltpu.make_async_copy(coarse_v.at[r], coarse_hbm.at[r], c_sem.at[r])

    def lift_diag(quarter_at):
        def step(k, carry):
            key = order[k]
            i = key % rows
            earlier = order[jnp.maximum(k - 1, 0)]
            goes_on = jnp.where((k > 0) & (earlier // rows == key // rows), 1, 0)
            carried = jnp.dot(fine[i], own_prolong[i], preferred_element_type=F32).astype(BF)
            lifted = jnp.dot(turned[i], carried, preferred_element_type=F32)
            seg[k] = lifted + seg[jnp.maximum(k - 1, 0)] * goes_on.astype(F32)
            return carry

        if quarter_at == 0:
            take_fine.wait()
            seg[0] = jnp.zeros((width, width), F32)
        lax.fori_loop(quarter_at * quarter, (quarter_at + 1) * quarter, step, 0, unroll=True)

    def sort_diag():
        to_scalar(2).wait()
        lax.fori_loop(0, rows, classify_diag, 0)
        lax.fori_loop(0, rows, rank, 0)
        lax.fori_loop(0, rows, place_key, 0)
        lax.fori_loop(0, crows * slots, ends, 0)

    def send_diag():
        for r in diag:
            value = part(r, 0)
            coarse_v[r] = value
            put(own_pack, r, value)
            keep(r).start()
            keep_coarse(r).start()
            to_other(r).start()
            to_core(own, r).start()

            @pl.when(has_next)
            def _(r=r):
                to_next(r).start()

    plan_out = pltpu.make_async_copy(plan, plan_hbm, o_sem)

    def matches(i, carry):
        row = crows + i // slots
        q = i % slots
        origin = row_base - 2 * crows

        def column(at, n):
            return tab[at // crows, 1 + at % crows, n] - origin

        col = column(row, q)
        lowest = jnp.minimum(row, col)
        lowest_at = jnp.clip(lowest, 0, 3 * crows - 1)
        plan[i // slots, q * 8] = (lowest_at // crows) * slots * crows + lowest_at % crows
        plan[i // slots, q * 8 + 4] = jnp.where(row > col, 0, jnp.where(row < col, 1, 2))
        for m in range(1, slots):
            k = column(row, m)
            at = jnp.clip(k, 0, 3 * crows - 1)
            pick = -1
            for n in range(slots):
                spot = ((at // crows) * slots + n) * crows + at % crows
                pick = jnp.where(column(at, n) == col, spot, pick)
            plan[i // slots, q * 8 + m] = jnp.where(k < lowest, pick, -1)
        return carry

    def planned():
        lax.fori_loop(0, 2 * crows * slots, matches, 0)
        plan_out.start()

    chores.append(planned)

    def run(chore):
        chore()

    lag = 2
    for k in range(direct + lag):
        if k < direct:
            arrived(0, k)
        if k >= lag:
            other_side(arrived, k - lag)
        if k == 0:
            for i in range(rows):
                turned[i] = own_prolong[i].astype(F32).T.astype(BF)
        if k == 0:
            pl.when(c == 0)(sort_diag)
        if k < 4:
            pl.when(c == 0)(functools.partial(lift_diag, k))
        if k == 4:
            pl.when(c == 0)(send_diag)
        if k == 5:
            pl.when(c == 0)(integers)
        for chore in chores[(0, 2, 4, 5, 6)[min(k, 4)]:(2, 4, 5, 6, 6)[min(k, 4)]]:
            pl.when(c > 0)(functools.partial(run, chore))
        if 0 <= k - 3 < alone:
            crossed(0, k - 3)
        if 0 <= k - 4 < alone:
            other_side(crossed, k - 4)
        if k == 6:
            pl.when(c == 0)(planned)
    assert direct + lag >= 7

    def exchange_sent():
        ints_all(lambda copy: copy.wait_send())
        for k in range(direct):
            for h in pieces:
                push(k, h).wait_send()

        @pl.when(can_relay)
        def _():
            for k in range(direct):
                for h in pieces:
                    relay(k, h).wait_send()

        left(0)
        other_side(left)

    def landed(at, i, only=None):
        for h in (shares if only is None else (only,)):
            view = piece(ext, at + i, h, HALO_PARTS)
            remote(view, view, e_send.at[0, at + i, h], e_recv.at[at + i, h], (a, c1)).wait_recv()

    def own_ready(i, act):
        @pl.when(has_ahead)
        def _():
            act(to_ahead(i))

        @pl.when(even & has_next)
        def _():
            act(to_next(i))

        act(to_core(own, i))

    def neighbours(i):
        @pl.when(has_far)
        def _():
            for h in shares:
                landed(pp, i, h)

                @pl.when(odd)
                def _(h=h):
                    to_behind(i, h).start()

                to_core(pp, i, only=h).start()

        @pl.when(odd)
        def _():
            for h in shares:
                landed(prev, i, h)
                to_core(prev, i, only=h).start()

    def relayed(i):
        @pl.when(even & has_far)
        def _():
            for h in shares:
                landed(prev, i, h)
                to_core(prev, i, only=h).start()

    def flow(tiles, finish, after, lag, sent, hook):
        count = len(tiles)
        for k in range(count + 2 * lag):
            if k < count:
                value = finish(k)
                own_ready(tiles[k], lambda copy: copy.start())
                keep(tiles[k]).start()
                after(k, value)
            if 0 <= k - lag < count:
                neighbours(tiles[k - lag])
            hook(k)
            if 0 <= k - 2 * lag < count:
                relayed(tiles[k - 2 * lag])
                sent(k - 2 * lag)
                flow_sent(tiles[k - 2 * lag])

    def flow_sent(i):
        keep(i).wait()
        own_ready(i, lambda copy: copy.wait_send())

    def passed(tiles):
        for i in tiles:
            @pl.when(has_far)
            def _(i=i):
                to_core(pp, i).wait_send()

                @pl.when(odd)
                def _():
                    to_behind(i).wait_send()

            @pl.when(has_prev)
            def _(i=i):
                to_core(prev, i).wait_send()

    def arrivals(tiles):
        for i in tiles:
            landed(own, i)

            @pl.when(has_prev)
            def _(i=i):
                landed(prev, i)

            @pl.when(has_far)
            def _(i=i):
                landed(pp, i)

    def set_of(who):
        tiles = [(j, who) for j in range(crows)]
        return tiles + [((who - 2) * half + j, 1) for j in range(half)]

    def arrivals_diag():
        for r in diag:
            landed(own, r)

            @pl.when(has_prev)
            def _(r=r):
                landed(prev, r)

    @pl.when(c == 0)
    def _():
        complete(0)
        other_side(complete)
        for r in diag:
            @pl.when(has_prev)
            def _(r=r):
                landed(prev, r)
                to_core(prev, r).start()
        exchange_sent()
        arrivals([q * crows + r for q in range(1, slots) for r in range(crows)])
        for r in diag:
            keep(r).wait()
            to_other(r).wait_send()
            to_core(own, r).wait_send()

            @pl.when(has_next)
            def _(r=r):
                to_next(r).wait_send()

            @pl.when(has_prev)
            def _(r=r):
                to_core(prev, r).wait_send()

    @pl.when(c > 0)
    def _():
        complete(0)
        other_side(complete)
        take_fine.wait()
        lift_all(near_prior)

    @pl.when(c == 1)
    def _():
        listed = [(f, j) for j in range(part_count) for f in (2, 3)]

        def cross(k):
            f, j = listed[k]
            at = (f - 2) * part_count + j
            return remote(
                y_out.at[pl.ds(at, 1)], y_in.at[pl.ds(j, 1)], y_send.at[at], y_recv.at[j], (a, f)
            )

        tiles = []
        for k, (f, j) in enumerate(listed):
            r, q = set_of(f)[j]
            tiles.append(q * crows + r)
            at = (f - 2) * part_count + j
            left, rest = pack(part(r, q), F32)
            sums[at, 0:width] = left
            sums[at, width:] = rest
            y_out[at] = sums[at].astype(BF)
            cross(k).start()

        def finish(k):
            f, j = listed[k]
            r, q = set_of(f)[j]
            at = (f - 2) * part_count + j
            view = y_in.at[pl.ds(at, 1)]
            remote(view, view, y_send.at[at], y_recv.at[at], (a, f)).wait_recv()
            value = sums[at] + y_in[at].astype(F32)
            own_pack[q * crows + r] = value.astype(BF)
            return value

        def after(k, value):
            f, j = listed[k]
            r, q = set_of(f)[j]
            if q == 1:
                coarse_v[r] = unpack(value, width)
                keep_coarse(r).start()

        exchange_sent()
        flow(tiles, finish, after, 3, lambda k: cross(k).wait_send(), lambda k: None)
        arrivals_diag()
        passed(tiles)

    @pl.when(c > 1)
    def _():
        mine = [(j, c) for j in range(crows)] + [((c - 2) * half + j, 1) for j in range(half)]
        theirs = [(j, c1) for j in range(crows)] + [((c1 - 2) * half + j, 1) for j in range(half)]

        def swap(j):
            return remote(
                pair_out.at[pl.ds(j, 1)], pair_in.at[pl.ds(j, 1)], p_send.at[j], p_recv.at[j], (a, c1)
            )

        def cross(j):
            return remote(
                y_out.at[pl.ds(j, 1)], y_in.at[pl.ds((c - 2) * part_count + j, 1)],
                y_send.at[j], y_recv.at[(c - 2) * part_count + j], (a, 1),
            )

        def share_diag():
            @pl.when(c == 2)
            def _():
                for r in diag:
                    landed(own, r)
                    to_core(own, r, True).start()

                    @pl.when(has_next)
                    def _(r=r):
                        pass_next(r).start()

        for j, (r, q) in enumerate(theirs):
            put(pair_out, j, part(r, q))
            swap(j).start()
        share_diag()
        for j, (r, q) in enumerate(mine):
            swap(j).wait_recv()
            left, rest = pack(part(r, q), F32)
            sums[j, 0:width] = left
            sums[j, width:] = rest
            value = sums[j] + pair_in[j].astype(F32)
            y_out[j] = value.astype(BF)
            cross(j).start()
            sums[j] = value

        def finish(j):
            r, q = mine[j]
            view = y_in.at[pl.ds(j, 1)]
            remote(view, view, y_send.at[j], y_recv.at[j], (a, 1)).wait_recv()
            value = sums[j] + y_in[j].astype(F32)
            own_pack[q * crows + r] = value.astype(BF)
            return value

        def after(j, value):
            if j < crows:
                coarse_v[j] = unpack(value, width)
                keep_coarse(j).start()

        tiles = [q * crows + r for r, q in mine]

        def hook(k):
            r = k - part_count
            if 0 <= r < crows:
                @pl.when((c == 2) & has_prev)
                def _():
                    landed(prev, r)
                    to_core(prev, r).start()

        def sent(j):
            swap(j).wait_send()
            cross(j).wait_send()

        exchange_sent()
        assert crows <= 4
        flow(tiles, finish, after, 2, sent, hook)

        @pl.when(c == 3)
        def _():
            arrivals_diag()

        arrivals([q * crows + r for r, q in theirs])
        passed(tiles)

        @pl.when(c == 2)
        def _():
            for r in diag:
                to_core(own, r, True).wait_send()

                @pl.when(has_next)
                def _(r=r):
                    pass_next(r).wait_send()

                @pl.when(has_prev)
                def _(r=r):
                    to_core(prev, r).wait_send()

    for r in range(crows):
        keep_coarse(r).wait()

    plan_out.wait()


def sweep_kernel(
    dims, plan, ext, coarse, coarse_out, factor_out,
    first, acc, done, masks, need, tiles, terms, in_sem, out_sem,
):
    crows, slots, width = dims
    count = slots * crows
    group = 4
    c = lax.axis_index("col")
    give = pltpu.make_async_copy(coarse, coarse_out, in_sem)
    give.start()
    ids_r = lax.broadcasted_iota(jnp.int32, (width, width), 0)
    ids_c = lax.broadcasted_iota(jnp.int32, (width, width), 1)
    masks[0] = jnp.ones((width, width), BF)
    masks[1] = (ids_c < ids_r).astype(F32).astype(BF)
    masks[2] = (ids_c > ids_r).astype(F32).astype(BF)
    masks[3] = jnp.zeros((width, width), BF)

    def planned(row, q, j):
        return plan[row - crows, q * 8 + j]

    def spot(row, q):
        return ((row // crows) * slots + q) * crows + row % crows

    for i in range(count, 3 * count):
        need[i] = 0
    for r in range(crows):
        row = 2 * crows + r
        need[spot(row, c)] = 1
        need[planned(row, c, 0)] = 1
        for m in range(1, slots):
            pick = planned(row, c, m)

            @pl.when(pick >= 0)
            def _(row=row, m=m, pick=pick):
                need[spot(row, m)] = 1
                need[pick] = 1

    def list_terms(row, q, wanted, at, size):
        for m in range(1, slots):
            pick = planned(row, q, m)
            terms[0, size] = at
            terms[1, size] = spot(row, m)
            terms[2, size] = pick
            size = size + jnp.where(pick >= 0, wanted, 0)
        return size

    def pad_terms(size):
        for j in range(group - 1):
            terms[0, size + j] = 2 * count + group
            terms[1, size + j] = 2 * count
            terms[2, size + j] = 2 * count

    def add_terms(size, tile):
        def body(k, carry):
            for j in range(group):
                t = k * group + j
                product = jnp.dot(tile(terms[1, t]), tile(terms[2, t]), preferred_element_type=F32)
                acc[terms[0, t]] += product
            return carry

        lax.fori_loop(0, (size + group - 1) // group, body, 0)

    def clear(k, carry):
        acc[k] = jnp.zeros((width, width), F32)
        return carry

    def relax(own, diag_at, kind, start, total, tile):
        diag = tile(diag_at)
        mine = tile(own)
        left = jnp.where(kind == 0, mine, diag * masks[1])
        right = jnp.where(kind == 1, mine, diag * masks[2])
        value = start - total - jnp.dot(left, right, preferred_element_type=F32)
        chosen = jnp.where(ids_c == ids_r, diag.astype(F32), 0.0)
        inverse = 1.0 / jnp.maximum(jnp.sum(chosen, axis=0, keepdims=True), 1.0)
        scaled = masks[jnp.where(kind == 0, 0, jnp.where(kind == 1, 3, 1))].astype(F32)
        return value * jnp.where(scaled > 0.5, inverse, 1.0)

    def old(i):
        return unpack(ext[i], width)

    def new(i):
        return first[i]

    size = 0
    found = 0
    for row in range(crows, 3 * crows):
        for q in range(slots):
            wanted = need[spot(row, q)]
            tiles[0, found] = spot(row, q)
            tiles[1, found] = planned(row, q, 0)
            tiles[2, found] = planned(row, q, 4)
            size = list_terms(row, q, wanted, found, size)
            found = found + wanted
    pad_terms(size)
    for j in range(group - 1):
        tiles[0, found + j] = 3 * count
        tiles[1, found + j] = 2 * count
        tiles[2, found + j] = 0
    lax.fori_loop(0, found, clear, 0)
    add_terms(size, old)

    def sweep(k, carry):
        for j in range(group):
            t = k * group + j
            i = jnp.minimum(tiles[0, t], 3 * count - 1)
            start = old(i).astype(F32)
            first[tiles[0, t]] = relax(i, tiles[1, t], tiles[2, t], start, acc[t], old).astype(BF)
        return carry

    lax.fori_loop(0, (found + group - 1) // group, sweep, 0)

    size = 0
    for r in range(crows):
        size = list_terms(2 * crows + r, c, 1, r, size)
        acc[r] = jnp.zeros((width, width), F32)
    pad_terms(size)
    add_terms(size, new)

    def put_out(r):
        return pltpu.make_async_copy(done.at[r], factor_out.at[r], out_sem.at[r])

    for r in range(crows):
        row = 2 * crows + r
        done[r] = relax(spot(row, c), planned(row, c, 0), planned(row, c, 4), coarse[r], acc[r], new)
        put_out(r).start()
    give.wait()
    for r in range(crows):
        put_out(r).wait()


def on_device(groups, peers, fine_tiles, fine_cols, agg_of, prolong, coarse_cols):
    rows, width = prolong.shape[0], prolong.shape[-1]
    crows, slots = coarse_cols.shape
    assert SWEEPS == 2 and slots == peers == 4 and fine_tiles.shape[1] == 1
    assert groups % 2 == 0 and groups >= 4 and crows % 2 == 0
    direct = sum(shares_of(rows, peers))
    dma = pltpu.SemaphoreType.DMA
    tile = (width, width)
    packed = (width + width // 2, 2 * width // 3)
    count = slots * crows
    pairs = crows + crows // 2
    room = (-(-(crows + 2) // 8) * 8, 128)
    vmem = pl.BlockSpec(memory_space=pltpu.VMEM)
    smem = pl.BlockSpec(memory_space=pltpu.SMEM)
    anywhere = pl.BlockSpec(memory_space=pl.ANY)
    hbm = pl.BlockSpec(memory_space=pltpu.HBM)
    ext, coarse, plan = pl.pallas_call(
        functools.partial(gather_kernel, (groups, peers, rows, crows, slots, width)),
        out_shape=(
            pltpu.VMEM((3 * count,) + packed, BF),
            pltpu.VMEM((crows,) + tile, F32),
            pltpu.VMEM((2 * crows, 128), jnp.int32),
        ),
        in_specs=[hbm] * 5,
        out_specs=(anywhere, anywhere, anywhere),
        scratch_shapes=[
            pltpu.VMEM((rows,) + tile, BF),
            pltpu.VMEM((rows,) + tile, BF),
            pltpu.VMEM((rows,) + tile, BF),
            pltpu.VMEM((3 * rows,) + packed, BF),
            pltpu.VMEM((rows,) + tile, F32),
            pltpu.VMEM((count,) + packed, BF),
            pltpu.VMEM((crows,) + tile, F32),
            pltpu.VMEM((2 * pairs,) + packed, F32),
            pltpu.VMEM((pairs,) + packed, BF),
            pltpu.VMEM((pairs,) + packed, BF),
            pltpu.VMEM((2 * pairs,) + packed, BF),
            pltpu.VMEM((2 * pairs,) + packed, BF),
            pltpu.VMEM((1, rows), jnp.int32),
            pltpu.VMEM((1, rows), jnp.int32),
            pltpu.VMEM((crows, slots), jnp.int32),
            pltpu.VMEM((4,) + room, jnp.int32),
            pltpu.SMEM((4,) + room, jnp.int32),
            pltpu.SMEM((rows,), jnp.int32),
            pltpu.SMEM((2 * rows,), jnp.int32),
            pltpu.SMEM((2 * count,), jnp.int32),
            pltpu.SMEM((2 * crows, 128), jnp.int32),
            dma((3,)), dma((7,)), dma((4,)), dma((3,)), dma((3,)), dma,
            dma((2, 4, direct, EXCHANGE_PARTS)), dma((2, 4, direct, EXCHANGE_PARTS)),
            dma((pairs,)), dma((pairs,)), dma((2 * pairs,)), dma((2 * pairs,)),
            dma((3, 3 * count, HALO_PARTS)), dma((3 * count, HALO_PARTS)), dma((count,)), dma((crows,)),
        ],
        compiler_params=pltpu.CompilerParams(
            collective_id=0, has_side_effects=True, vmem_limit_bytes=56 * 1024 * 1024
        ),
    )(agg_of.reshape(1, rows), fine_cols.reshape(1, rows), coarse_cols, fine_tiles.reshape((rows,) + tile), prolong)
    out = jax.ShapeDtypeStruct((crows,) + tile, F32)
    coarse, factor = pl.pallas_call(
        functools.partial(sweep_kernel, (crows, slots, width)),
        out_shape=(out, out),
        in_specs=[smem, vmem, vmem],
        out_specs=(anywhere, anywhere),
        scratch_shapes=[
            pltpu.VMEM((3 * count + 1,) + tile, BF),
            pltpu.VMEM((2 * count + 5,) + tile, F32),
            pltpu.VMEM((crows,) + tile, F32),
            pltpu.VMEM((4,) + tile, BF),
            pltpu.SMEM((3 * count,), jnp.int32),
            pltpu.SMEM((3, 2 * count + 4), jnp.int32),
            pltpu.SMEM((3, 2 * count * (slots - 1) + 4), jnp.int32),
            dma, dma((crows,)),
        ],
        compiler_params=pltpu.CompilerParams(vmem_limit_bytes=40 * 1024 * 1024),
    )(plan, ext, coarse)
    return coarse.reshape((crows, 1) + tile), factor.reshape((crows, 1) + tile)


def solution(mesh):
    in_specs = (
        P("agg", "col", None, None),
        P("agg", "col"),
        P("agg"),
        P("agg", None, None),
        P("agg", None),
    )
    out_specs = (P("agg", "col", None, None), P("agg", "col", None, None))
    return jax.shard_map(
        functools.partial(on_device, mesh.shape["agg"], mesh.shape["col"]),
        mesh=mesh, in_specs=in_specs, out_specs=out_specs, check_vma=False,
    )
```

```python
import functools

import jax
import jax.numpy as jnp
from jax import lax
from jax.experimental import pallas as pl
from jax.experimental.pallas import tpu as pltpu
from jax.sharding import PartitionSpec as P

SWEEPS = 2
EXCHANGE_PARTS = 1
HALO_PARTS = 1
MESH = pl.DeviceIdType.MESH
BF = jnp.bfloat16
F32 = jnp.float32


def pack(tile, dtype):
    width = tile.shape[-1]
    lanes = 2 * width // 3
    half = width // 2
    rest = tile[:, lanes:]
    return tile[:, :lanes].astype(dtype), jnp.concatenate([rest[:half], rest[half:]], axis=1).astype(dtype)


def put(ref, index, tile):
    left, rest = pack(tile, ref.dtype)
    width = tile.shape[-1]
    ref[index, 0:width] = left
    ref[index, width:] = rest


def unpack(tile, width):
    half = width // 2
    rest = tile[width:]
    fold = width - tile.shape[-1]
    right = jnp.concatenate([rest[:, :fold], rest[:, fold:]], axis=0)
    return jnp.concatenate([tile[:width], right], axis=1)


def shares_of(rows, peers):
    alone = 3 * rows // (4 * peers)
    return alone, (rows - peers * alone) // 2


def gather_kernel(
    dims, agg_hbm, fcol_hbm, ccol_hbm, fine_hbm, prolong_hbm, ext, coarse_hbm, plan_hbm,
    fine, own_prolong, turned, near, seg, own_pack, coarse_v, sums, pair_out, pair_in, y_out, y_in,
    agg_v, fcol_v, ccol_v, tab_v, tab, cls, order, table, plan,
    i_sem, in_sem, t_sem, t_send, t_recv, o_sem,
    h_send, h_recv, p_send, p_recv, y_send, y_recv, e_send, e_recv, l_sem, c_sem,
):
    groups, peers, rows, crows, slots, width = dims
    a = lax.axis_index("agg")
    c = lax.axis_index("col")
    c1 = c + 1 - 2 * (c % 2)
    c2 = (c + 2) % peers
    c3 = c2 + 1 - 2 * (c2 % 2)
    has_prev = a > 0
    has_next = a < groups - 1
    parity = a % 2
    partner_agg = a + 1 - 2 * parity
    relay_to = a + 2 - 4 * parity
    relay_from = a - 2 + 4 * parity
    can_relay = (relay_to >= 0) & (relay_to < groups)
    has_other = (relay_from >= 0) & (relay_from < groups)
    alone, both = shares_of(rows, peers)
    direct = alone + both
    o_some = crows * slots
    half = crows // 2
    odd = parity == 1
    even = parity == 0
    has_far = a > 1
    has_ahead = a < groups - 2

    blocks = [(c * alone, alone), (peers * alone + (c % 2) * both, both)]
    blocks += [(other * alone, alone) for other in (c1, c2, c3)]
    blocks += [(peers * alone + (c1 % 2) * both, both)]

    def take(j):
        start, size = blocks[j]
        return pltpu.make_async_copy(
            prolong_hbm.at[pl.ds(start, size)], own_prolong.at[pl.ds(start, size)], in_sem.at[j]
        )

    for j in range(2):
        take(j).start()
    take_ints = [
        pltpu.make_async_copy(src, dst, i_sem.at[j])
        for j, (src, dst) in enumerate(((agg_hbm, agg_v), (fcol_hbm, fcol_v), (ccol_hbm, ccol_v)))
    ]
    for copy in take_ints:
        copy.start()
    for j in range(2, len(blocks)):
        take(j).start()
    take_fine = pltpu.make_async_copy(fine_hbm, fine, in_sem.at[6])
    take_fine.start()

    barrier = pltpu.get_barrier_semaphore()
    for other in (c1, c2, c3):
        pl.semaphore_signal(barrier, inc=1, device_id=(a, other), device_id_type=MESH)

    @pl.when(has_prev)
    def _():
        pl.semaphore_signal(barrier, inc=1, device_id=(a - 1, c), device_id_type=MESH)

    @pl.when(has_next)
    def _():
        pl.semaphore_signal(barrier, inc=1, device_id=(a + 1, c), device_id_type=MESH)

    @pl.when(has_far)
    def _():
        pl.semaphore_signal(barrier, inc=1, device_id=(a - 2, c), device_id_type=MESH)

    @pl.when(has_ahead)
    def _():
        pl.semaphore_signal(barrier, inc=1, device_id=(a + 2, c), device_id_type=MESH)

    tab_v[2] = jnp.zeros(tab_v.shape[1:], jnp.int32)
    for copy in take_ints:
        copy.wait()
    tab_v[2, 0:1, 0:rows] = agg_v[...]
    tab_v[2, 1:1 + crows, 0:slots] = ccol_v[...]
    tab_v[2, 1 + crows:2 + crows, 0:rows] = fcol_v[...]

    def remote(src, dst, send, recv, device):
        return pltpu.make_async_remote_copy(
            src_ref=src, dst_ref=dst, send_sem=send, recv_sem=recv,
            device_id=device, device_id_type=MESH,
        )

    def piece(ref, index, h, parts):
        size = ref.shape[1] // parts
        return ref.at[pl.ds(index, 1), pl.ds(h * size, size)]

    def pack_own(j):
        start, size = blocks[j]

        def body(k, carry):
            put(near, rows + start + k, own_prolong[start + k].astype(F32))
            return carry
        lax.fori_loop(0, size, body, 0)

    for j in range(2):
        take(j).wait()
        pack_own(j)

    @pl.when((a > 1) & (a < groups - 2))
    def _():
        pl.semaphore_wait(barrier, 7)

    @pl.when((a == 1) | (a == groups - 2))
    def _():
        pl.semaphore_wait(barrier, 6)

    @pl.when((a == 0) | (a == groups - 1))
    def _():
        pl.semaphore_wait(barrier, 5)

    def ints_to(j):
        ahead = (1, -1, 2)[j]
        return remote(tab_v.at[2], tab_v.at[(1, 3, 0)[j]], t_send.at[j], t_recv.at[j], (a + ahead, c))

    def tile_of(who, k):
        if k < alone:
            return who * alone + k
        return peers * alone + (who % 2) * both + k - alone

    def block_at(side):
        return ((1 - parity) if side == 0 else parity) * 2 * rows

    gives = c != 1
    pieces = range(EXCHANGE_PARTS)

    def near_piece(index, h):
        return piece(near, index, h, EXCHANGE_PARTS)

    def push(k, h):
        src = near_piece(rows + tile_of(c, k), h)
        dst = near_piece(parity * 2 * rows + tile_of(c, k), h)
        return remote(src, dst, h_send.at[0, 0, k, h], h_recv.at[0, 0, k, h], (partner_agg, c))

    def relay(k, h):
        src = near_piece(block_at(0) + tile_of(c, k), h)
        dst = near_piece(parity * 2 * rows + tile_of(c, k), h)
        return remote(src, dst, h_send.at[1, 0, k, h], h_recv.at[1, 0, k, h], (relay_to, c))

    def pass_on(side, kind, who, k, h, device):
        view = near_piece(block_at(side) + tile_of(who, k), h)
        return remote(view, view, h_send.at[side, kind, k, h], h_recv.at[side, kind, k, h], device)

    def arrived(side, k):
        for h in pieces:
            pass_on(side, 0, c, k, h, (a, c1)).wait_recv()
            if side == 0:
                @pl.when(can_relay)
                def _(h=h):
                    relay(k, h).start()
            if k < alone:
                pass_on(side, 2, c, k, h, (a, c2)).start()

            @pl.when(gives)
            def _(h=h):
                pass_on(side, 1, c, k, h, (a, c1)).start()

    def crossed(side, k):
        for h in pieces:
            pass_on(side, 2, c2, k, h, (a, c2)).wait_recv()

            @pl.when(gives)
            def _(h=h):
                pass_on(side, 3, c2, k, h, (a, c1)).start()

    def complete(side):
        for k in range(direct):
            for h in pieces:
                pass_on(side, 1, c1, k, h, (a, c1)).wait_recv()
                if k < alone:
                    pass_on(side, 3, c3, k, h, (a, c1)).wait_recv()

    def left(side):
        for k in range(direct):
            for h in pieces:
                if k < alone:
                    pass_on(side, 2, c, k, h, (a, c2)).wait_send()

                @pl.when(gives)
                def _(h=h, k=k):
                    pass_on(side, 1, c, k, h, (a, c1)).wait_send()
                    if k < alone:
                        pass_on(side, 3, c2, k, h, (a, c1)).wait_send()

    def other_side(step, *args):
        pl.when(has_other)(functools.partial(step, 1, *args))

    can_send = (has_next, has_prev, has_ahead)
    can_take = (has_prev, has_next, has_far)

    def ints_all(act):
        for j in range(3):
            @pl.when(can_send[j])
            def _(j=j):
                act(ints_to(j))

    ints_all(lambda copy: copy.start())
    for k in range(direct):
        for h in pieces:
            push(k, h).start()
    for j in range(2, len(blocks)):
        take(j).wait()
        pack_own(j)

    def to_scalar(g):
        return pltpu.make_async_copy(tab_v.at[g], tab.at[g], t_sem.at[g])

    to_scalar(2).start()

    def integers():
        pl.when(c > 0)(lambda: to_scalar(2).wait())
        for j in range(3):
            @pl.when(can_take[j])
            def _(j=j):
                ints_to(j).wait_recv()
                to_scalar((1, 3, 0)[j]).start()
        for j in range(3):
            @pl.when(can_take[j])
            def _(j=j):
                to_scalar((1, 3, 0)[j]).wait()

    chores = [integers]
    row_base = a * crows

    def place_of(i):
        return tab[2, 1 + crows, i] - (a - 1) * rows

    def classify(i, carry):
        place = jnp.clip(place_of(i), 0, 3 * rows - 1)
        target = tab[1 + place // rows, 0, place % rows]
        r = jnp.clip(tab[2, 0, i] - row_base, 0, crows - 1)
        q = 0
        for s in range(1, slots):
            q = jnp.where(tab[2, 1 + r, s] == target, s, q)
        cls[i] = (r * slots + q) * rows + i
        return carry

    chores.append(lambda: lax.fori_loop(0, rows, classify, 0))

    def classify_diag(i, carry):
        r = jnp.clip(tab[2, 0, i] - row_base, 0, crows - 1)
        cls[i] = r * slots * rows + i
        return carry

    def rank(i, carry):
        key = cls[i]
        below = 0
        for j in range(rows):
            below = below + jnp.where(cls[j] < key, 1, 0)
        order[rows + i] = below
        return carry

    chores.append(lambda: lax.fori_loop(0, rows, rank, 0))

    def place_key(k, carry):
        key = 0
        for i in range(rows):
            key = key + jnp.where(order[rows + i] == k, cls[i], 0)
        order[k] = key
        return carry

    chores.append(lambda: lax.fori_loop(0, rows, place_key, 0))

    def ends(s, carry):
        upto = 0
        some = 0
        for i in range(rows):
            own_class = cls[i] // rows
            upto = upto + jnp.where(own_class <= s, 1, 0)
            some = jnp.where(own_class == s, 1, some)
        table[s] = jnp.maximum(upto - 1, 0)
        table[o_some + s] = some
        return carry

    chores.append(lambda: lax.fori_loop(0, crows * slots, ends, 0))

    part_count = crows + half
    diag = list(range(crows))
    quarter = rows // 4

    def lift_at(k, total, prior):
        key = order[k]
        i = key % rows
        earlier = order[jnp.maximum(k - 1, 0)]
        goes_on = jnp.where(earlier // rows == key // rows, 1, 0)
        carried = jnp.dot(fine[i], prior(i), preferred_element_type=F32).astype(BF)
        lifted = jnp.dot(turned[i], carried, preferred_element_type=F32)
        total = lifted + total * goes_on.astype(F32)
        seg[k] = total
        return total

    def lift_all(prior):
        def step(k, total):
            return lift_at(k, total, prior)

        lax.fori_loop(0, rows, step, jnp.zeros((width, width), F32), unroll=True)

    def near_prior(i):
        place = jnp.clip(place_of(i), 0, 3 * rows - 1)
        return unpack(near[place], width)

    def part(r, q):
        s = r * slots + q
        return seg[table[s]] * table[o_some + s].astype(F32)

    pp, prev, own = (g * slots * crows for g in range(3))

    class Group:
        def __init__(self, copies):
            self.copies = copies

        def start(self):
            for copy in self.copies:
                copy.start()

        def wait_send(self):
            for copy in self.copies:
                copy.wait_send()

    shares = range(HALO_PARTS)

    def send(src, at, dst, to, kind, device, only=None):
        return Group([
            remote(
                piece(src, at, h, HALO_PARTS), piece(ext, dst, h, HALO_PARTS),
                e_send.at[kind, to, h], e_recv.at[dst, h], device,
            )
            for h in (shares if only is None else (only,))
        ])

    def to_core(at, i, through=False, only=None):
        packed_here = at == own and not through
        src, place = (own_pack, i) if packed_here else (ext, at + i)
        return send(src, place, at + i, at + i, 0, (a, c1), only)

    def to_next(i):
        return send(own_pack, i, prev + i, own + i, 1, (a + 1, c))

    def to_ahead(i):
        return send(own_pack, i, pp + i, own + i, 2, (a + 2, c))

    def to_behind(i, only=None):
        return send(ext, pp + i, prev + i, pp + i, 1, (a - 1, c), only)

    def to_other(i):
        return send(own_pack, i, own + i, own + i, 2, (a, c2))

    def pass_next(i):
        return send(ext, own + i, prev + i, own + i, 1, (a + 1, c))

    def keep(i):
        return pltpu.make_async_copy(own_pack.at[i], ext.at[own + i], l_sem.at[i])

    def keep_coarse(r):
        return pltpu.make_async_copy(coarse_v.at[r], coarse_hbm.at[r], c_sem.at[r])

    def lift_diag(quarter_at):
        def step(k, carry):
            key = order[k]
            i = key % rows
            earlier = order[jnp.maximum(k - 1, 0)]
            goes_on = jnp.where((k > 0) & (earlier // rows == key // rows), 1, 0)
            carried = jnp.dot(fine[i], own_prolong[i], preferred_element_type=F32).astype(BF)
            lifted = jnp.dot(turned[i], carried, preferred_element_type=F32)
            seg[k] = lifted + seg[jnp.maximum(k - 1, 0)] * goes_on.astype(F32)
            return carry

        if quarter_at == 0:
            take_fine.wait()
            seg[0] = jnp.zeros((width, width), F32)
        lax.fori_loop(quarter_at * quarter, (quarter_at + 1) * quarter, step, 0, unroll=True)

    def sort_diag():
        to_scalar(2).wait()
        lax.fori_loop(0, rows, classify_diag, 0)
        lax.fori_loop(0, rows, rank, 0)
        lax.fori_loop(0, rows, place_key, 0)
        lax.fori_loop(0, crows * slots, ends, 0)

    def send_diag():
        for r in diag:
            value = part(r, 0)
            coarse_v[r] = value
            put(own_pack, r, value)
            keep(r).start()
            keep_coarse(r).start()
            to_other(r).start()
            to_core(own, r).start()

            @pl.when(has_next)
            def _(r=r):
                to_next(r).start()

    plan_out = pltpu.make_async_copy(plan, plan_hbm, o_sem)

    def matches(i, carry):
        row = crows + i // slots
        q = i % slots
        origin = row_base - 2 * crows

        def column(at, n):
            return tab[at // crows, 1 + at % crows, n] - origin

        col = column(row, q)
        lowest = jnp.minimum(row, col)
        lowest_at = jnp.clip(lowest, 0, 3 * crows - 1)
        plan[i // slots, q * 8] = (lowest_at // crows) * slots * crows + lowest_at % crows
        plan[i // slots, q * 8 + 4] = jnp.where(row > col, 0, jnp.where(row < col, 1, 2))
        for m in range(1, slots):
            k = column(row, m)
            at = jnp.clip(k, 0, 3 * crows - 1)
            pick = -1
            for n in range(slots):
                spot = ((at // crows) * slots + n) * crows + at % crows
                pick = jnp.where(column(at, n) == col, spot, pick)
            plan[i // slots, q * 8 + m] = jnp.where(k < lowest, pick, -1)
        return carry

    def planned():
        lax.fori_loop(0, 2 * crows * slots, matches, 0)
        plan_out.start()

    chores.append(planned)

    def run(chore):
        chore()

    lag = 2
    for k in range(direct + lag):
        if k < direct:
            arrived(0, k)
        if k >= lag:
            other_side(arrived, k - lag)
        if k == 0:
            for i in range(rows):
                turned[i] = own_prolong[i].astype(F32).T.astype(BF)
        if k == 0:
            pl.when(c == 0)(sort_diag)
        if k < 4:
            pl.when(c == 0)(functools.partial(lift_diag, k))
        if k == 4:
            pl.when(c == 0)(send_diag)
        if k == 5:
            pl.when(c == 0)(integers)
        for chore in chores[(0, 2, 4, 5, 6)[min(k, 4)]:(2, 4, 5, 6, 6)[min(k, 4)]]:
            pl.when(c > 0)(functools.partial(run, chore))
        if 0 <= k - 3 < alone:
            crossed(0, k - 3)
        if 0 <= k - 4 < alone:
            other_side(crossed, k - 4)
        if k == 6:
            pl.when(c == 0)(planned)
    assert direct + lag >= 7

    def exchange_sent():
        ints_all(lambda copy: copy.wait_send())
        for k in range(direct):
            for h in pieces:
                push(k, h).wait_send()

        @pl.when(can_relay)
        def _():
            for k in range(direct):
                for h in pieces:
                    relay(k, h).wait_send()

        left(0)
        other_side(left)

    def landed(at, i, only=None):
        for h in (shares if only is None else (only,)):
            view = piece(ext, at + i, h, HALO_PARTS)
            remote(view, view, e_send.at[0, at + i, h], e_recv.at[at + i, h], (a, c1)).wait_recv()

    def own_ready(i, act):
        @pl.when(has_ahead)
        def _():
            act(to_ahead(i))

        @pl.when(even & has_next)
        def _():
            act(to_next(i))

        act(to_core(own, i))

    def neighbours(i):
        @pl.when(has_far)
        def _():
            for h in shares:
                landed(pp, i, h)

                @pl.when(odd)
                def _(h=h):
                    to_behind(i, h).start()

                to_core(pp, i, only=h).start()

        @pl.when(odd)
        def _():
            for h in shares:
                landed(prev, i, h)
                to_core(prev, i, only=h).start()

    def relayed(i):
        @pl.when(even & has_far)
        def _():
            for h in shares:
                landed(prev, i, h)
                to_core(prev, i, only=h).start()

    def flow(tiles, finish, after, lag, late, sent, hook):
        count = len(tiles)
        for k in range(count + late):
            if k < count:
                value = finish(k)
                own_ready(tiles[k], lambda copy: copy.start())
                keep(tiles[k]).start()
                after(k, value)
            if 0 <= k - lag < count:
                neighbours(tiles[k - lag])
            hook(k)
            if 0 <= k - late < count:
                relayed(tiles[k - late])
                sent(k - late)
                flow_sent(tiles[k - late])

    def flow_sent(i):
        keep(i).wait()
        own_ready(i, lambda copy: copy.wait_send())

    def passed(tiles):
        for i in tiles:
            @pl.when(has_far)
            def _(i=i):
                to_core(pp, i).wait_send()

                @pl.when(odd)
                def _():
                    to_behind(i).wait_send()

            @pl.when(has_prev)
            def _(i=i):
                to_core(prev, i).wait_send()

    def arrivals(tiles):
        for i in tiles:
            landed(own, i)

            @pl.when(has_prev)
            def _(i=i):
                landed(prev, i)

            @pl.when(has_far)
            def _(i=i):
                landed(pp, i)

    def set_of(who):
        tiles = [(j, who) for j in range(crows)]
        return tiles + [((who - 2) * half + j, 1) for j in range(half)]

    def arrivals_diag():
        for r in diag:
            landed(own, r)

            @pl.when(has_prev)
            def _(r=r):
                landed(prev, r)

    @pl.when(c == 0)
    def _():
        exchange_sent()
        for r in diag:
            @pl.when(has_prev)
            def _(r=r):
                landed(prev, r)
                to_core(prev, r).start()
        arrivals([q * crows + r for q in range(1, slots) for r in range(crows)])
        for r in diag:
            keep(r).wait()
            to_other(r).wait_send()
            to_core(own, r).wait_send()

            @pl.when(has_next)
            def _(r=r):
                to_next(r).wait_send()

            @pl.when(has_prev)
            def _(r=r):
                to_core(prev, r).wait_send()

    @pl.when(c > 0)
    def _():
        complete(0)
        other_side(complete)
        take_fine.wait()
        lift_all(near_prior)

    @pl.when(c == 1)
    def _():
        listed = [(f, j) for j in range(part_count) for f in (2, 3)]

        def cross(k):
            f, j = listed[k]
            at = (f - 2) * part_count + j
            return remote(
                y_out.at[pl.ds(at, 1)], y_in.at[pl.ds(j, 1)], y_send.at[at], y_recv.at[j], (a, f)
            )

        tiles = [q * crows + r for r, q in (set_of(f)[j] for f, j in listed)]
        pairs = [4 * n + m for n in range(part_count // 2) for m in (0, 2, 1, 3)]
        for k in pairs:
            f, j = listed[k]
            r, q = set_of(f)[j]
            at = (f - 2) * part_count + j
            left, rest = pack(part(r, q), F32)
            sums[at, 0:width] = left
            sums[at, width:] = rest
            y_out[at] = sums[at].astype(BF)
            cross(k).start()

        def finish(k):
            f, j = listed[k]
            r, q = set_of(f)[j]
            at = (f - 2) * part_count + j
            view = y_in.at[pl.ds(at, 1)]
            remote(view, view, y_send.at[at], y_recv.at[at], (a, f)).wait_recv()
            value = sums[at] + y_in[at].astype(F32)
            own_pack[q * crows + r] = value.astype(BF)
            return value

        def after(k, value):
            f, j = listed[k]
            r, q = set_of(f)[j]
            if q == 1:
                coarse_v[r] = unpack(value, width)
                keep_coarse(r).start()

        exchange_sent()
        flow(tiles, finish, after, 2, 5, lambda k: cross(k).wait_send(), lambda k: None)
        arrivals_diag()
        passed(tiles)

    @pl.when(c > 1)
    def _():
        mine = [(j, c) for j in range(crows)] + [((c - 2) * half + j, 1) for j in range(half)]
        theirs = [(j, c1) for j in range(crows)] + [((c1 - 2) * half + j, 1) for j in range(half)]

        def swap(j):
            return remote(
                pair_out.at[pl.ds(j, 1)], pair_in.at[pl.ds(j, 1)], p_send.at[j], p_recv.at[j], (a, c1)
            )

        def cross(j):
            return remote(
                y_out.at[pl.ds(j, 1)], y_in.at[pl.ds((c - 2) * part_count + j, 1)],
                y_send.at[j], y_recv.at[(c - 2) * part_count + j], (a, 1),
            )

        def share_diag():
            @pl.when(c == 2)
            def _():
                for r in diag:
                    landed(own, r)
                    to_core(own, r, True).start()

                    @pl.when(has_next)
                    def _(r=r):
                        pass_next(r).start()

        for j, (r, q) in enumerate(theirs):
            put(pair_out, j, part(r, q))
            swap(j).start()
        share_diag()
        for j, (r, q) in enumerate(mine):
            swap(j).wait_recv()
            left, rest = pack(part(r, q), F32)
            sums[j, 0:width] = left
            sums[j, width:] = rest
            value = sums[j] + pair_in[j].astype(F32)
            y_out[j] = value.astype(BF)
            cross(j).start()
            sums[j] = value

        def finish(j):
            r, q = mine[j]
            view = y_in.at[pl.ds(j, 1)]
            remote(view, view, y_send.at[j], y_recv.at[j], (a, 1)).wait_recv()
            value = sums[j] + y_in[j].astype(F32)
            own_pack[q * crows + r] = value.astype(BF)
            return value

        def after(j, value):
            if j < crows:
                coarse_v[j] = unpack(value, width)
                keep_coarse(j).start()

        tiles = [q * crows + r for r, q in mine]

        def hook(k):
            r = k - part_count
            if 0 <= r < crows:
                @pl.when((c == 2) & has_prev)
                def _():
                    landed(prev, r)
                    to_core(prev, r).start()

        def sent(j):
            swap(j).wait_send()
            cross(j).wait_send()

        exchange_sent()
        assert crows <= 4
        flow(tiles, finish, after, 2, 4, sent, hook)

        @pl.when(c == 3)
        def _():
            arrivals_diag()

        arrivals([q * crows + r for r, q in theirs])
        passed(tiles)

        @pl.when(c == 2)
        def _():
            for r in diag:
                to_core(own, r, True).wait_send()

                @pl.when(has_next)
                def _(r=r):
                    pass_next(r).wait_send()

                @pl.when(has_prev)
                def _(r=r):
                    to_core(prev, r).wait_send()

    for r in range(crows):
        keep_coarse(r).wait()

    plan_out.wait()


def sweep_kernel(
    dims, plan, ext, coarse, coarse_out, factor_out,
    first, acc, done, masks, need, tiles, terms, in_sem, out_sem,
):
    crows, slots, width = dims
    count = slots * crows
    group = 4
    c = lax.axis_index("col")
    give = pltpu.make_async_copy(coarse, coarse_out, in_sem)
    give.start()
    ids_r = lax.broadcasted_iota(jnp.int32, (width, width), 0)
    ids_c = lax.broadcasted_iota(jnp.int32, (width, width), 1)
    masks[0] = jnp.ones((width, width), BF)
    masks[1] = (ids_c < ids_r).astype(F32).astype(BF)
    masks[2] = (ids_c > ids_r).astype(F32).astype(BF)
    masks[3] = jnp.zeros((width, width), BF)

    def planned(row, q, j):
        return plan[row - crows, q * 8 + j]

    def spot(row, q):
        return ((row // crows) * slots + q) * crows + row % crows

    for i in range(count, 3 * count):
        need[i] = 0
    for r in range(crows):
        row = 2 * crows + r
        need[spot(row, c)] = 1
        need[planned(row, c, 0)] = 1
        for m in range(1, slots):
            pick = planned(row, c, m)

            @pl.when(pick >= 0)
            def _(row=row, m=m, pick=pick):
                need[spot(row, m)] = 1
                need[pick] = 1

    def list_terms(row, q, wanted, at, size):
        for m in range(1, slots):
            pick = planned(row, q, m)
            terms[0, size] = at
            terms[1, size] = spot(row, m)
            terms[2, size] = pick
            size = size + jnp.where(pick >= 0, wanted, 0)
        return size

    def pad_terms(size):
        for j in range(group - 1):
            terms[0, size + j] = 2 * count + group
            terms[1, size + j] = 2 * count
            terms[2, size + j] = 2 * count

    def add_terms(size, tile):
        def body(k, carry):
            for j in range(group):
                t = k * group + j
                product = jnp.dot(tile(terms[1, t]), tile(terms[2, t]), preferred_element_type=F32)
                acc[terms[0, t]] += product
            return carry

        lax.fori_loop(0, (size + group - 1) // group, body, 0)

    def clear(k, carry):
        acc[k] = jnp.zeros((width, width), F32)
        return carry

    def relax(own, diag_at, kind, start, total, tile):
        diag = tile(diag_at)
        mine = tile(own)
        left = jnp.where(kind == 0, mine, diag * masks[1])
        right = jnp.where(kind == 1, mine, diag * masks[2])
        value = start - total - jnp.dot(left, right, preferred_element_type=F32)
        chosen = jnp.where(ids_c == ids_r, diag.astype(F32), 0.0)
        inverse = 1.0 / jnp.maximum(jnp.sum(chosen, axis=0, keepdims=True), 1.0)
        scaled = masks[jnp.where(kind == 0, 0, jnp.where(kind == 1, 3, 1))].astype(F32)
        return value * jnp.where(scaled > 0.5, inverse, 1.0)

    def old(i):
        return unpack(ext[i], width)

    def new(i):
        return first[i]

    size = 0
    found = 0
    for row in range(crows, 3 * crows):
        for q in range(slots):
            wanted = need[spot(row, q)]
            tiles[0, found] = spot(row, q)
            tiles[1, found] = planned(row, q, 0)
            tiles[2, found] = planned(row, q, 4)
            size = list_terms(row, q, wanted, found, size)
            found = found + wanted
    pad_terms(size)
    for j in range(group - 1):
        tiles[0, found + j] = 3 * count
        tiles[1, found + j] = 2 * count
        tiles[2, found + j] = 0
    lax.fori_loop(0, found, clear, 0)
    add_terms(size, old)

    def sweep(k, carry):
        for j in range(group):
            t = k * group + j
            i = jnp.minimum(tiles[0, t], 3 * count - 1)
            start = old(i).astype(F32)
            first[tiles[0, t]] = relax(i, tiles[1, t], tiles[2, t], start, acc[t], old).astype(BF)
        return carry

    lax.fori_loop(0, (found + group - 1) // group, sweep, 0)

    size = 0
    for r in range(crows):
        size = list_terms(2 * crows + r, c, 1, r, size)
        acc[r] = jnp.zeros((width, width), F32)
    pad_terms(size)
    add_terms(size, new)

    def put_out(r):
        return pltpu.make_async_copy(done.at[r], factor_out.at[r], out_sem.at[r])

    for r in range(crows):
        row = 2 * crows + r
        done[r] = relax(spot(row, c), planned(row, c, 0), planned(row, c, 4), coarse[r], acc[r], new)
        put_out(r).start()
    give.wait()
    for r in range(crows):
        put_out(r).wait()


def on_device(groups, peers, fine_tiles, fine_cols, agg_of, prolong, coarse_cols):
    rows, width = prolong.shape[0], prolong.shape[-1]
    crows, slots = coarse_cols.shape
    assert SWEEPS == 2 and slots == peers == 4 and fine_tiles.shape[1] == 1
    assert groups % 2 == 0 and groups >= 4 and crows % 4 == 0
    direct = sum(shares_of(rows, peers))
    dma = pltpu.SemaphoreType.DMA
    tile = (width, width)
    packed = (width + width // 2, 2 * width // 3)
    count = slots * crows
    pairs = crows + crows // 2
    room = (-(-(crows + 2) // 8) * 8, 128)
    vmem = pl.BlockSpec(memory_space=pltpu.VMEM)
    smem = pl.BlockSpec(memory_space=pltpu.SMEM)
    anywhere = pl.BlockSpec(memory_space=pl.ANY)
    hbm = pl.BlockSpec(memory_space=pltpu.HBM)
    ext, coarse, plan = pl.pallas_call(
        functools.partial(gather_kernel, (groups, peers, rows, crows, slots, width)),
        out_shape=(
            pltpu.VMEM((3 * count,) + packed, BF),
            pltpu.VMEM((crows,) + tile, F32),
            pltpu.VMEM((2 * crows, 128), jnp.int32),
        ),
        in_specs=[hbm] * 5,
        out_specs=(anywhere, anywhere, anywhere),
        scratch_shapes=[
            pltpu.VMEM((rows,) + tile, BF),
            pltpu.VMEM((rows,) + tile, BF),
            pltpu.VMEM((rows,) + tile, BF),
            pltpu.VMEM((3 * rows,) + packed, BF),
            pltpu.VMEM((rows,) + tile, F32),
            pltpu.VMEM((count,) + packed, BF),
            pltpu.VMEM((crows,) + tile, F32),
            pltpu.VMEM((2 * pairs,) + packed, F32),
            pltpu.VMEM((pairs,) + packed, BF),
            pltpu.VMEM((pairs,) + packed, BF),
            pltpu.VMEM((2 * pairs,) + packed, BF),
            pltpu.VMEM((2 * pairs,) + packed, BF),
            pltpu.VMEM((1, rows), jnp.int32),
            pltpu.VMEM((1, rows), jnp.int32),
            pltpu.VMEM((crows, slots), jnp.int32),
            pltpu.VMEM((4,) + room, jnp.int32),
            pltpu.SMEM((4,) + room, jnp.int32),
            pltpu.SMEM((rows,), jnp.int32),
            pltpu.SMEM((2 * rows,), jnp.int32),
            pltpu.SMEM((2 * count,), jnp.int32),
            pltpu.SMEM((2 * crows, 128), jnp.int32),
            dma((3,)), dma((7,)), dma((4,)), dma((3,)), dma((3,)), dma,
            dma((2, 4, direct, EXCHANGE_PARTS)), dma((2, 4, direct, EXCHANGE_PARTS)),
            dma((pairs,)), dma((pairs,)), dma((2 * pairs,)), dma((2 * pairs,)),
            dma((3, 3 * count, HALO_PARTS)), dma((3 * count, HALO_PARTS)), dma((count,)), dma((crows,)),
        ],
        compiler_params=pltpu.CompilerParams(
            collective_id=0, has_side_effects=True, vmem_limit_bytes=56 * 1024 * 1024
        ),
    )(agg_of.reshape(1, rows), fine_cols.reshape(1, rows), coarse_cols, fine_tiles.reshape((rows,) + tile), prolong)
    out = jax.ShapeDtypeStruct((crows,) + tile, F32)
    coarse, factor = pl.pallas_call(
        functools.partial(sweep_kernel, (crows, slots, width)),
        out_shape=(out, out),
        in_specs=[smem, vmem, vmem],
        out_specs=(anywhere, anywhere),
        scratch_shapes=[
            pltpu.VMEM((3 * count + 1,) + tile, BF),
            pltpu.VMEM((2 * count + 5,) + tile, F32),
            pltpu.VMEM((crows,) + tile, F32),
            pltpu.VMEM((4,) + tile, BF),
            pltpu.SMEM((3 * count,), jnp.int32),
            pltpu.SMEM((3, 2 * count + 4), jnp.int32),
            pltpu.SMEM((3, 2 * count * (slots - 1) + 4), jnp.int32),
            dma, dma((crows,)),
        ],
        compiler_params=pltpu.CompilerParams(vmem_limit_bytes=40 * 1024 * 1024),
    )(plan, ext, coarse)
    return coarse.reshape((crows, 1) + tile), factor.reshape((crows, 1) + tile)


def solution(mesh):
    in_specs = (
        P("agg", "col", None, None),
        P("agg", "col"),
        P("agg"),
        P("agg", None, None),
        P("agg", None),
    )
    out_specs = (P("agg", "col", None, None), P("agg", "col", None, None))
    return jax.shard_map(
        functools.partial(on_device, mesh.shape["agg"], mesh.shape["col"]),
        mesh=mesh, in_specs=in_specs, out_specs=out_specs, check_vma=False,
    )
```

```python
import functools

import jax
import jax.numpy as jnp
from jax import lax
from jax.experimental import pallas as pl
from jax.experimental.pallas import tpu as pltpu
from jax.sharding import PartitionSpec as P

SWEEPS = 2
EXCHANGE_PARTS = 1
HALO_PARTS = 1
MESH = pl.DeviceIdType.MESH
BF = jnp.bfloat16
F32 = jnp.float32


def pack(tile, dtype):
    width = tile.shape[-1]
    lanes = 2 * width // 3
    half = width // 2
    rest = tile[:, lanes:]
    return tile[:, :lanes].astype(dtype), jnp.concatenate([rest[:half], rest[half:]], axis=1).astype(dtype)


def put(ref, index, tile):
    left, rest = pack(tile, ref.dtype)
    width = tile.shape[-1]
    ref[index, 0:width] = left
    ref[index, width:] = rest


def unpack(tile, width):
    half = width // 2
    rest = tile[width:]
    fold = width - tile.shape[-1]
    right = jnp.concatenate([rest[:, :fold], rest[:, fold:]], axis=0)
    return jnp.concatenate([tile[:width], right], axis=1)


def shares_of(rows, peers):
    alone = 3 * rows // (4 * peers)
    return alone, (rows - peers * alone) // 2


def gather_kernel(
    dims, agg_hbm, fcol_hbm, ccol_hbm, fine_hbm, prolong_hbm, ext, coarse_hbm, plan_hbm,
    fine, own_prolong, turned, near, seg, own_pack, coarse_v, sums, pair_out, pair_in, y_out, y_in,
    agg_v, fcol_v, ccol_v, tab_v, tab, cls, order, table, plan,
    i_sem, in_sem, t_sem, t_send, t_recv, o_sem,
    h_send, h_recv, p_send, p_recv, y_send, y_recv, e_send, e_recv, l_sem, c_sem,
):
    groups, peers, rows, crows, slots, width = dims
    a = lax.axis_index("agg")
    c = lax.axis_index("col")
    c1 = c + 1 - 2 * (c % 2)
    c2 = (c + 2) % peers
    c3 = c2 + 1 - 2 * (c2 % 2)
    has_prev = a > 0
    has_next = a < groups - 1
    parity = a % 2
    partner_agg = a + 1 - 2 * parity
    relay_to = a + 2 - 4 * parity
    relay_from = a - 2 + 4 * parity
    can_relay = (relay_to >= 0) & (relay_to < groups)
    has_other = (relay_from >= 0) & (relay_from < groups)
    alone, both = shares_of(rows, peers)
    direct = alone + both
    o_some = crows * slots
    half = crows // 2
    odd = parity == 1
    even = parity == 0
    has_far = a > 1
    has_ahead = a < groups - 2

    blocks = [(c * alone, alone), (peers * alone + (c % 2) * both, both)]
    blocks += [(other * alone, alone) for other in (c1, c2, c3)]
    blocks += [(peers * alone + (c1 % 2) * both, both)]

    def take(j):
        start, size = blocks[j]
        return pltpu.make_async_copy(
            prolong_hbm.at[pl.ds(start, size)], own_prolong.at[pl.ds(start, size)], in_sem.at[j]
        )

    for j in range(2):
        take(j).start()
    take_ints = [
        pltpu.make_async_copy(src, dst, i_sem.at[j])
        for j, (src, dst) in enumerate(((agg_hbm, agg_v), (fcol_hbm, fcol_v), (ccol_hbm, ccol_v)))
    ]
    for copy in take_ints:
        copy.start()
    for j in range(2, len(blocks)):
        take(j).start()
    take_fine = pltpu.make_async_copy(fine_hbm, fine, in_sem.at[6])
    take_fine.start()

    barrier = pltpu.get_barrier_semaphore()
    for other in (c1, c2, c3):
        pl.semaphore_signal(barrier, inc=1, device_id=(a, other), device_id_type=MESH)

    @pl.when(has_prev)
    def _():
        pl.semaphore_signal(barrier, inc=1, device_id=(a - 1, c), device_id_type=MESH)

    @pl.when(has_next)
    def _():
        pl.semaphore_signal(barrier, inc=1, device_id=(a + 1, c), device_id_type=MESH)

    @pl.when(has_far)
    def _():
        pl.semaphore_signal(barrier, inc=1, device_id=(a - 2, c), device_id_type=MESH)

    @pl.when(has_ahead)
    def _():
        pl.semaphore_signal(barrier, inc=1, device_id=(a + 2, c), device_id_type=MESH)

    tab_v[2] = jnp.zeros(tab_v.shape[1:], jnp.int32)
    for copy in take_ints:
        copy.wait()
    tab_v[2, 0:1, 0:rows] = agg_v[...]
    tab_v[2, 1:1 + crows, 0:slots] = ccol_v[...]
    tab_v[2, 1 + crows:2 + crows, 0:rows] = fcol_v[...]

    def remote(src, dst, send, recv, device):
        return pltpu.make_async_remote_copy(
            src_ref=src, dst_ref=dst, send_sem=send, recv_sem=recv,
            device_id=device, device_id_type=MESH,
        )

    def piece(ref, index, h, parts):
        size = ref.shape[1] // parts
        return ref.at[pl.ds(index, 1), pl.ds(h * size, size)]

    def pack_own(j):
        start, size = blocks[j]

        def body(k, carry):
            put(near, rows + start + k, own_prolong[start + k].astype(F32))
            return carry
        lax.fori_loop(0, size, body, 0)

    for j in range(2):
        take(j).wait()
        pack_own(j)

    @pl.when((a > 1) & (a < groups - 2))
    def _():
        pl.semaphore_wait(barrier, 7)

    @pl.when((a == 1) | (a == groups - 2))
    def _():
        pl.semaphore_wait(barrier, 6)

    @pl.when((a == 0) | (a == groups - 1))
    def _():
        pl.semaphore_wait(barrier, 5)

    def ints_to(j):
        ahead = (1, -1, 2)[j]
        return remote(tab_v.at[2], tab_v.at[(1, 3, 0)[j]], t_send.at[j], t_recv.at[j], (a + ahead, c))

    def tile_of(who, k):
        if k < alone:
            return who * alone + k
        return peers * alone + (who % 2) * both + k - alone

    def block_at(side):
        return ((1 - parity) if side == 0 else parity) * 2 * rows

    gives = c != 1
    pieces = range(EXCHANGE_PARTS)

    def near_piece(index, h):
        return piece(near, index, h, EXCHANGE_PARTS)

    def push(k, h):
        src = near_piece(rows + tile_of(c, k), h)
        dst = near_piece(parity * 2 * rows + tile_of(c, k), h)
        return remote(src, dst, h_send.at[0, 0, k, h], h_recv.at[0, 0, k, h], (partner_agg, c))

    def relay(k, h):
        src = near_piece(block_at(0) + tile_of(c, k), h)
        dst = near_piece(parity * 2 * rows + tile_of(c, k), h)
        return remote(src, dst, h_send.at[1, 0, k, h], h_recv.at[1, 0, k, h], (relay_to, c))

    def pass_on(side, kind, who, k, h, device):
        view = near_piece(block_at(side) + tile_of(who, k), h)
        return remote(view, view, h_send.at[side, kind, k, h], h_recv.at[side, kind, k, h], device)

    def arrived(side, k):
        for h in pieces:
            pass_on(side, 0, c, k, h, (a, c1)).wait_recv()
            if side == 0:
                @pl.when(can_relay)
                def _(h=h):
                    relay(k, h).start()
            if k < alone:
                pass_on(side, 2, c, k, h, (a, c2)).start()

            @pl.when(gives)
            def _(h=h):
                pass_on(side, 1, c, k, h, (a, c1)).start()

    def crossed(side, k):
        for h in pieces:
            pass_on(side, 2, c2, k, h, (a, c2)).wait_recv()

            @pl.when(gives)
            def _(h=h):
                pass_on(side, 3, c2, k, h, (a, c1)).start()

    def complete(side):
        for k in range(direct):
            for h in pieces:
                pass_on(side, 1, c1, k, h, (a, c1)).wait_recv()
                if k < alone:
                    pass_on(side, 3, c3, k, h, (a, c1)).wait_recv()

    def left(side):
        for k in range(direct):
            for h in pieces:
                if k < alone:
                    pass_on(side, 2, c, k, h, (a, c2)).wait_send()

                @pl.when(gives)
                def _(h=h, k=k):
                    pass_on(side, 1, c, k, h, (a, c1)).wait_send()
                    if k < alone:
                        pass_on(side, 3, c2, k, h, (a, c1)).wait_send()

    def other_side(step, *args):
        pl.when(has_other)(functools.partial(step, 1, *args))

    can_send = (has_next, has_prev, has_ahead)
    can_take = (has_prev, has_next, has_far)

    def ints_all(act):
        for j in range(3):
            @pl.when(can_send[j])
            def _(j=j):
                act(ints_to(j))

    ints_all(lambda copy: copy.start())
    for k in range(direct):
        for h in pieces:
            push(k, h).start()
    for j in range(2, len(blocks)):
        take(j).wait()
        pack_own(j)

    def to_scalar(g):
        return pltpu.make_async_copy(tab_v.at[g], tab.at[g], t_sem.at[g])

    to_scalar(2).start()

    def integers():
        pl.when(c > 0)(lambda: to_scalar(2).wait())
        for j in range(3):
            @pl.when(can_take[j])
            def _(j=j):
                ints_to(j).wait_recv()
                to_scalar((1, 3, 0)[j]).start()
        for j in range(3):
            @pl.when(can_take[j])
            def _(j=j):
                to_scalar((1, 3, 0)[j]).wait()

    chores = [integers]
    row_base = a * crows

    def place_of(i):
        return tab[2, 1 + crows, i] - (a - 1) * rows

    def classify(i, carry):
        place = jnp.clip(place_of(i), 0, 3 * rows - 1)
        target = tab[1 + place // rows, 0, place % rows]
        r = jnp.clip(tab[2, 0, i] - row_base, 0, crows - 1)
        q = 0
        for s in range(1, slots):
            q = jnp.where(tab[2, 1 + r, s] == target, s, q)
        cls[i] = (r * slots + q) * rows + i
        return carry

    chores.append(lambda: lax.fori_loop(0, rows, classify, 0))

    def classify_diag(i, carry):
        r = jnp.clip(tab[2, 0, i] - row_base, 0, crows - 1)
        cls[i] = r * slots * rows + i
        return carry

    def rank(i, carry):
        key = cls[i]
        below = 0
        for j in range(rows):
            below = below + jnp.where(cls[j] < key, 1, 0)
        order[rows + i] = below
        return carry

    chores.append(lambda: lax.fori_loop(0, rows, rank, 0))

    def place_key(k, carry):
        key = 0
        for i in range(rows):
            key = key + jnp.where(order[rows + i] == k, cls[i], 0)
        order[k] = key
        return carry

    chores.append(lambda: lax.fori_loop(0, rows, place_key, 0))

    def ends(s, carry):
        upto = 0
        some = 0
        for i in range(rows):
            own_class = cls[i] // rows
            upto = upto + jnp.where(own_class <= s, 1, 0)
            some = jnp.where(own_class == s, 1, some)
        table[s] = jnp.maximum(upto - 1, 0)
        table[o_some + s] = some
        return carry

    chores.append(lambda: lax.fori_loop(0, crows * slots, ends, 0))

    part_count = crows + half
    diag = list(range(crows))
    quarter = rows // 4

    def lift_at(k, total, prior):
        key = order[k]
        i = key % rows
        earlier = order[jnp.maximum(k - 1, 0)]
        goes_on = jnp.where(earlier // rows == key // rows, 1, 0)
        carried = jnp.dot(fine[i], prior(i), preferred_element_type=F32).astype(BF)
        lifted = jnp.dot(turned[i], carried, preferred_element_type=F32)
        total = lifted + total * goes_on.astype(F32)
        seg[k] = total
        return total

    def lift_all(prior):
        def step(k, total):
            return lift_at(k, total, prior)

        lax.fori_loop(0, rows, step, jnp.zeros((width, width), F32), unroll=True)

    def near_prior(i):
        place = jnp.clip(place_of(i), 0, 3 * rows - 1)
        return unpack(near[place], width)

    def part(r, q):
        s = r * slots + q
        return seg[table[s]] * table[o_some + s].astype(F32)

    pp, prev, own = (g * slots * crows for g in range(3))

    class Group:
        def __init__(self, copies):
            self.copies = copies

        def start(self):
            for copy in self.copies:
                copy.start()

        def wait_send(self):
            for copy in self.copies:
                copy.wait_send()

    shares = range(HALO_PARTS)

    def send(src, at, dst, to, kind, device, only=None):
        return Group([
            remote(
                piece(src, at, h, HALO_PARTS), piece(ext, dst, h, HALO_PARTS),
                e_send.at[kind, to, h], e_recv.at[dst, h], device,
            )
            for h in (shares if only is None else (only,))
        ])

    def to_core(at, i, through=False, only=None):
        packed_here = at == own and not through
        src, place = (own_pack, i) if packed_here else (ext, at + i)
        return send(src, place, at + i, at + i, 0, (a, c1), only)

    def to_next(i):
        return send(own_pack, i, prev + i, own + i, 1, (a + 1, c))

    def to_ahead(i):
        return send(own_pack, i, pp + i, own + i, 2, (a + 2, c))

    def to_behind(i, only=None):
        return send(ext, pp + i, prev + i, pp + i, 1, (a - 1, c), only)

    def to_other(i):
        return send(own_pack, i, own + i, own + i, 2, (a, c2))

    def pass_next(i):
        return send(ext, own + i, prev + i, own + i, 1, (a + 1, c))

    def keep(i):
        return pltpu.make_async_copy(own_pack.at[i], ext.at[own + i], l_sem.at[i])

    def keep_coarse(r):
        return pltpu.make_async_copy(coarse_v.at[r], coarse_hbm.at[r], c_sem.at[r])

    def lift_diag(quarter_at):
        def step(k, carry):
            key = order[k]
            i = key % rows
            earlier = order[jnp.maximum(k - 1, 0)]
            goes_on = jnp.where((k > 0) & (earlier // rows == key // rows), 1, 0)
            carried = jnp.dot(fine[i], own_prolong[i], preferred_element_type=F32).astype(BF)
            lifted = jnp.dot(turned[i], carried, preferred_element_type=F32)
            seg[k] = lifted + seg[jnp.maximum(k - 1, 0)] * goes_on.astype(F32)
            return carry

        if quarter_at == 0:
            take_fine.wait()
            seg[0] = jnp.zeros((width, width), F32)
        lax.fori_loop(quarter_at * quarter, (quarter_at + 1) * quarter, step, 0, unroll=True)

    def sort_diag():
        to_scalar(2).wait()
        lax.fori_loop(0, rows, classify_diag, 0)
        lax.fori_loop(0, rows, rank, 0)
        lax.fori_loop(0, rows, place_key, 0)
        lax.fori_loop(0, crows * slots, ends, 0)

    def send_diag():
        for r in diag:
            value = part(r, 0)
            coarse_v[r] = value
            put(own_pack, r, value)
            keep(r).start()
            keep_coarse(r).start()
            to_other(r).start()
            to_core(own, r).start()

            @pl.when(has_next)
            def _(r=r):
                to_next(r).start()

    plan_out = pltpu.make_async_copy(plan, plan_hbm, o_sem)

    def matches(i, carry):
        row = crows + i // slots
        q = i % slots
        origin = row_base - 2 * crows

        def column(at, n):
            return tab[at // crows, 1 + at % crows, n] - origin

        col = column(row, q)
        lowest = jnp.minimum(row, col)
        lowest_at = jnp.clip(lowest, 0, 3 * crows - 1)
        plan[i // slots, q * 8] = (lowest_at // crows) * slots * crows + lowest_at % crows
        plan[i // slots, q * 8 + 4] = jnp.where(row > col, 0, jnp.where(row < col, 1, 2))
        for m in range(1, slots):
            k = column(row, m)
            at = jnp.clip(k, 0, 3 * crows - 1)
            pick = -1
            for n in range(slots):
                spot = ((at // crows) * slots + n) * crows + at % crows
                pick = jnp.where(column(at, n) == col, spot, pick)
            plan[i // slots, q * 8 + m] = jnp.where(k < lowest, pick, -1)
        return carry

    def planned():
        lax.fori_loop(0, 2 * crows * slots, matches, 0)
        plan_out.start()

    chores.append(planned)

    def run(chore):
        chore()

    lag = 2
    for k in range(direct + lag):
        if k < direct:
            arrived(0, k)
        if k >= lag:
            other_side(arrived, k - lag)
        if k == 0:
            for i in range(rows):
                turned[i] = own_prolong[i].astype(F32).T.astype(BF)
        if k == 0:
            pl.when(c == 0)(sort_diag)
        if k < 4:
            pl.when(c == 0)(functools.partial(lift_diag, k))
        if k == 4:
            pl.when(c == 0)(send_diag)
        if k == 5:
            pl.when(c == 0)(integers)
        for chore in chores[(0, 2, 4, 5, 6)[min(k, 4)]:(2, 4, 5, 6, 6)[min(k, 4)]]:
            pl.when(c > 0)(functools.partial(run, chore))
        if 0 <= k - 3 < alone:
            crossed(0, k - 3)
        if 0 <= k - 4 < alone:
            other_side(crossed, k - 4)
        if k == 6:
            pl.when(c == 0)(planned)
    assert direct + lag >= 7

    def exchange_sent():
        ints_all(lambda copy: copy.wait_send())
        for k in range(direct):
            for h in pieces:
                push(k, h).wait_send()

        @pl.when(can_relay)
        def _():
            for k in range(direct):
                for h in pieces:
                    relay(k, h).wait_send()

        left(0)
        other_side(left)

    def landed(at, i, only=None):
        for h in (shares if only is None else (only,)):
            view = piece(ext, at + i, h, HALO_PARTS)
            remote(view, view, e_send.at[0, at + i, h], e_recv.at[at + i, h], (a, c1)).wait_recv()

    def own_ready(i, act):
        @pl.when(has_ahead)
        def _():
            act(to_ahead(i))

        @pl.when(even & has_next)
        def _():
            act(to_next(i))

        act(to_core(own, i))

    def neighbours(i):
        @pl.when(has_far)
        def _():
            for h in shares:
                landed(pp, i, h)

                @pl.when(odd)
                def _(h=h):
                    to_behind(i, h).start()

                to_core(pp, i, only=h).start()

        @pl.when(odd)
        def _():
            for h in shares:
                landed(prev, i, h)
                to_core(prev, i, only=h).start()

    def relayed(i):
        @pl.when(even & has_far)
        def _():
            for h in shares:
                landed(prev, i, h)
                to_core(prev, i, only=h).start()

    def flow(tiles, finish, after, lag, late, sent, hook):
        count = len(tiles)
        for k in range(count + late):
            if k < count:
                value = finish(k)
                own_ready(tiles[k], lambda copy: copy.start())
                keep(tiles[k]).start()
                after(k, value)
            if 0 <= k - lag < count:
                neighbours(tiles[k - lag])
            hook(k)
            if 0 <= k - late < count:
                relayed(tiles[k - late])
                sent(k - late)
                flow_sent(tiles[k - late])

    def flow_sent(i):
        keep(i).wait()
        own_ready(i, lambda copy: copy.wait_send())

    def passed(tiles):
        for i in tiles:
            @pl.when(has_far)
            def _(i=i):
                to_core(pp, i).wait_send()

                @pl.when(odd)
                def _():
                    to_behind(i).wait_send()

            @pl.when(has_prev)
            def _(i=i):
                to_core(prev, i).wait_send()

    def arrivals(tiles):
        for i in tiles:
            landed(own, i)

            @pl.when(has_prev)
            def _(i=i):
                landed(prev, i)

            @pl.when(has_far)
            def _(i=i):
                landed(pp, i)

    def set_of(who):
        tiles = [(j, who) for j in range(crows)]
        return tiles + [((who - 2) * half + j, 1) for j in range(half)]

    def arrivals_diag():
        for r in diag:
            landed(own, r)

            @pl.when(has_prev)
            def _(r=r):
                landed(prev, r)

    @pl.when(c == 0)
    def _():
        exchange_sent()
        for r in diag:
            @pl.when(has_prev)
            def _(r=r):
                landed(prev, r)
                to_core(prev, r).start()
        arrivals([q * crows + r for q in range(1, slots) for r in range(crows)])
        for r in diag:
            keep(r).wait()
            to_other(r).wait_send()
            to_core(own, r).wait_send()

            @pl.when(has_next)
            def _(r=r):
                to_next(r).wait_send()

            @pl.when(has_prev)
            def _(r=r):
                to_core(prev, r).wait_send()

    @pl.when(c > 0)
    def _():
        complete(0)
        other_side(complete)
        take_fine.wait()
        lift_all(near_prior)

    @pl.when(c == 1)
    def _():
        listed = [(f, j) for j in range(part_count) for f in (2, 3)]

        def cross(k):
            f, j = listed[k]
            at = (f - 2) * part_count + j
            return remote(
                y_out.at[pl.ds(at, 1)], y_in.at[pl.ds(j, 1)], y_send.at[at], y_recv.at[j], (a, f)
            )

        tiles = [q * crows + r for r, q in (set_of(f)[j] for f, j in listed)]
        pairs = [4 * n + m for n in range(part_count // 2) for m in (0, 2, 1, 3)]
        for k in pairs:
            f, j = listed[k]
            r, q = set_of(f)[j]
            at = (f - 2) * part_count + j
            left, rest = pack(part(r, q), F32)
            sums[at, 0:width] = left
            sums[at, width:] = rest
            y_out[at] = sums[at].astype(BF)
            cross(k).start()

        def finish(k):
            f, j = listed[k]
            r, q = set_of(f)[j]
            at = (f - 2) * part_count + j
            view = y_in.at[pl.ds(at, 1)]
            remote(view, view, y_send.at[at], y_recv.at[at], (a, f)).wait_recv()
            value = sums[at] + y_in[at].astype(F32)
            own_pack[q * crows + r] = value.astype(BF)
            return value

        def after(k, value):
            f, j = listed[k]
            r, q = set_of(f)[j]
            if q == 1:
                coarse_v[r] = unpack(value, width)
                keep_coarse(r).start()

        exchange_sent()
        flow(tiles, finish, after, 2, 5, lambda k: cross(k).wait_send(), lambda k: None)
        arrivals_diag()
        passed(tiles)

    @pl.when(c > 1)
    def _():
        mine = [(j, c) for j in range(crows)] + [((c - 2) * half + j, 1) for j in range(half)]
        theirs = [(j, c1) for j in range(crows)] + [((c1 - 2) * half + j, 1) for j in range(half)]

        def swap(j):
            return remote(
                pair_out.at[pl.ds(j, 1)], pair_in.at[pl.ds(j, 1)], p_send.at[j], p_recv.at[j], (a, c1)
            )

        def cross(j):
            return remote(
                y_out.at[pl.ds(j, 1)], y_in.at[pl.ds((c - 2) * part_count + j, 1)],
                y_send.at[j], y_recv.at[(c - 2) * part_count + j], (a, 1),
            )

        def share_diag():
            @pl.when(c == 2)
            def _():
                for r in diag:
                    landed(own, r)
                    to_core(own, r, True).start()

                    @pl.when(has_next)
                    def _(r=r):
                        pass_next(r).start()

        for j, (r, q) in enumerate(theirs):
            put(pair_out, j, part(r, q))
            swap(j).start()
        share_diag()
        for j, (r, q) in enumerate(mine):
            swap(j).wait_recv()
            left, rest = pack(part(r, q), F32)
            sums[j, 0:width] = left
            sums[j, width:] = rest
            value = sums[j] + pair_in[j].astype(F32)
            y_out[j] = value.astype(BF)
            cross(j).start()
            sums[j] = value

        def finish(j):
            r, q = mine[j]
            view = y_in.at[pl.ds(j, 1)]
            remote(view, view, y_send.at[j], y_recv.at[j], (a, 1)).wait_recv()
            value = sums[j] + y_in[j].astype(F32)
            own_pack[q * crows + r] = value.astype(BF)
            return value

        def after(j, value):
            if j < crows:
                coarse_v[j] = unpack(value, width)
                keep_coarse(j).start()

        tiles = [q * crows + r for r, q in mine]

        def hook(k):
            r = k - part_count
            if 0 <= r < crows:
                @pl.when((c == 2) & has_prev)
                def _():
                    landed(prev, r)
                    to_core(prev, r).start()

        def sent(j):
            swap(j).wait_send()
            cross(j).wait_send()

        exchange_sent()
        assert crows <= 4
        flow(tiles, finish, after, 2, 4, sent, hook)

        @pl.when(c == 3)
        def _():
            arrivals_diag()

        arrivals([q * crows + r for r, q in theirs])
        passed(tiles)

        @pl.when(c == 2)
        def _():
            for r in diag:
                to_core(own, r, True).wait_send()

                @pl.when(has_next)
                def _(r=r):
                    pass_next(r).wait_send()

                @pl.when(has_prev)
                def _(r=r):
                    to_core(prev, r).wait_send()

    for r in range(crows):
        keep_coarse(r).wait()

    plan_out.wait()


def sweep_kernel(
    dims, plan, ext, coarse, coarse_out, factor_out,
    first, acc, done, masks, need, tiles, terms, in_sem, out_sem,
):
    crows, slots, width = dims
    count = slots * crows
    group = 4
    c = lax.axis_index("col")
    give = pltpu.make_async_copy(coarse, coarse_out, in_sem)
    give.start()
    ids_r = lax.broadcasted_iota(jnp.int32, (width, width), 0)
    ids_c = lax.broadcasted_iota(jnp.int32, (width, width), 1)
    masks[0] = jnp.ones((width, width), BF)
    masks[1] = (ids_c < ids_r).astype(F32).astype(BF)
    masks[2] = (ids_c > ids_r).astype(F32).astype(BF)
    masks[3] = jnp.zeros((width, width), BF)

    def planned(row, q, j):
        return plan[row - crows, q * 8 + j]

    def spot(row, q):
        return ((row // crows) * slots + q) * crows + row % crows

    for i in range(count, 3 * count):
        need[i] = 0
    for r in range(crows):
        row = 2 * crows + r
        need[spot(row, c)] = 1
        need[planned(row, c, 0)] = 1
        for m in range(1, slots):
            pick = planned(row, c, m)

            @pl.when(pick >= 0)
            def _(row=row, m=m, pick=pick):
                need[spot(row, m)] = 1
                need[pick] = 1

    def list_terms(row, q, wanted, at, size):
        for m in range(1, slots):
            pick = planned(row, q, m)
            terms[0, size] = at
            terms[1, size] = spot(row, m)
            terms[2, size] = pick
            size = size + jnp.where(pick >= 0, wanted, 0)
        return size

    def pad_terms(size):
        for j in range(group - 1):
            terms[0, size + j] = 2 * count + group
            terms[1, size + j] = 2 * count
            terms[2, size + j] = 2 * count

    def add_terms(size, tile):
        def body(k, carry):
            for j in range(group):
                t = k * group + j
                product = jnp.dot(tile(terms[1, t]), tile(terms[2, t]), preferred_element_type=F32)
                acc[terms[0, t]] += product
            return carry

        lax.fori_loop(0, (size + group - 1) // group, body, 0)

    def clear(k, carry):
        for j in range(group):
            acc[k * group + j] = jnp.zeros((width, width), F32)
        return carry

    def relax(own, diag_at, kind, start, total, tile):
        diag = tile(diag_at)
        mine = tile(own)
        left = jnp.where(kind == 0, mine, diag * masks[1])
        right = jnp.where(kind == 1, mine, diag * masks[2])
        value = start - total - jnp.dot(left, right, preferred_element_type=F32)
        chosen = jnp.where(ids_c == ids_r, diag.astype(F32), 0.0)
        inverse = 1.0 / jnp.maximum(jnp.sum(chosen, axis=0, keepdims=True), 1.0)
        scaled = masks[jnp.where(kind == 0, 0, jnp.where(kind == 1, 3, 1))].astype(F32)
        return value * jnp.where(scaled > 0.5, inverse, 1.0)

    def old(i):
        return unpack(ext[i], width)

    def new(i):
        return first[i]

    size = 0
    found = 0
    for row in range(crows, 3 * crows):
        for q in range(slots):
            wanted = need[spot(row, q)]
            tiles[0, found] = spot(row, q)
            tiles[1, found] = planned(row, q, 0)
            tiles[2, found] = planned(row, q, 4)
            size = list_terms(row, q, wanted, found, size)
            found = found + wanted
    pad_terms(size)
    for j in range(group - 1):
        tiles[0, found + j] = 3 * count
        tiles[1, found + j] = 2 * count
        tiles[2, found + j] = 0
    lax.fori_loop(0, (found + group - 1) // group, clear, 0)
    add_terms(size, old)

    def sweep(k, carry):
        for j in range(group):
            t = k * group + j
            i = jnp.minimum(tiles[0, t], 3 * count - 1)
            start = old(i).astype(F32)
            first[tiles[0, t]] = relax(i, tiles[1, t], tiles[2, t], start, acc[t], old).astype(BF)
        return carry

    lax.fori_loop(0, (found + group - 1) // group, sweep, 0)

    size = 0
    for r in range(crows):
        size = list_terms(2 * crows + r, c, 1, r, size)
        acc[r] = jnp.zeros((width, width), F32)
    pad_terms(size)
    add_terms(size, new)

    def put_out(r):
        return pltpu.make_async_copy(done.at[r], factor_out.at[r], out_sem.at[r])

    for r in range(crows):
        row = 2 * crows + r
        done[r] = relax(spot(row, c), planned(row, c, 0), planned(row, c, 4), coarse[r], acc[r], new)
        put_out(r).start()
    give.wait()
    for r in range(crows):
        put_out(r).wait()


def on_device(groups, peers, fine_tiles, fine_cols, agg_of, prolong, coarse_cols):
    rows, width = prolong.shape[0], prolong.shape[-1]
    crows, slots = coarse_cols.shape
    assert SWEEPS == 2 and slots == peers == 4 and fine_tiles.shape[1] == 1
    assert groups % 2 == 0 and groups >= 4 and crows % 4 == 0
    direct = sum(shares_of(rows, peers))
    dma = pltpu.SemaphoreType.DMA
    tile = (width, width)
    packed = (width + width // 2, 2 * width // 3)
    count = slots * crows
    pairs = crows + crows // 2
    room = (-(-(crows + 2) // 8) * 8, 128)
    vmem = pl.BlockSpec(memory_space=pltpu.VMEM)
    smem = pl.BlockSpec(memory_space=pltpu.SMEM)
    anywhere = pl.BlockSpec(memory_space=pl.ANY)
    hbm = pl.BlockSpec(memory_space=pltpu.HBM)
    ext, coarse, plan = pl.pallas_call(
        functools.partial(gather_kernel, (groups, peers, rows, crows, slots, width)),
        out_shape=(
            pltpu.VMEM((3 * count,) + packed, BF),
            pltpu.VMEM((crows,) + tile, F32),
            pltpu.VMEM((2 * crows, 128), jnp.int32),
        ),
        in_specs=[hbm] * 5,
        out_specs=(anywhere, anywhere, anywhere),
        scratch_shapes=[
            pltpu.VMEM((rows,) + tile, BF),
            pltpu.VMEM((rows,) + tile, BF),
            pltpu.VMEM((rows,) + tile, BF),
            pltpu.VMEM((3 * rows,) + packed, BF),
            pltpu.VMEM((rows,) + tile, F32),
            pltpu.VMEM((count,) + packed, BF),
            pltpu.VMEM((crows,) + tile, F32),
            pltpu.VMEM((2 * pairs,) + packed, F32),
            pltpu.VMEM((pairs,) + packed, BF),
            pltpu.VMEM((pairs,) + packed, BF),
            pltpu.VMEM((2 * pairs,) + packed, BF),
            pltpu.VMEM((2 * pairs,) + packed, BF),
            pltpu.VMEM((1, rows), jnp.int32),
            pltpu.VMEM((1, rows), jnp.int32),
            pltpu.VMEM((crows, slots), jnp.int32),
            pltpu.VMEM((4,) + room, jnp.int32),
            pltpu.SMEM((4,) + room, jnp.int32),
            pltpu.SMEM((rows,), jnp.int32),
            pltpu.SMEM((2 * rows,), jnp.int32),
            pltpu.SMEM((2 * count,), jnp.int32),
            pltpu.SMEM((2 * crows, 128), jnp.int32),
            dma((3,)), dma((7,)), dma((4,)), dma((3,)), dma((3,)), dma,
            dma((2, 4, direct, EXCHANGE_PARTS)), dma((2, 4, direct, EXCHANGE_PARTS)),
            dma((pairs,)), dma((pairs,)), dma((2 * pairs,)), dma((2 * pairs,)),
            dma((3, 3 * count, HALO_PARTS)), dma((3 * count, HALO_PARTS)), dma((count,)), dma((crows,)),
        ],
        compiler_params=pltpu.CompilerParams(
            collective_id=0, has_side_effects=True, vmem_limit_bytes=56 * 1024 * 1024
        ),
    )(agg_of.reshape(1, rows), fine_cols.reshape(1, rows), coarse_cols, fine_tiles.reshape((rows,) + tile), prolong)
    out = jax.ShapeDtypeStruct((crows,) + tile, F32)
    coarse, factor = pl.pallas_call(
        functools.partial(sweep_kernel, (crows, slots, width)),
        out_shape=(out, out),
        in_specs=[smem, vmem, vmem],
        out_specs=(anywhere, anywhere),
        scratch_shapes=[
            pltpu.VMEM((3 * count + 1,) + tile, BF),
            pltpu.VMEM((2 * count + 5,) + tile, F32),
            pltpu.VMEM((crows,) + tile, F32),
            pltpu.VMEM((4,) + tile, BF),
            pltpu.SMEM((3 * count,), jnp.int32),
            pltpu.SMEM((3, 2 * count + 4), jnp.int32),
            pltpu.SMEM((3, 2 * count * (slots - 1) + 4), jnp.int32),
            dma, dma((crows,)),
        ],
        compiler_params=pltpu.CompilerParams(vmem_limit_bytes=40 * 1024 * 1024),
    )(plan, ext, coarse)
    return coarse.reshape((crows, 1) + tile), factor.reshape((crows, 1) + tile)


def solution(mesh):
    in_specs = (
        P("agg", "col", None, None),
        P("agg", "col"),
        P("agg"),
        P("agg", None, None),
        P("agg", None),
    )
    out_specs = (P("agg", "col", None, None), P("agg", "col", None, None))
    return jax.shard_map(
        functools.partial(on_device, mesh.shape["agg"], mesh.shape["col"]),
        mesh=mesh, in_specs=in_specs, out_specs=out_specs, check_vma=False,
    )
```
